32 devices in a mesh: gz: 8 (over z, y), gy: 4 (over x, core).
Axes of the slice: x: 2, y: 2, z: 4, core: 2. Of those that a mesh axis runs over, the one named last changes fastest.
Arguments:
- image: bfloat16 [8, 512, 512], P('gz', 'gy'), may hold values from -30 to 30, as said below
- conv_one: bfloat16 [16, 9], replicated, may hold values from -2 to 2
- conv_two: bfloat16 [32, 144], replicated, may hold values from -0.5 to 0.5
- tissue: int32 [8, 4096], P('gz', 'gy'), may hold values 0 or 1
Outputs:
- increments: float32 [2, 8, 4096], P(None, 'gz', 'gy')
The draws below stay inside these ranges and needn't reach their ends.
Inputs may be any that keep to these rules, and one draw needn't show every extreme that they name: `image`: pixel intensities of each section's crop.
All inputs are finite; a program needn't handle non-finite values. No bound on the sum of `tissue` on one device may be relied on, other than what follows from the above.
Results may differ from the reference program's by a relative error of at most 0.0029.
Values may be sent and summed in bfloat16 or wider, within the bound.
No kernel may reach another device: no remote copies, remote signals or barrier semaphores. Data moves between devices by JAX's collectives and lax.ppermute only.
A program may use at most 64 MiB of HBM per device.

```python
import jax
import jax.numpy as jnp
from jax import lax

CROP = 512
NODES = 64
CH_ONE = 16
CH_TWO = 32
REACH = 6
SECTIONS = 8


def draw_image(key, part):
    shape = (SECTIONS, CROP, CROP)
    result = jnp.clip(jax.random.normal(key, shape, jnp.float32), -6.0, 6.0)
    return result.astype(jnp.bfloat16)


def with_ends(values, rng, least, largest):
    dims = values.shape
    place = [jax.random.randint(jax.random.fold_in(rng, axis), (), 0, dims[axis]) for axis in range(len(dims))]
    values = values.at[tuple(place)].set(least)
    longest = dims.index(max(dims))
    place[longest] = (place[longest] + 1) % dims[longest]
    return values.at[tuple(place)].set(largest)


def bell_draw(rng, shape, width, bound, kind=jnp.bfloat16):
    values = width * jax.random.normal(rng, shape, jnp.float32)
    return jnp.clip(values, min=-bound, max=bound).astype(kind)


def setup_inputs(seed: int = 0) -> dict:
    streams_of = jax.random.split(jax.random.key(seed), 5)
    image = draw_image(jax.random.fold_in(streams_of[4], 71), 0)
    conv_one = bell_draw(streams_of[1], (CH_ONE, 9), 9 ** -0.5, 2.0)
    conv_two = bell_draw(streams_of[2], (CH_TWO, 9 * CH_ONE), (9 * CH_ONE) ** -0.5, 0.5)
    tissue = with_ends((jax.random.randint(streams_of[3], (SECTIONS, NODES * NODES), 0, 4) < 3).astype(jnp.int32), jax.random.fold_in(streams_of[3], 1), 0, 1)
    return {"image": image, "conv_one": conv_one, "conv_two": conv_two, "tissue": tissue}


spring_rate = 8.0
anchor_rate = 0.02
prior_var = 1.0


def first_conv(pixels, weights):
    height = (pixels.shape[0] - 1) // 2
    extent = pixels.shape[1]
    padded = jnp.pad(pixels, ((0, 0), (1, 0)))
    stencil = jnp.stack([padded[offset_row:offset_row + 2 * height:2, offset_col:offset_col + extent:2] for offset_row in range(3) for offset_col in range(3)])
    summed = jnp.dot(weights, stencil.reshape(9, -1), preferred_element_type=jnp.float32)
    return jnp.maximum(summed, 0.0).astype(jnp.bfloat16).reshape(weights.shape[0], height, extent // 2)


def second_conv(layers, weights):
    height = (layers.shape[1] - 1) // 2
    extent = layers.shape[2]
    padded = jnp.pad(layers, ((0, 0), (0, 0), (1, 0)))
    stencil = jnp.stack([padded[:, offset_row:offset_row + 2 * height:2, offset_col:offset_col + extent:2] for offset_row in range(3) for offset_col in range(3)], axis=1)
    summed = jnp.dot(weights, stencil.reshape(weights.shape[1], -1), preferred_element_type=jnp.float32)
    return jnp.maximum(summed, 0.0).astype(jnp.bfloat16).reshape(weights.shape[0], height, extent // 2)


def correlate(own, window, patch):
    channels, total_rows, extent = own.shape
    reach = (window.shape[1] - total_rows) // 2
    block = min(32, total_rows)
    span = 2 * reach + 1
    offsets = lax.broadcasted_iota(jnp.int32, (span * span, 1, 1), 0)
    shift_row = (offsets // span - reach).astype(jnp.float32)
    shift_col = (offsets % span - reach).astype(jnp.float32)

    def one_block(number):
        start = number * block
        mine = lax.dynamic_slice_in_dim(own, start, block, 1).astype(jnp.float32)
        theirs = lax.dynamic_slice_in_dim(window, start, block + 2 * reach, 1).astype(jnp.float32)
        scores = jnp.stack([jnp.sum(mine * theirs[:, offset_row:offset_row + block, offset_col:offset_col + extent], axis=0) for offset_row in range(span) for offset_col in range(span)]) * channels ** -0.5
        highest = jnp.max(scores, axis=0, keepdims=True)
        expo = jnp.exp(scores - highest)
        prob = expo / jnp.sum(expo, axis=0, keepdims=True)
        mean_row = jnp.sum(prob * shift_row, axis=0)
        mean_col = jnp.sum(prob * shift_col, axis=0)
        var_row = jnp.sum(prob * shift_row * shift_row, axis=0) - mean_row * mean_row + prior_var
        var_col = jnp.sum(prob * shift_col * shift_col, axis=0) - mean_col * mean_col + prior_var
        covar = jnp.sum(prob * shift_row * shift_col, axis=0) - mean_row * mean_col
        determ = var_row * var_col - covar * covar
        info_rr = var_col / determ
        info_rc = -covar / determ
        info_cc = var_row / determ
        pull_row = info_rr * mean_row + info_rc * mean_col
        pull_col = info_rc * mean_row + info_cc * mean_col
        fields = jnp.stack([info_rr, info_rc, info_cc, pull_row, pull_col])
        return fields.reshape(5, block // patch, patch, extent // patch, patch).mean(axis=(2, 4))

    pooled = lax.map(one_block, jnp.arange(total_rows // block, dtype=jnp.int32))
    return jnp.transpose(pooled, (1, 0, 2, 3)).reshape(5, -1)


def times_two(left, right):
    return (left[0] * right[0] + left[1] * right[2], left[0] * right[1] + left[1] * right[3], left[2] * right[0] + left[3] * right[2], left[2] * right[1] + left[3] * right[3])


def invert_two(matrix):
    determ = matrix[0] * matrix[3] - matrix[1] * matrix[2]
    return (matrix[3] / determ, -matrix[1] / determ, -matrix[2] / determ, matrix[0] / determ)


def apply_two(matrix, vector):
    return (matrix[0] * vector[0] + matrix[1] * vector[1], matrix[2] * vector[0] + matrix[3] * vector[1])


def minus_parts(left, right):
    return tuple(first - second for first, second in zip(left, right))


def negate_parts(parts):
    return tuple(-member for member in parts)


def lower_parts(parts):
    return tuple(jnp.concatenate([jnp.zeros_like(member[:1]), member[:-1]], axis=0) for member in parts)


def upper_parts(parts):
    return tuple(jnp.concatenate([member[1:], jnp.zeros_like(member[:1])], axis=0) for member in parts)


def pick_parts(parts, first):
    return tuple(member[first::2] for member in parts)


def reduce_solve(diag, below, above, rhs):
    count = diag[0].shape[0]
    if count == 1:
        return apply_two(invert_two(diag), rhs)
    inv_odd = invert_two(pick_parts(diag, 1))
    below_odd = pick_parts(below, 1)
    above_odd = pick_parts(above, 1)
    rhs_odd = pick_parts(rhs, 1)
    alpha = times_two(pick_parts(below, 0), lower_parts(inv_odd))
    gamma = times_two(pick_parts(above, 0), inv_odd)
    new_diag = minus_parts(minus_parts(pick_parts(diag, 0), times_two(alpha, lower_parts(above_odd))), times_two(gamma, below_odd))
    new_below = negate_parts(times_two(alpha, lower_parts(below_odd)))
    new_above = negate_parts(times_two(gamma, above_odd))
    new_rhs = minus_parts(minus_parts(pick_parts(rhs, 0), apply_two(alpha, lower_parts(rhs_odd))), apply_two(gamma, rhs_odd))
    solved_even = reduce_solve(new_diag, new_below, new_above, new_rhs)
    residue = minus_parts(minus_parts(rhs_odd, apply_two(below_odd, solved_even)), apply_two(above_odd, upper_parts(solved_even)))
    solved_odd = apply_two(inv_odd, residue)
    return tuple(jnp.stack([even, odd], axis=1).reshape((count,) + even.shape[1:]) for even, odd in zip(solved_even, solved_odd))


def pad_to(member, total, value):
    extra = total - member.shape[0]
    if extra == 0:
        return member
    return jnp.concatenate([member, jnp.full((extra,) + member.shape[1:], value, member.dtype)], axis=0)


def solve_columns(blocks):
    count = blocks[0].shape[0]
    index = lax.broadcasted_iota(jnp.int32, blocks[0].shape, 0)
    neighbours = (index > 0).astype(jnp.float32) + (index < count - 1).astype(jnp.float32)
    extra = spring_rate * neighbours + anchor_rate
    zeros = jnp.zeros_like(blocks[0])
    coupling_low = jnp.where(index > 0, -spring_rate, zeros)
    coupling_high = jnp.where(index < count - 1, -spring_rate, zeros)
    total = 1 << (count - 1).bit_length()
    diag = (pad_to(blocks[0] + extra, total, 1.0), pad_to(blocks[1], total, 0.0), pad_to(blocks[1], total, 0.0), pad_to(blocks[2] + extra, total, 1.0))
    below = tuple(pad_to(member, total, 0.0) for member in (coupling_low, zeros, zeros, coupling_low))
    above = tuple(pad_to(member, total, 0.0) for member in (coupling_high, zeros, zeros, coupling_high))
    rhs = (pad_to(blocks[3], total, 0.0), pad_to(blocks[4], total, 0.0))
    solved = reduce_solve(diag, below, above, rhs)
    return tuple(member[:count] for member in solved)


def section_features(pixels, conv_one, conv_two):
    first = first_conv(jnp.concatenate([jnp.zeros((1, pixels.shape[1]), jnp.bfloat16), pixels], axis=0), conv_one)
    top = jnp.zeros((first.shape[0], 1, first.shape[2]), jnp.bfloat16)
    return second_conv(jnp.concatenate([top, first], axis=1), conv_two)


def reference(image, conv_one, conv_two, tissue):
    patch = CROP // (4 * NODES)

    def step(following, inputs):
        pixels, marks, position = inputs
        own = section_features(pixels, conv_one, conv_two)
        window = jnp.pad(following, ((0, 0), (REACH, REACH), (REACH, REACH)))
        data = correlate(own, window, patch)
        keep = marks.astype(jnp.float32) * (position < SECTIONS - 1).astype(jnp.float32)
        return own, data * keep[None, :]

    start = jnp.zeros((CH_TWO, CROP // 4, CROP // 4), jnp.bfloat16)
    positions = jnp.arange(SECTIONS, dtype=jnp.int32)
    unused, data = lax.scan(step, start, (image, tissue, positions), reverse=True)
    blocks = tuple(data[:, number, :] for number in range(5))
    return jnp.stack(solve_columns(blocks))
```

```python
import functools

import jax
import jax.numpy as jnp
from jax import lax
from jax.experimental import pallas as pl
from jax.experimental.pallas import tpu as pltpu
from jax.sharding import PartitionSpec as P


NODES = 64
REACH = 6
SPRING = 8.0
ANCHOR = 0.02
PRIOR = 1.0

HALO = 32
CHUNK = 32
DEPTH = 80
TALL = 8
WIDE = 16
EDGE = 8
GROUP = 4
FAR = -1e30

FIRST_ROW = HALO - (4 * REACH + 3)


def iota(shape, dim):
    return lax.broadcasted_iota(jnp.int32, shape, dim)


def pick_columns(extent):
    quarter = extent // 4
    parts = []
    for b in range(3):
        source = iota((extent, 2 * quarter), 0)
        place = iota((extent, 2 * quarter), 1)
        wanted = 4 * (place % quarter) + 2 * (place // quarter) + b - 1
        parts.append(jnp.where(source == wanted, 1.0, 0.0).astype(jnp.bfloat16))
    return parts


def first_matrix(conv_one):
    channels = conv_one.shape[0]
    spread = []
    for a in range(3):
        tap = iota((9, 3 * DEPTH), 0)
        b = iota((9, 3 * DEPTH), 1) // DEPTH
        chosen = jnp.where(tap == 3 * a + b, 1.0, 0.0).astype(jnp.bfloat16)
        spread.append(jnp.dot(conv_one, chosen, preferred_element_type=jnp.float32))
    row = iota((channels, 3 * DEPTH), 1) % DEPTH - FIRST_ROW
    blocks = []
    for out in range(CHUNK):
        block = jnp.zeros_like(spread[0])
        for a in range(3):
            block = jnp.where(row == 2 * out + a, spread[a], block)
        blocks.append(block.astype(jnp.bfloat16))
    return jnp.concatenate(blocks, axis=0)


def second_matrix(conv_two):
    taps = conv_two.shape[1]
    inner = taps // 9
    rows = []
    for out in range(2):
        source = iota((taps, 15 * inner), 0)
        place = iota((taps, 15 * inner), 1)
        a = place // (3 * inner) - 2 * out
        b = (place // inner) % 3
        wanted = 9 * (place % inner) + 3 * a + b
        inside = (a >= 0) & (a < 3) & (source == wanted)
        chosen = jnp.where(inside, 1.0, 0.0).astype(jnp.bfloat16)
        rows.append(jnp.dot(conv_two, chosen, preferred_element_type=jnp.float32))
    return jnp.concatenate(rows, axis=0).astype(jnp.bfloat16)


def first_maps(pixels, conv_one, maps):
    extent = pixels.shape[1]
    quarter = extent // 4
    channels = conv_one.shape[0]
    columns = [
        jnp.dot(pixels, part, preferred_element_type=jnp.float32).astype(jnp.bfloat16)
        for part in pick_columns(extent)
    ]
    matrix = first_matrix(conv_one)
    for chunk in range(maps.shape[0] // CHUNK):
        start = 2 * CHUNK * chunk
        taken = jnp.concatenate([part[start : start + DEPTH] for part in columns], axis=0)
        values = jnp.maximum(jnp.dot(matrix, taken, preferred_element_type=jnp.float32), 0.0)
        even, odd = values[:, :quarter], values[:, quarter:]
        before = jnp.where(iota(odd.shape, 1) == 0, 0.0, pltpu.roll(odd, 1, 1))
        for b, part in enumerate((before, even, odd)):
            maps[chunk * CHUNK : (chunk + 1) * CHUNK, b] = part.astype(jnp.bfloat16).reshape(
                CHUNK, channels, quarter
            )


def two_rows(maps, matrix, pair):
    rows = maps[4 * pair : 4 * pair + 5]
    rows = rows.reshape(-1, rows.shape[-1])
    return jnp.maximum(jnp.dot(matrix, rows, preferred_element_type=jnp.float32), 0.0)


def keys_kernel(total, image, near, far, conv_one, conv_two, keys, maps):
    place = lax.axis_index("gy")
    odd = place % 2 == 1
    a, b = near[0], far[0]
    above = jnp.where(odd, a, b)
    below = jnp.where(odd, b, a)
    spare = jnp.zeros((DEPTH - 2 * CHUNK, above.shape[1]), jnp.bfloat16)
    pixels = jnp.concatenate([above, image[0], below, spare], axis=0)
    first_maps(pixels, conv_one[...], maps)
    matrix = second_matrix(conv_two[...])
    channels = conv_two.shape[0]
    local = image.shape[1] // 4
    last = place == total - 1
    edge = jnp.zeros((EDGE, GROUP * channels), jnp.float32)
    for group in range(keys.shape[0]):
        both = [two_rows(maps, matrix, 2 * group + half) for half in range(2)]
        both = jnp.concatenate(both, axis=0)
        if GROUP * (group + 1) > local + REACH:
            row = GROUP * group + iota(both.shape, 0) // channels
            both = jnp.where(last & (row >= local + REACH), 0.0, both)
        turned = jnp.concatenate([edge, both.T, edge], axis=0)
        keys[group] = turned.astype(jnp.bfloat16)


def swap_blocks(rows, width):
    count = len(rows)
    lanes = rows[0].shape[1]
    step = 1
    while step < count:
        low = (iota(rows[0].shape, 1) // width) % (2 * step) < step
        fresh = list(rows)
        for index in range(count):
            if index & step == 0:
                one, two = rows[index], rows[index + step]
                shift = width * step
                fresh[index] = jnp.where(low, one, pltpu.roll(two, shift, 1))
                fresh[index + step] = jnp.where(low, pltpu.roll(one, lanes - shift, 1), two)
        rows = fresh
        step *= 2
    return rows


def match_kernel(image, corner, conv_one, conv_two, keys, tissue, blocks, maps, queries, mask, sums):
    below = jnp.zeros((HALO + DEPTH - 2 * CHUNK, image.shape[2]), jnp.bfloat16)
    pixels = jnp.concatenate([corner[0], image[0], below], axis=0)
    first_maps(pixels, conv_one[...], maps)
    matrix = second_matrix(conv_two[...])
    channels = conv_two.shape[0]
    lanes = TALL * WIDE
    across = queries.shape[2] // WIDE
    tiles = queries.shape[0]
    for tall in range(tiles // across):
        rows = []
        for pair in range(TALL // 2):
            both = two_rows(maps, matrix, (REACH + TALL * tall) // 2 + pair)
            rows += [both[:channels], both[channels:]]
        for wide, block in enumerate(swap_blocks(rows, WIDE)):
            queries[across * tall + wide] = block.astype(jnp.bfloat16)

    depth = TALL + 2 * REACH
    breadth = WIDE + 2 * EDGE
    own_row = iota((breadth, lanes), 1) // WIDE
    own_col = iota((breadth, lanes), 1) % WIDE
    shift_col = iota((breadth, lanes), 0) - EDGE - own_col
    outside = jnp.where(jnp.abs(shift_col) > REACH, FAR, 0.0)
    for row in range(depth):
        shift_row = row - REACH - own_row
        mask[row] = jnp.where(jnp.abs(shift_row) > REACH, FAR, outside)
    shift_col = shift_col.astype(jnp.float32)
    factor = channels**-0.5 * 1.4426950408889634

    def one_tile(tile):
        tall, wide = tile // across, tile % across
        window = keys[pl.ds(TALL // GROUP * tall, depth // GROUP), pl.ds(WIDE * wide, breadth), :]
        own = queries[tile]
        empty = jnp.zeros_like(own)
        spread = jnp.concatenate(
            [
                jnp.concatenate([own if i == j else empty for j in range(GROUP)], axis=1)
                for i in range(GROUP)
            ],
            axis=0,
        )
        scores = jnp.dot(
            window.reshape(-1, GROUP * channels), spread, preferred_element_type=jnp.float32
        )
        parts = []
        for row in range(depth):
            i, j = row // GROUP, row % GROUP
            part = scores[i * breadth : (i + 1) * breadth, j * lanes : (j + 1) * lanes]
            parts.append(part + mask[row])
        highest = functools.reduce(jnp.maximum, parts)
        highest = jnp.max(highest, axis=0, keepdims=True)
        mass = jnp.zeros((breadth, lanes), jnp.float32)
        once, twice = mass, mass
        for row in range(depth - 1, -1, -1):
            mass = mass + jnp.exp2((parts[row] - highest) * factor)
            if row > 0:
                once = once + mass
                twice = twice + once
        moments = (
            mass,
            once,
            twice,
            mass * shift_col,
            mass * shift_col * shift_col,
            once * shift_col,
        )
        for number, moment in enumerate(moments):
            sums[number, pl.ds(tile, 1), :] = jnp.sum(moment, axis=0, keepdims=True)

    unroll = 2

    def step(number, carry):
        for sub in range(unroll):
            one_tile(number * unroll + sub)
        return carry

    lax.fori_loop(0, tiles // unroll, step, 0)

    total = sums[0]
    row_mean = sums[1] / total
    row_square = (2.0 * sums[2] - sums[1]) / total
    col_mean = sums[3] / total
    col_square = sums[4] / total
    product = sums[5] / total
    var_row = row_square - row_mean * row_mean + PRIOR
    var_col = col_square - col_mean * col_mean + PRIOR
    covar = product - row_mean * col_mean
    mean_row = row_mean - (REACH + iota(total.shape, 1) // WIDE).astype(jnp.float32)
    determ = var_row * var_col - covar * covar
    info_rr = var_col / determ
    info_rc = -covar / determ
    info_cc = var_row / determ
    pull_row = info_rr * mean_row + info_rc * col_mean
    pull_col = info_rc * mean_row + info_cc * col_mean
    fields = jnp.concatenate([info_rr, info_rc, info_cc, pull_row, pull_col], axis=0)

    patch = across * WIDE // NODES
    high, broad = TALL // patch, WIDE // patch
    out_lanes = high * NODES
    source = iota((lanes, out_lanes), 0)
    place = iota((lanes, out_lanes), 1)
    same = (source // WIDE // patch == place // NODES) & (
        source % WIDE // patch == place % NODES % broad
    )
    pool = jnp.where(same, 1.0 / (patch * patch), 0.0)
    pooled = jnp.dot(
        fields, pool, preferred_element_type=jnp.float32, precision=lax.Precision.HIGHEST
    )
    mine = iota(pooled.shape, 0) % across == iota(pooled.shape, 1) % NODES // broad
    pooled = jnp.where(mine, pooled, 0.0)
    pooled = jnp.sum(pooled.reshape(-1, across, out_lanes), axis=1)
    bands = tiles // across
    pieces = []
    for field in range(5):
        for half in range(out_lanes // 128):
            pieces.append(
                pooled[field * bands : (field + 1) * bands, half * 128 : (half + 1) * 128]
            )
    for half in range(out_lanes // 128):
        for band in range(bands):
            start = band * out_lanes + half * 128
            pieces.append(tissue[:, start : start + 128].astype(jnp.float32))
    block = jnp.concatenate(pieces, axis=0)

    def put(peer, carry):
        blocks[peer] = block
        return carry

    lax.fori_loop(0, blocks.shape[0], put, 0)


def solve_kernel(bands, gathered, out, inverse, partial):
    count = gathered.shape[0]
    place = lax.axis_index("gz")
    size = gathered.shape[1] // 6

    def forward(section, carry):
        inv_a, inv_b, inv_c, one, two = carry
        inside = jnp.where(section < count - 1, 1.0, 0.0)
        above = jnp.where(section > 0, 1.0, 0.0)
        extra = SPRING * (inside + above) + ANCHOR
        data = gathered[jnp.minimum(section + 1, count - 1)]
        keep = gathered[section, 5 * size :] * inside
        fields = [data[k * size : (k + 1) * size] * keep for k in range(5)]
        square = SPRING * SPRING * above
        pulled = SPRING * above
        a = fields[0] + extra - square * inv_a
        b = fields[1] - square * inv_b
        c = fields[2] + extra - square * inv_c
        right_one = fields[3] + pulled * one
        right_two = fields[4] + pulled * two
        scale = 1.0 / (a * c - b * b)
        inv_a, inv_b, inv_c = c * scale, -b * scale, a * scale
        one, two = inv_a * right_one + inv_b * right_two, inv_b * right_one + inv_c * right_two
        for k, member in enumerate((inv_a, inv_b, inv_c)):
            inverse[section, k] = member
        partial[section, 0], partial[section, 1] = one, two
        return inv_a, inv_b, inv_c, one, two

    def backward(number, carry):
        one, two, own_one, own_two = carry
        section = count - 1 - number
        inv_a, inv_b, inv_c = (inverse[section, k] for k in range(3))
        fresh_one = partial[section, 0] + SPRING * (inv_a * one + inv_b * two)
        fresh_two = partial[section, 1] + SPRING * (inv_b * one + inv_c * two)
        mine = section == place
        own_one = jnp.where(mine, fresh_one, own_one)
        own_two = jnp.where(mine, fresh_two, own_two)
        return fresh_one, fresh_two, own_one, own_two

    zero = jnp.zeros((size, 128), jnp.float32)
    unroll = count <= 16
    lax.fori_loop(0, count, forward, (zero,) * 5, unroll=unroll)
    _, _, one, two = lax.fori_loop(0, count, backward, (zero,) * 4, unroll=unroll)
    halves = size // bands
    for number, solved in enumerate((one, two)):
        for band in range(bands):
            for half in range(halves):
                row = half * bands + band
                start = (band * halves + half) * 128
                out[number, :, start : start + 128] = solved[row : row + 1]


def body(image, conv_one, conv_two, tissue):
    height, extent = image.shape[1:]
    width = extent // 4
    rows = height // 4
    channels = conv_two.shape[0]
    across, bands = width // WIDE, rows // TALL
    tiles = across * bands
    peers, total = lax.axis_size("gz"), lax.axis_size("gy")
    vmem = pl.BlockSpec(memory_space=pltpu.VMEM)

    main = lax.ppermute(image, "gz", [(z, z + 1) for z in range(peers - 1)])
    top, bottom = image[:, :HALO], image[:, height - HALO :]
    odd = lax.axis_index("gy") % 2 == 1
    pairs = [(y, y + 1) for y in range(0, total - 1, 2)]
    near = lax.ppermute(
        jnp.where(odd, top, bottom), "gy", pairs + [(b, a) for a, b in pairs]
    )
    pairs = [(y, y + 1) for y in range(1, total - 1, 2)]
    far = lax.ppermute(jnp.where(odd, bottom, top), "gy", pairs + [(b, a) for a, b in pairs])
    corner = lax.ppermute(
        bottom,
        ("gz", "gy"),
        [
            (z * total + y, (z + 1) * total + y + 1)
            for z in range(peers - 1)
            for y in range(total - 1)
        ],
    )

    key_rows = rows + 2 * REACH
    map_rows = -(-(2 * key_rows + 1) // CHUNK) * CHUNK
    maps = pltpu.VMEM((map_rows, 3, conv_one.shape[0], width), jnp.bfloat16)
    keys = pl.pallas_call(
        functools.partial(keys_kernel, total),
        out_shape=jax.ShapeDtypeStruct(
            (key_rows // GROUP, width + 2 * EDGE, GROUP * channels), jnp.bfloat16
        ),
        in_specs=[vmem] * 5,
        out_specs=vmem,
        scratch_shapes=[maps],
        name="keys",
        cost_estimate=pl.CostEstimate(flops=10**9, bytes_accessed=2 * 10**6, transcendentals=0),
    )(image, near, far, conv_one, conv_two)

    size = tiles * TALL * WIDE // (width // NODES) ** 2 // 128
    depth = TALL + 2 * REACH
    blocks = pl.pallas_call(
        match_kernel,
        out_shape=jax.ShapeDtypeStruct((peers, 6 * size, 128), jnp.float32),
        in_specs=[vmem] * 6,
        out_specs=vmem,
        scratch_shapes=[
            maps,
            pltpu.VMEM((tiles, channels, TALL * WIDE), jnp.bfloat16),
            pltpu.VMEM((depth, WIDE + 2 * EDGE, TALL * WIDE), jnp.float32),
            pltpu.VMEM((6, tiles, TALL * WIDE), jnp.float32),
        ],
        name="match",
        cost_estimate=pl.CostEstimate(flops=10**9, bytes_accessed=2 * 10**6, transcendentals=0),
    )(main, corner, conv_one, conv_two, keys, tissue)

    gathered = lax.all_to_all(blocks, "gz", split_axis=0, concat_axis=0, tiled=True)
    return pl.pallas_call(
        functools.partial(solve_kernel, bands),
        out_shape=jax.ShapeDtypeStruct((2, 1, tissue.shape[1]), jnp.float32),
        in_specs=[vmem],
        out_specs=vmem,
        scratch_shapes=[
            pltpu.VMEM((peers, 3, size, 128), jnp.float32),
            pltpu.VMEM((peers, 2, size, 128), jnp.float32),
        ],
        name="solve",
    )(gathered)


def solution(mesh):
    placed = (P("gz", "gy", None), P(), P(), P("gz", "gy"))
    return jax.shard_map(
        body, mesh=mesh, in_specs=placed, out_specs=P(None, "gz", "gy"), check_vma=False
    )
```

```python
import functools

import jax
import jax.numpy as jnp
from jax import lax
from jax.experimental import pallas as pl
from jax.experimental.pallas import tpu as pltpu
from jax.sharding import PartitionSpec as P


NODES = 64
REACH = 6
SPRING = 8.0
ANCHOR = 0.02
PRIOR = 1.0

HALO = 32
CHUNK = 32
DEPTH = 80
TALL = 8
WIDE = 16
EDGE = 8
GROUP = 4
FAR = -1e30

FIRST_ROW = HALO - (4 * REACH + 3)


def iota(shape, dim):
    return lax.broadcasted_iota(jnp.int32, shape, dim)


def pick_columns(extent):
    quarter = extent // 4
    parts = []
    for b in range(3):
        source = iota((extent, 2 * quarter), 0)
        place = iota((extent, 2 * quarter), 1)
        wanted = 4 * (place % quarter) + 2 * (place // quarter) + b - 1
        parts.append(jnp.where(source == wanted, 1.0, 0.0).astype(jnp.bfloat16))
    return parts


def first_matrix(conv_one):
    channels = conv_one.shape[0]
    spread = []
    for a in range(3):
        tap = iota((9, 3 * DEPTH), 0)
        b = iota((9, 3 * DEPTH), 1) // DEPTH
        chosen = jnp.where(tap == 3 * a + b, 1.0, 0.0).astype(jnp.bfloat16)
        spread.append(jnp.dot(conv_one, chosen, preferred_element_type=jnp.float32))
    row = iota((channels, 3 * DEPTH), 1) % DEPTH - FIRST_ROW
    blocks = []
    for out in range(CHUNK):
        block = jnp.zeros_like(spread[0])
        for a in range(3):
            block = jnp.where(row == 2 * out + a, spread[a], block)
        blocks.append(block.astype(jnp.bfloat16))
    return jnp.concatenate(blocks, axis=0)


def second_matrix(conv_two):
    taps = conv_two.shape[1]
    inner = taps // 9
    rows = []
    for out in range(2):
        source = iota((taps, 15 * inner), 0)
        place = iota((taps, 15 * inner), 1)
        a = place // (3 * inner) - 2 * out
        b = (place // inner) % 3
        wanted = 9 * (place % inner) + 3 * a + b
        inside = (a >= 0) & (a < 3) & (source == wanted)
        chosen = jnp.where(inside, 1.0, 0.0).astype(jnp.bfloat16)
        rows.append(jnp.dot(conv_two, chosen, preferred_element_type=jnp.float32))
    return jnp.concatenate(rows, axis=0).astype(jnp.bfloat16)


def first_maps(pixels, conv_one, maps):
    extent = pixels.shape[1]
    quarter = extent // 4
    channels = conv_one.shape[0]
    columns = [
        jnp.dot(pixels, part, preferred_element_type=jnp.float32).astype(jnp.bfloat16)
        for part in pick_columns(extent)
    ]
    matrix = first_matrix(conv_one)
    for chunk in range(maps.shape[0] // CHUNK):
        start = 2 * CHUNK * chunk
        taken = jnp.concatenate([part[start : start + DEPTH] for part in columns], axis=0)
        values = jnp.maximum(jnp.dot(matrix, taken, preferred_element_type=jnp.float32), 0.0)
        even, odd = values[:, :quarter], values[:, quarter:]
        before = jnp.where(iota(odd.shape, 1) == 0, 0.0, pltpu.roll(odd, 1, 1))
        for b, part in enumerate((before, even, odd)):
            maps[chunk * CHUNK : (chunk + 1) * CHUNK, b] = part.astype(jnp.bfloat16).reshape(
                CHUNK, channels, quarter
            )


def two_rows(maps, matrix, pair):
    rows = maps[4 * pair : 4 * pair + 5]
    rows = rows.reshape(-1, rows.shape[-1])
    return jnp.maximum(jnp.dot(matrix, rows, preferred_element_type=jnp.float32), 0.0)


def keys_kernel(total, image, near, far, conv_one, conv_two, keys, maps):
    place = lax.axis_index("gy")
    odd = place % 2 == 1
    a, b = near[0], far[0]
    above = jnp.where(odd, a, b)
    below = jnp.where(odd, b, a)
    spare = jnp.zeros((DEPTH - 2 * CHUNK, above.shape[1]), jnp.bfloat16)
    pixels = jnp.concatenate([above, image[0], below, spare], axis=0)
    first_maps(pixels, conv_one[...], maps)
    matrix = second_matrix(conv_two[...])
    channels = conv_two.shape[0]
    local = image.shape[1] // 4
    last = place == total - 1
    edge = jnp.zeros((EDGE, GROUP * channels), jnp.float32)
    for group in range(keys.shape[0]):
        both = [two_rows(maps, matrix, 2 * group + half) for half in range(2)]
        both = jnp.concatenate(both, axis=0)
        if GROUP * (group + 1) > local + REACH:
            row = GROUP * group + iota(both.shape, 0) // channels
            both = jnp.where(last & (row >= local + REACH), 0.0, both)
        turned = jnp.concatenate([edge, both.T, edge], axis=0)
        keys[group] = turned.astype(jnp.bfloat16)


def swap_blocks(rows, width):
    count = len(rows)
    lanes = rows[0].shape[1]
    step = 1
    while step < count:
        low = (iota(rows[0].shape, 1) // width) % (2 * step) < step
        fresh = list(rows)
        for index in range(count):
            if index & step == 0:
                one, two = rows[index], rows[index + step]
                shift = width * step
                fresh[index] = jnp.where(low, one, pltpu.roll(two, shift, 1))
                fresh[index + step] = jnp.where(low, pltpu.roll(one, lanes - shift, 1), two)
        rows = fresh
        step *= 2
    return rows


def match_kernel(image, corner, conv_one, conv_two, keys, tissue, blocks, maps, queries, mask, sums):
    below = jnp.zeros((HALO + DEPTH - 2 * CHUNK, image.shape[2]), jnp.bfloat16)
    pixels = jnp.concatenate([corner[0], image[0], below], axis=0)
    first_maps(pixels, conv_one[...], maps)
    matrix = second_matrix(conv_two[...])
    channels = conv_two.shape[0]
    lanes = TALL * WIDE
    across = queries.shape[2] // WIDE
    tiles = queries.shape[0]
    for tall in range(tiles // across):
        rows = []
        for pair in range(TALL // 2):
            both = two_rows(maps, matrix, (REACH + TALL * tall) // 2 + pair)
            rows += [both[:channels], both[channels:]]
        for wide, block in enumerate(swap_blocks(rows, WIDE)):
            queries[across * tall + wide] = block.astype(jnp.bfloat16)

    depth = TALL + 2 * REACH
    breadth = WIDE + 2 * EDGE
    own_row = iota((breadth, lanes), 1) // WIDE
    own_col = iota((breadth, lanes), 1) % WIDE
    shift_col = iota((breadth, lanes), 0) - EDGE - own_col
    outside = jnp.where(jnp.abs(shift_col) > REACH, FAR, 0.0)
    for row in range(depth):
        shift_row = row - REACH - own_row
        mask[row] = jnp.where(jnp.abs(shift_row) > REACH, FAR, outside)
    shift_col = shift_col.astype(jnp.float32)
    factor = channels**-0.5 * 1.4426950408889634

    def one_tile(tile):
        tall, wide = tile // across, tile % across
        window = keys[pl.ds(TALL // GROUP * tall, depth // GROUP), pl.ds(WIDE * wide, breadth), :]
        own = queries[tile]
        empty = jnp.zeros_like(own)
        spread = jnp.concatenate(
            [
                jnp.concatenate([own if i == j else empty for j in range(GROUP)], axis=1)
                for i in range(GROUP)
            ],
            axis=0,
        )
        scores = jnp.dot(
            window.reshape(-1, GROUP * channels), spread, preferred_element_type=jnp.float32
        )
        parts = []
        for row in range(depth):
            i, j = row // GROUP, row % GROUP
            part = scores[i * breadth : (i + 1) * breadth, j * lanes : (j + 1) * lanes]
            parts.append(part + mask[row])
        highest = functools.reduce(jnp.maximum, parts)
        highest = jnp.max(highest, axis=0, keepdims=True)
        mass = jnp.zeros((breadth, lanes), jnp.float32)
        once, twice = mass, mass
        for row in range(depth - 1, -1, -1):
            mass = mass + jnp.exp2((parts[row] - highest) * factor)
            if row > 0:
                once = once + mass
                twice = twice + once
        moments = (
            mass,
            once,
            twice,
            mass * shift_col,
            mass * shift_col * shift_col,
            once * shift_col,
        )
        for number, moment in enumerate(moments):
            sums[number, pl.ds(tile, 1), :] = jnp.sum(moment, axis=0, keepdims=True)

    unroll = 2

    def step(number, carry):
        for sub in range(unroll):
            one_tile(number * unroll + sub)
        return carry

    lax.fori_loop(0, tiles // unroll, step, 0)

    total = sums[0]
    row_mean = sums[1] / total
    row_square = (2.0 * sums[2] - sums[1]) / total
    col_mean = sums[3] / total
    col_square = sums[4] / total
    product = sums[5] / total
    var_row = row_square - row_mean * row_mean + PRIOR
    var_col = col_square - col_mean * col_mean + PRIOR
    covar = product - row_mean * col_mean
    mean_row = row_mean - (REACH + iota(total.shape, 1) // WIDE).astype(jnp.float32)
    determ = var_row * var_col - covar * covar
    info_rr = var_col / determ
    info_rc = -covar / determ
    info_cc = var_row / determ
    pull_row = info_rr * mean_row + info_rc * col_mean
    pull_col = info_rc * mean_row + info_cc * col_mean
    fields = jnp.concatenate([info_rr, info_rc, info_cc, pull_row, pull_col], axis=0)

    patch = across * WIDE // NODES
    high, broad = TALL // patch, WIDE // patch
    out_lanes = high * NODES
    source = iota((lanes, out_lanes), 0)
    place = iota((lanes, out_lanes), 1)
    same = (source // WIDE // patch == place // NODES) & (
        source % WIDE // patch == place % NODES % broad
    )
    pool = jnp.where(same, 1.0 / (patch * patch), 0.0)
    pooled = jnp.dot(
        fields, pool, preferred_element_type=jnp.float32, precision=lax.Precision.HIGHEST
    )
    mine = iota(pooled.shape, 0) % across == iota(pooled.shape, 1) % NODES // broad
    pooled = jnp.where(mine, pooled, 0.0)
    pooled = jnp.sum(pooled.reshape(-1, across, out_lanes), axis=1)
    bands = tiles // across
    pieces = []
    for field in range(5):
        for half in range(out_lanes // 128):
            pieces.append(
                pooled[field * bands : (field + 1) * bands, half * 128 : (half + 1) * 128]
            )
    for half in range(out_lanes // 128):
        for band in range(bands):
            start = band * out_lanes + half * 128
            pieces.append(tissue[:, start : start + 128].astype(jnp.float32))
    block = jnp.concatenate(pieces, axis=0)

    def put(peer, carry):
        blocks[peer] = block
        return carry

    lax.fori_loop(0, blocks.shape[0], put, 0)


def solve_kernel(bands, gathered, out, inverse, partial):
    count = gathered.shape[0]
    place = lax.axis_index("gz")
    size = gathered.shape[1] // 6

    def forward(section, carry):
        inv_a, inv_b, inv_c, one, two = carry
        inside = jnp.where(section < count - 1, 1.0, 0.0)
        above = jnp.where(section > 0, 1.0, 0.0)
        extra = SPRING * (inside + above) + ANCHOR
        data = gathered[jnp.minimum(section + 1, count - 1)]
        keep = gathered[section, 5 * size :] * inside
        fields = [data[k * size : (k + 1) * size] * keep for k in range(5)]
        square = SPRING * SPRING * above
        pulled = SPRING * above
        a = fields[0] + extra - square * inv_a
        b = fields[1] - square * inv_b
        c = fields[2] + extra - square * inv_c
        right_one = fields[3] + pulled * one
        right_two = fields[4] + pulled * two
        scale = 1.0 / (a * c - b * b)
        inv_a, inv_b, inv_c = c * scale, -b * scale, a * scale
        one, two = inv_a * right_one + inv_b * right_two, inv_b * right_one + inv_c * right_two
        for k, member in enumerate((inv_a, inv_b, inv_c)):
            inverse[section, k] = member
        partial[section, 0], partial[section, 1] = one, two
        return inv_a, inv_b, inv_c, one, two

    def backward(number, carry):
        one, two, own_one, own_two = carry
        section = count - 1 - number
        inv_a, inv_b, inv_c = (inverse[section, k] for k in range(3))
        fresh_one = partial[section, 0] + SPRING * (inv_a * one + inv_b * two)
        fresh_two = partial[section, 1] + SPRING * (inv_b * one + inv_c * two)
        mine = section == place
        own_one = jnp.where(mine, fresh_one, own_one)
        own_two = jnp.where(mine, fresh_two, own_two)
        return fresh_one, fresh_two, own_one, own_two

    zero = jnp.zeros((size, 128), jnp.float32)
    unroll = count <= 16
    lax.fori_loop(0, count, forward, (zero,) * 5, unroll=unroll)
    _, _, one, two = lax.fori_loop(0, count, backward, (zero,) * 4, unroll=unroll)
    halves = size // bands
    for number, solved in enumerate((one, two)):
        for band in range(bands):
            for half in range(halves):
                row = half * bands + band
                start = (band * halves + half) * 128
                out[number, :, start : start + 128] = solved[row : row + 1]


def body(image, conv_one, conv_two, tissue):
    height, extent = image.shape[1:]
    width = extent // 4
    rows = height // 4
    channels = conv_two.shape[0]
    across, bands = width // WIDE, rows // TALL
    tiles = across * bands
    peers, total = lax.axis_size("gz"), lax.axis_size("gy")
    vmem = pl.BlockSpec(memory_space=pltpu.VMEM)

    main = lax.ppermute(image, "gz", [(z, z + 1) for z in range(peers - 1)])
    top, bottom = image[:, :HALO], image[:, height - HALO :]
    odd = lax.axis_index("gy") % 2 == 1
    pairs = [(y, y + 1) for y in range(0, total - 1, 2)]
    near = lax.ppermute(
        jnp.where(odd, top, bottom), "gy", pairs + [(b, a) for a, b in pairs]
    )
    pairs = [(y, y + 1) for y in range(1, total - 1, 2)]
    far = lax.ppermute(jnp.where(odd, bottom, top), "gy", pairs + [(b, a) for a, b in pairs])
    corner = lax.ppermute(
        bottom,
        ("gz", "gy"),
        [
            (z * total + y, (z + 1) * total + y + 1)
            for z in range(peers - 1)
            for y in range(total - 1)
        ],
    )

    key_rows = rows + 2 * REACH
    map_rows = -(-(2 * key_rows + 1) // CHUNK) * CHUNK
    maps = pltpu.VMEM((map_rows, 3, conv_one.shape[0], width), jnp.bfloat16)
    keys = pl.pallas_call(
        functools.partial(keys_kernel, total),
        out_shape=jax.ShapeDtypeStruct(
            (key_rows // GROUP, width + 2 * EDGE, GROUP * channels), jnp.bfloat16
        ),
        in_specs=[vmem] * 5,
        out_specs=vmem,
        scratch_shapes=[maps],
        compiler_params=pltpu.CompilerParams(vmem_limit_bytes=16 << 20),
        name="keys",
        cost_estimate=pl.CostEstimate(flops=10**9, bytes_accessed=2 * 10**6, transcendentals=0),
    )(image, near, far, conv_one, conv_two)

    size = tiles * TALL * WIDE // (width // NODES) ** 2 // 128
    depth = TALL + 2 * REACH
    blocks = pl.pallas_call(
        match_kernel,
        out_shape=jax.ShapeDtypeStruct((peers, 6 * size, 128), jnp.float32),
        in_specs=[vmem] * 6,
        out_specs=vmem,
        scratch_shapes=[
            maps,
            pltpu.VMEM((tiles, channels, TALL * WIDE), jnp.bfloat16),
            pltpu.VMEM((depth, WIDE + 2 * EDGE, TALL * WIDE), jnp.float32),
            pltpu.VMEM((6, tiles, TALL * WIDE), jnp.float32),
        ],
        compiler_params=pltpu.CompilerParams(vmem_limit_bytes=16 << 20),
        name="match",
        cost_estimate=pl.CostEstimate(flops=10**9, bytes_accessed=2 * 10**6, transcendentals=0),
    )(main, corner, conv_one, conv_two, keys, tissue)

    gathered = lax.all_to_all(blocks, "gz", split_axis=0, concat_axis=0, tiled=True)
    return pl.pallas_call(
        functools.partial(solve_kernel, bands),
        out_shape=jax.ShapeDtypeStruct((2, 1, tissue.shape[1]), jnp.float32),
        in_specs=[vmem],
        out_specs=vmem,
        scratch_shapes=[
            pltpu.VMEM((peers, 3, size, 128), jnp.float32),
            pltpu.VMEM((peers, 2, size, 128), jnp.float32),
        ],
        compiler_params=pltpu.CompilerParams(vmem_limit_bytes=16 << 20),
        name="solve",
    )(gathered)


def solution(mesh):
    placed = (P("gz", "gy", None), P(), P(), P("gz", "gy"))
    return jax.shard_map(
        body, mesh=mesh, in_specs=placed, out_specs=P(None, "gz", "gy"), check_vma=False
    )
```

```python
import functools

import jax
import jax.numpy as jnp
from jax import lax
from jax.experimental import pallas as pl
from jax.experimental.pallas import tpu as pltpu
from jax.sharding import PartitionSpec as P


NODES = 64
REACH = 6
SPRING = 8.0
ANCHOR = 0.02
PRIOR = 1.0

HALO = 32
CHUNK = 32
DEPTH = 80
TALL = 8
WIDE = 16
EDGE = 8
GROUP = 4
FAR = -1e30
UNROLL = 32

FIRST_ROW = HALO - (4 * REACH + 3)


def iota(shape, dim):
    return lax.broadcasted_iota(jnp.int32, shape, dim)


def pick_columns(extent):
    quarter = extent // 4
    parts = []
    for b in range(3):
        source = iota((extent, 2 * quarter), 0)
        place = iota((extent, 2 * quarter), 1)
        wanted = 4 * (place % quarter) + 2 * (place // quarter) + b - 1
        parts.append(jnp.where(source == wanted, 1.0, 0.0).astype(jnp.bfloat16))
    return parts


def first_matrix(conv_one):
    channels = conv_one.shape[0]
    spread = []
    for a in range(3):
        tap = iota((9, 3 * DEPTH), 0)
        b = iota((9, 3 * DEPTH), 1) // DEPTH
        chosen = jnp.where(tap == 3 * a + b, 1.0, 0.0).astype(jnp.bfloat16)
        spread.append(jnp.dot(conv_one, chosen, preferred_element_type=jnp.float32))
    row = iota((channels, 3 * DEPTH), 1) % DEPTH - FIRST_ROW
    blocks = []
    for out in range(CHUNK):
        block = jnp.zeros_like(spread[0])
        for a in range(3):
            block = jnp.where(row == 2 * out + a, spread[a], block)
        blocks.append(block.astype(jnp.bfloat16))
    return jnp.concatenate(blocks, axis=0)


def second_matrix(conv_two):
    taps = conv_two.shape[1]
    inner = taps // 9
    rows = []
    for out in range(2):
        source = iota((taps, 15 * inner), 0)
        place = iota((taps, 15 * inner), 1)
        a = place // (3 * inner) - 2 * out
        b = (place // inner) % 3
        wanted = 9 * (place % inner) + 3 * a + b
        inside = (a >= 0) & (a < 3) & (source == wanted)
        chosen = jnp.where(inside, 1.0, 0.0).astype(jnp.bfloat16)
        rows.append(jnp.dot(conv_two, chosen, preferred_element_type=jnp.float32))
    return jnp.concatenate(rows, axis=0).astype(jnp.bfloat16)


def first_maps(pixels, picks, matrix, maps):
    extent = pixels.shape[1]
    quarter = extent // 4
    channels = maps.shape[2]
    columns = [
        jnp.dot(pixels, part, preferred_element_type=jnp.float32).astype(jnp.bfloat16)
        for part in picks
    ]
    for chunk in range(maps.shape[0] // CHUNK):
        start = 2 * CHUNK * chunk
        taken = jnp.concatenate([part[start : start + DEPTH] for part in columns], axis=0)
        values = jnp.maximum(jnp.dot(matrix, taken, preferred_element_type=jnp.float32), 0.0)
        even, odd = values[:, :quarter], values[:, quarter:]
        before = jnp.where(iota(odd.shape, 1) == 0, 0.0, pltpu.roll(odd, 1, 1))
        for b, part in enumerate((before, even, odd)):
            maps[chunk * CHUNK : (chunk + 1) * CHUNK, b] = part.astype(jnp.bfloat16).reshape(
                CHUNK, channels, quarter
            )


def two_rows(maps, matrix, pair):
    rows = maps[4 * pair : 4 * pair + 5]
    rows = rows.reshape(-1, rows.shape[-1])
    return jnp.maximum(jnp.dot(matrix, rows, preferred_element_type=jnp.float32), 0.0)


def keys_kernel(
    total, image, near, far, conv_one, conv_two, keys, columns, matrix_one, matrix_two, maps
):
    place = lax.axis_index("gy")
    odd = place % 2 == 1
    a, b = near[0], far[0]
    above = jnp.where(odd, a, b)
    below = jnp.where(odd, b, a)
    spare = jnp.zeros((DEPTH - 2 * CHUNK, above.shape[1]), jnp.bfloat16)
    pixels = jnp.concatenate([above, image[0], below, spare], axis=0)
    picks = pick_columns(image.shape[2])
    for b, part in enumerate(picks):
        columns[b] = part
    first = first_matrix(conv_one[...])
    matrix_one[...] = first
    first_maps(pixels, picks, first, maps)
    matrix = second_matrix(conv_two[...])
    matrix_two[...] = matrix
    channels = conv_two.shape[0]
    local = image.shape[1] // 4
    last = place == total - 1
    edge = jnp.zeros((EDGE, GROUP * channels), jnp.float32)
    for group in range(keys.shape[0]):
        both = [two_rows(maps, matrix, 2 * group + half) for half in range(2)]
        both = jnp.concatenate(both, axis=0)
        if GROUP * (group + 1) > local + REACH:
            row = GROUP * group + iota(both.shape, 0) // channels
            both = jnp.where(last & (row >= local + REACH), 0.0, both)
        turned = jnp.concatenate([edge, both.T, edge], axis=0)
        keys[group] = turned.astype(jnp.bfloat16)


def swap_blocks(rows, width):
    count = len(rows)
    lanes = rows[0].shape[1]
    step = 1
    while step < count:
        low = (iota(rows[0].shape, 1) // width) % (2 * step) < step
        fresh = list(rows)
        for index in range(count):
            if index & step == 0:
                one, two = rows[index], rows[index + step]
                shift = width * step
                fresh[index] = jnp.where(low, one, pltpu.roll(two, shift, 1))
                fresh[index + step] = jnp.where(low, pltpu.roll(one, lanes - shift, 1), two)
        rows = fresh
        step *= 2
    return rows


def match_kernel(
    image, corner, columns, matrix_one, matrix_two, keys, tissue, blocks, maps, queries, sums
):
    below = jnp.zeros((HALO + DEPTH - 2 * CHUNK, image.shape[2]), jnp.bfloat16)
    pixels = jnp.concatenate([corner[0], image[0], below], axis=0)
    first_maps(pixels, [columns[b] for b in range(3)], matrix_one[...], maps)
    matrix = matrix_two[...]
    channels = queries.shape[1]
    lanes = TALL * WIDE
    across = queries.shape[2] // WIDE
    tiles = queries.shape[0]
    for tall in range(tiles // across):
        rows = []
        for pair in range(TALL // 2):
            both = two_rows(maps, matrix, (REACH + TALL * tall) // 2 + pair)
            rows += [both[:channels], both[channels:]]
        for wide, block in enumerate(swap_blocks(rows, WIDE)):
            queries[across * tall + wide] = block.astype(jnp.bfloat16)

    depth, breadth = TALL + 2 * REACH, 2 * WIDE
    span = 2 * REACH + 1
    own_row = iota((WIDE, lanes), 1) // WIDE
    own_col = iota((WIDE, lanes), 1) % WIDE
    shift_col = iota((WIDE, lanes), 0) - EDGE - own_col
    left = shift_col >= -REACH
    shift_col = jnp.where(left, shift_col, shift_col + WIDE)
    outside = jnp.where(jnp.abs(shift_col) > REACH, FAR, 0.0)
    shift_col = shift_col.astype(jnp.float32)
    own_row = own_row[:8]
    shift_row = []
    for row in range(span):
        shift = row - REACH - own_row
        shift_row.append(jnp.where(shift < -REACH, shift + span, shift).astype(jnp.float32))
    factor = channels**-0.5 * 1.4426950408889634

    def one_tile(tile):
        tall, wide = tile // across, tile % across
        window = keys[pl.ds(TALL // GROUP * tall, depth // GROUP), pl.ds(WIDE * wide, breadth), :]
        own = queries[tile]
        empty = jnp.zeros_like(own)
        spread = jnp.concatenate(
            [
                jnp.concatenate([own if i == j else empty for j in range(GROUP)], axis=1)
                for i in range(GROUP)
            ],
            axis=0,
        )
        scores = jnp.dot(
            window.reshape(-1, GROUP * channels), spread, preferred_element_type=jnp.float32
        )
        parts = []
        for row in range(depth):
            i, j = row // GROUP, row % GROUP
            part = scores[i * breadth : (i + 1) * breadth, j * lanes : (j + 1) * lanes]
            parts.append(jnp.where(left, part[:WIDE], part[WIDE:]))
        for row in range(depth - span):
            low = iota((WIDE, lanes), 1) // WIDE <= row
            parts[row] = jnp.where(low, parts[row], parts[row + span])
        parts = [part + outside for part in parts[:span]]
        highest = functools.reduce(jnp.maximum, parts)
        highest = jnp.max(highest, axis=0, keepdims=True)
        mass = jnp.zeros((WIDE, lanes), jnp.float32)
        once = mass
        twice = jnp.zeros((8, lanes), jnp.float32)
        for row in range(span):
            prob = jnp.exp2((parts[row] - highest) * factor)
            mass = mass + prob
            weighted = (prob.reshape(-1, 8, lanes) * shift_row[row]).reshape(WIDE, lanes)
            once = once + weighted
            twice = twice + jnp.sum(weighted.reshape(-1, 8, lanes), axis=0) * shift_row[row]
        moments = (
            mass,
            once,
            twice,
            mass * shift_col,
            mass * shift_col * shift_col,
            once * shift_col,
        )
        for number, moment in enumerate(moments):
            sums[number, pl.ds(tile, 1), :] = jnp.sum(moment, axis=0, keepdims=True)

    unroll = min(UNROLL, tiles)

    def step(number, carry):
        for sub in range(unroll):
            one_tile(number * unroll + sub)
        return carry

    if unroll == tiles:
        step(0, 0)
    else:
        lax.fori_loop(0, tiles // unroll, step, 0)

    total = sums[0]
    mean_row = sums[1] / total
    row_square = sums[2] / total
    col_mean = sums[3] / total
    col_square = sums[4] / total
    product = sums[5] / total
    var_row = row_square - mean_row * mean_row + PRIOR
    var_col = col_square - col_mean * col_mean + PRIOR
    covar = product - mean_row * col_mean
    determ = var_row * var_col - covar * covar
    info_rr = var_col / determ
    info_rc = -covar / determ
    info_cc = var_row / determ
    pull_row = info_rr * mean_row + info_rc * col_mean
    pull_col = info_rc * mean_row + info_cc * col_mean
    fields = jnp.concatenate([info_rr, info_rc, info_cc, pull_row, pull_col], axis=0)

    patch = across * WIDE // NODES
    high, broad = TALL // patch, WIDE // patch
    out_lanes = high * NODES
    source = iota((lanes, out_lanes), 0)
    place = iota((lanes, out_lanes), 1)
    same = (source // WIDE // patch == place // NODES) & (
        source % WIDE // patch == place % NODES % broad
    )
    pool = jnp.where(same, 1.0 / (patch * patch), 0.0)
    pooled = jnp.dot(
        fields, pool, preferred_element_type=jnp.float32, precision=lax.Precision.HIGHEST
    )
    mine = iota(pooled.shape, 0) % across == iota(pooled.shape, 1) % NODES // broad
    pooled = jnp.where(mine, pooled, 0.0)
    pooled = jnp.sum(pooled.reshape(-1, across, out_lanes), axis=1)
    bands = tiles // across
    pieces = []
    for field in range(5):
        for half in range(out_lanes // 128):
            pieces.append(
                pooled[field * bands : (field + 1) * bands, half * 128 : (half + 1) * 128]
            )
    for half in range(out_lanes // 128):
        for band in range(bands):
            start = band * out_lanes + half * 128
            pieces.append(tissue[:, start : start + 128].astype(jnp.float32))
    block = jnp.concatenate(pieces, axis=0)

    def put(peer, carry):
        blocks[peer] = block
        return carry

    lax.fori_loop(0, blocks.shape[0], put, 0)


def solve_kernel(bands, gathered, out, inverse, partial):
    count = gathered.shape[0]
    place = lax.axis_index("gz")
    size = gathered.shape[1] // 6

    def forward(section, carry):
        inv_a, inv_b, inv_c, one, two = carry
        inside = jnp.where(section < count - 1, 1.0, 0.0)
        above = jnp.where(section > 0, 1.0, 0.0)
        extra = SPRING * (inside + above) + ANCHOR
        data = gathered[jnp.minimum(section + 1, count - 1)]
        keep = gathered[section, 5 * size :] * inside
        fields = [data[k * size : (k + 1) * size] * keep for k in range(5)]
        square = SPRING * SPRING * above
        pulled = SPRING * above
        a = fields[0] + extra - square * inv_a
        b = fields[1] - square * inv_b
        c = fields[2] + extra - square * inv_c
        right_one = fields[3] + pulled * one
        right_two = fields[4] + pulled * two
        scale = 1.0 / (a * c - b * b)
        inv_a, inv_b, inv_c = c * scale, -b * scale, a * scale
        one, two = inv_a * right_one + inv_b * right_two, inv_b * right_one + inv_c * right_two
        for k, member in enumerate((inv_a, inv_b, inv_c)):
            inverse[section, k] = member
        partial[section, 0], partial[section, 1] = one, two
        return inv_a, inv_b, inv_c, one, two

    def backward(number, carry):
        one, two, own_one, own_two = carry
        section = count - 1 - number
        inv_a, inv_b, inv_c = (inverse[section, k] for k in range(3))
        fresh_one = partial[section, 0] + SPRING * (inv_a * one + inv_b * two)
        fresh_two = partial[section, 1] + SPRING * (inv_b * one + inv_c * two)
        mine = section == place
        own_one = jnp.where(mine, fresh_one, own_one)
        own_two = jnp.where(mine, fresh_two, own_two)
        return fresh_one, fresh_two, own_one, own_two

    zero = jnp.zeros((size, 128), jnp.float32)
    unroll = count <= 16
    lax.fori_loop(0, count, forward, (zero,) * 5, unroll=unroll)
    _, _, one, two = lax.fori_loop(0, count, backward, (zero,) * 4, unroll=unroll)
    halves = size // bands
    for number, solved in enumerate((one, two)):
        for band in range(bands):
            for half in range(halves):
                row = half * bands + band
                start = (band * halves + half) * 128
                out[number, :, start : start + 128] = solved[row : row + 1]


def body(image, conv_one, conv_two, tissue):
    height, extent = image.shape[1:]
    width = extent // 4
    rows = height // 4
    channels = conv_two.shape[0]
    across, bands = width // WIDE, rows // TALL
    tiles = across * bands
    peers, total = lax.axis_size("gz"), lax.axis_size("gy")
    vmem = pl.BlockSpec(memory_space=pltpu.VMEM)

    main = lax.ppermute(image, "gz", [(z, z + 1) for z in range(peers - 1)])
    top, bottom = image[:, :HALO], image[:, height - HALO :]
    odd = lax.axis_index("gy") % 2 == 1
    pairs = [(y, y + 1) for y in range(0, total - 1, 2)]
    near = lax.ppermute(
        jnp.where(odd, top, bottom), "gy", pairs + [(b, a) for a, b in pairs]
    )
    pairs = [(y, y + 1) for y in range(1, total - 1, 2)]
    far = lax.ppermute(jnp.where(odd, bottom, top), "gy", pairs + [(b, a) for a, b in pairs])
    corner = lax.ppermute(
        bottom,
        ("gz", "gy"),
        [
            (z * total + y, (z + 1) * total + y + 1)
            for z in range(peers - 1)
            for y in range(total - 1)
        ],
    )

    key_rows = rows + 2 * REACH
    map_rows = -(-(2 * key_rows + 1) // CHUNK) * CHUNK
    maps = pltpu.VMEM((map_rows, 3, conv_one.shape[0], width), jnp.bfloat16)
    inner = conv_one.shape[0]
    shapes = (
        (key_rows // GROUP, width + 2 * EDGE, GROUP * channels),
        (3, extent, 2 * width),
        (CHUNK * inner, 3 * DEPTH),
        (2 * channels, 15 * inner),
    )
    keys, *matrices = pl.pallas_call(
        functools.partial(keys_kernel, total),
        out_shape=[jax.ShapeDtypeStruct(shape, jnp.bfloat16) for shape in shapes],
        in_specs=[vmem] * 5,
        out_specs=[vmem] * 4,
        scratch_shapes=[maps],
        compiler_params=pltpu.CompilerParams(vmem_limit_bytes=16 << 20),
        name="keys",
        cost_estimate=pl.CostEstimate(flops=10**9, bytes_accessed=2 * 10**6, transcendentals=0),
    )(image, near, far, conv_one, conv_two)

    size = tiles * TALL * WIDE // (width // NODES) ** 2 // 128
    blocks = pl.pallas_call(
        match_kernel,
        out_shape=jax.ShapeDtypeStruct((peers, 6 * size, 128), jnp.float32),
        in_specs=[vmem] * 7,
        out_specs=vmem,
        scratch_shapes=[
            maps,
            pltpu.VMEM((tiles, channels, TALL * WIDE), jnp.bfloat16),
            pltpu.VMEM((6, tiles, TALL * WIDE), jnp.float32),
        ],
        compiler_params=pltpu.CompilerParams(vmem_limit_bytes=16 << 20),
        name="match",
        cost_estimate=pl.CostEstimate(flops=10**9, bytes_accessed=2 * 10**6, transcendentals=0),
    )(main, corner, *matrices, keys, tissue)

    gathered = lax.all_to_all(blocks, "gz", split_axis=0, concat_axis=0, tiled=True)
    return pl.pallas_call(
        functools.partial(solve_kernel, bands),
        out_shape=jax.ShapeDtypeStruct((2, 1, tissue.shape[1]), jnp.float32),
        in_specs=[vmem],
        out_specs=vmem,
        scratch_shapes=[
            pltpu.VMEM((peers, 3, size, 128), jnp.float32),
            pltpu.VMEM((peers, 2, size, 128), jnp.float32),
        ],
        compiler_params=pltpu.CompilerParams(vmem_limit_bytes=16 << 20),
        name="solve",
    )(gathered)


def solution(mesh):
    placed = (P("gz", "gy", None), P(), P(), P("gz", "gy"))
    return jax.shard_map(
        body, mesh=mesh, in_specs=placed, out_specs=P(None, "gz", "gy"), check_vma=False
    )
```

```python
import functools

import jax
import jax.numpy as jnp
from jax import lax
from jax.experimental import pallas as pl
from jax.experimental.pallas import tpu as pltpu
from jax.sharding import PartitionSpec as P


NODES = 64
REACH = 6
SPRING = 8.0
ANCHOR = 0.02
PRIOR = 1.0

HALO = 32
CHUNK = 32
DEPTH = 80
TALL = 8
WIDE = 16
EDGE = 8
GROUP = 4
FAR = -1e30

FIRST_ROW = HALO - (4 * REACH + 3)


def iota(shape, dim):
    return lax.broadcasted_iota(jnp.int32, shape, dim)


def pick_columns(extent):
    quarter = extent // 4
    parts = []
    for b in range(3):
        source = iota((extent, 2 * quarter), 0)
        place = iota((extent, 2 * quarter), 1)
        wanted = 4 * (place % quarter) + 2 * (place // quarter) + b - 1
        parts.append(jnp.where(source == wanted, 1.0, 0.0).astype(jnp.bfloat16))
    return parts


def first_matrix(conv_one):
    channels = conv_one.shape[0]
    spread = []
    for a in range(3):
        tap = iota((9, 3 * DEPTH), 0)
        b = iota((9, 3 * DEPTH), 1) // DEPTH
        chosen = jnp.where(tap == 3 * a + b, 1.0, 0.0).astype(jnp.bfloat16)
        spread.append(jnp.dot(conv_one, chosen, preferred_element_type=jnp.float32))
    row = iota((channels, 3 * DEPTH), 1) % DEPTH - FIRST_ROW
    blocks = []
    for out in range(CHUNK):
        block = jnp.zeros_like(spread[0])
        for a in range(3):
            block = jnp.where(row == 2 * out + a, spread[a], block)
        blocks.append(block.astype(jnp.bfloat16))
    return jnp.concatenate(blocks, axis=0)


def second_matrix(conv_two):
    taps = conv_two.shape[1]
    inner = taps // 9
    rows = []
    for out in range(2):
        source = iota((taps, 15 * inner), 0)
        place = iota((taps, 15 * inner), 1)
        a = place // (3 * inner) - 2 * out
        b = (place // inner) % 3
        wanted = 9 * (place % inner) + 3 * a + b
        inside = (a >= 0) & (a < 3) & (source == wanted)
        chosen = jnp.where(inside, 1.0, 0.0).astype(jnp.bfloat16)
        rows.append(jnp.dot(conv_two, chosen, preferred_element_type=jnp.float32))
    return jnp.concatenate(rows, axis=0).astype(jnp.bfloat16)


def split_columns(pixels, picks):
    return [
        jnp.dot(pixels, part, preferred_element_type=jnp.float32).astype(jnp.bfloat16)
        for part in picks
    ]


def first_maps(columns, matrix, maps, start):
    channels, quarter = maps.shape[2:]
    taken = jnp.concatenate([part[start : start + DEPTH] for part in columns], axis=0)
    values = jnp.maximum(jnp.dot(matrix, taken, preferred_element_type=jnp.float32), 0.0)
    even, odd = values[:, :quarter], values[:, quarter:]
    before = jnp.where(iota(odd.shape, 1) == 0, 0.0, pltpu.roll(odd, 1, 1))
    for b, part in enumerate((before, even, odd)):
        maps[:, b] = part.astype(jnp.bfloat16).reshape(-1, channels, quarter)


def all_maps(pixels, picks, matrix, maps):
    columns = split_columns(pixels, picks)
    for chunk in range(maps.shape[0] // CHUNK):
        first_maps(
            columns, matrix, maps.at[chunk * CHUNK : (chunk + 1) * CHUNK], 2 * CHUNK * chunk
        )


def two_rows(maps, matrix, pair):
    rows = maps[4 * pair : 4 * pair + 5]
    rows = rows.reshape(-1, rows.shape[-1])
    return jnp.maximum(jnp.dot(matrix, rows, preferred_element_type=jnp.float32), 0.0)


def keys_kernel(
    total, image, near, far, conv_one, conv_two, keys, columns, matrix_one, matrix_two, maps
):
    place = lax.axis_index("gy")
    odd = place % 2 == 1
    a, b = near[0], far[0]
    above = jnp.where(odd, a, b)
    below = jnp.where(odd, b, a)
    spare = jnp.zeros((DEPTH - 2 * CHUNK, above.shape[1]), jnp.bfloat16)
    pixels = jnp.concatenate([above, image[0], below, spare], axis=0)
    picks = pick_columns(image.shape[2])
    for b, part in enumerate(picks):
        columns[b] = part
    first = first_matrix(conv_one[...])
    matrix_one[...] = first
    all_maps(pixels, picks, first, maps)
    matrix = second_matrix(conv_two[...])
    matrix_two[...] = matrix
    channels = conv_two.shape[0]
    local = image.shape[1] // 4
    last = place == total - 1
    edge = jnp.zeros((EDGE, GROUP * channels), jnp.float32)
    for group in range(keys.shape[0]):
        both = [two_rows(maps, matrix, 2 * group + half) for half in range(2)]
        both = jnp.concatenate(both, axis=0)
        if GROUP * (group + 1) > local + REACH:
            row = GROUP * group + iota(both.shape, 0) // channels
            both = jnp.where(last & (row >= local + REACH), 0.0, both)
        turned = jnp.concatenate([edge, both.T, edge], axis=0)
        keys[group] = turned.astype(jnp.bfloat16)


def swap_blocks(rows, width):
    count = len(rows)
    lanes = rows[0].shape[1]
    step = 1
    while step < count:
        low = (iota(rows[0].shape, 1) // width) % (2 * step) < step
        fresh = list(rows)
        for index in range(count):
            if index & step == 0:
                one, two = rows[index], rows[index + step]
                shift = width * step
                fresh[index] = jnp.where(low, one, pltpu.roll(two, shift, 1))
                fresh[index + step] = jnp.where(low, pltpu.roll(one, lanes - shift, 1), two)
        rows = fresh
        step *= 2
    return rows


def match_tiles(queries, keys, sums, band):
    channels = queries.shape[1]
    lanes = TALL * WIDE
    tiles = queries.shape[0]
    across = (keys.shape[1] - 2 * EDGE) // WIDE
    depth, breadth = TALL + 2 * REACH, 2 * WIDE
    span = 2 * REACH + 1
    own_row = iota((WIDE, lanes), 1) // WIDE
    own_col = iota((WIDE, lanes), 1) % WIDE
    shift_col = iota((WIDE, lanes), 0) - EDGE - own_col
    left = shift_col >= -REACH
    shift_col = jnp.where(left, shift_col, shift_col + WIDE)
    outside = jnp.where(jnp.abs(shift_col) > REACH, FAR, 0.0)
    shift_col = shift_col.astype(jnp.float32)
    shift_row = []
    for row in range(span):
        shift = row - REACH - own_row[:8]
        shift_row.append(jnp.where(shift < -REACH, shift + span, shift).astype(jnp.float32))
    factor = channels**-0.5 * 1.4426950408889634

    for tile in range(tiles):
        tall, wide = band + tile // across, tile % across
        window = keys[
            TALL // GROUP * tall : TALL // GROUP * tall + depth // GROUP,
            WIDE * wide : WIDE * wide + breadth,
            :,
        ]
        own = queries[tile]
        empty = jnp.zeros_like(own)
        spread = jnp.concatenate(
            [
                jnp.concatenate([own if i == j else empty for j in range(GROUP)], axis=1)
                for i in range(GROUP)
            ],
            axis=0,
        )
        scores = jnp.dot(
            window.reshape(-1, GROUP * channels), spread, preferred_element_type=jnp.float32
        )
        parts = []
        for row in range(depth):
            i, j = row // GROUP, row % GROUP
            part = scores[i * breadth : (i + 1) * breadth, j * lanes : (j + 1) * lanes]
            parts.append(jnp.where(left, part[:WIDE], part[WIDE:]))
        for row in range(depth - span):
            parts[row] = jnp.where(own_row <= row, parts[row], parts[row + span])
        parts = [part + outside for part in parts[:span]]
        highest = functools.reduce(jnp.maximum, parts)
        highest = jnp.max(highest, axis=0, keepdims=True)
        mass = jnp.zeros((WIDE, lanes), jnp.float32)
        once = mass
        twice = jnp.zeros((8, lanes), jnp.float32)
        for row in range(span):
            prob = jnp.exp2((parts[row] - highest) * factor)
            mass = mass + prob
            weighted = (prob.reshape(-1, 8, lanes) * shift_row[row]).reshape(WIDE, lanes)
            once = once + weighted
            twice = twice + jnp.sum(weighted.reshape(-1, 8, lanes), axis=0) * shift_row[row]
        moments = (
            mass,
            once,
            twice,
            mass * shift_col,
            mass * shift_col * shift_col,
            once * shift_col,
        )
        for number, moment in enumerate(moments):
            sums[number, tile : tile + 1, :] = jnp.sum(moment, axis=0, keepdims=True)


def pooled_fields(sums, across):
    total = sums[0]
    mean_row = sums[1] / total
    row_square = sums[2] / total
    col_mean = sums[3] / total
    col_square = sums[4] / total
    product = sums[5] / total
    var_row = row_square - mean_row * mean_row + PRIOR
    var_col = col_square - col_mean * col_mean + PRIOR
    covar = product - mean_row * col_mean
    determ = var_row * var_col - covar * covar
    info_rr = var_col / determ
    info_rc = -covar / determ
    info_cc = var_row / determ
    pull_row = info_rr * mean_row + info_rc * col_mean
    pull_col = info_rc * mean_row + info_cc * col_mean
    fields = jnp.concatenate([info_rr, info_rc, info_cc, pull_row, pull_col], axis=0)

    lanes = TALL * WIDE
    patch = across * WIDE // NODES
    high, broad = TALL // patch, WIDE // patch
    out_lanes = high * NODES
    source = iota((lanes, out_lanes), 0)
    place = iota((lanes, out_lanes), 1)
    same = (source // WIDE // patch == place // NODES) & (
        source % WIDE // patch == place % NODES % broad
    )
    pool = jnp.where(same, 1.0 / (patch * patch), 0.0)
    pooled = jnp.dot(
        fields, pool, preferred_element_type=jnp.float32, precision=lax.Precision.HIGHEST
    )
    mine = iota(pooled.shape, 0) % across == iota(pooled.shape, 1) % NODES // broad
    pooled = jnp.where(mine, pooled, 0.0)
    return jnp.sum(pooled.reshape(-1, across, out_lanes), axis=1)


def rest_kernel(image, columns, matrix_one, matrix_two, keys, pooled, kept, maps, queries, sums):
    extent = image.shape[2]
    above = jnp.zeros((HALO, extent), jnp.bfloat16)
    below = jnp.zeros((HALO + DEPTH - 2 * CHUNK, extent), jnp.bfloat16)
    pixels = jnp.concatenate([above, image[0], below], axis=0)
    all_maps(pixels, [columns[b] for b in range(3)], matrix_one[...], maps)
    matrix = matrix_two[...]
    channels = queries.shape[1]
    across = (keys.shape[1] - 2 * EDGE) // WIDE
    for band in range(queries.shape[0] // across + 1):
        rows = []
        for pair in range(TALL // 2):
            if band + pair == 0:
                continue
            both = two_rows(maps, matrix, (REACH + TALL * band) // 2 + pair)
            rows += [both[:channels], both[channels:]]
        if band == 0:
            for number, row in enumerate(rows):
                kept[number] = row
            continue
        for wide, block in enumerate(swap_blocks(rows, WIDE)):
            queries[across * (band - 1) + wide] = block.astype(jnp.bfloat16)
    match_tiles(queries, keys, sums, 1)
    pooled[...] = pooled_fields(sums, across)


def first_kernel(
    image, corner, columns, matrix_one, matrix_two, keys, kept, pooled, tissue,
    blocks, maps, queries, sums,
):
    channels = queries.shape[1]
    across = queries.shape[0]
    pixels = jnp.concatenate([corner[0], image[0, : DEPTH - HALO]], axis=0)
    begin = 2 * REACH * matrix_one.shape[0] // CHUNK
    matrix = matrix_one[begin : begin + maps.shape[0] * maps.shape[2]]
    first_maps(split_columns(pixels, [columns[b] for b in range(3)]), matrix, maps, 0)
    both = two_rows(maps, matrix_two[...], 0)
    rows = [both[:channels], both[channels:]] + [kept[n] for n in range(TALL - 2)]
    for wide, block in enumerate(swap_blocks(rows, WIDE)):
        queries[wide] = block.astype(jnp.bfloat16)
    match_tiles(queries, keys, sums, 0)
    first = pooled_fields(sums, across)

    halves = first.shape[1] // 128
    others = pooled.shape[0] // 5
    pieces = []
    for field in range(5):
        for half in range(halves):
            place = slice(half * 128, (half + 1) * 128)
            pieces.append(first[field : field + 1, place])
            pieces.append(pooled[field * others : (field + 1) * others, place])
    for half in range(halves):
        for band in range(others + 1):
            start = (band * halves + half) * 128
            pieces.append(tissue[:, start : start + 128].astype(jnp.float32))
    block = jnp.concatenate(pieces, axis=0)

    def put(peer, carry):
        blocks[peer] = block
        return carry

    lax.fori_loop(0, blocks.shape[0], put, 0)


def solve_kernel(bands, gathered, out, inverse, partial):
    count = gathered.shape[0]
    place = lax.axis_index("gz")
    size = gathered.shape[1] // 6

    def forward(section, carry):
        inv_a, inv_b, inv_c, one, two = carry
        inside = jnp.where(section < count - 1, 1.0, 0.0)
        above = jnp.where(section > 0, 1.0, 0.0)
        extra = SPRING * (inside + above) + ANCHOR
        data = gathered[jnp.minimum(section + 1, count - 1)]
        keep = gathered[section, 5 * size :] * inside
        fields = [data[k * size : (k + 1) * size] * keep for k in range(5)]
        square = SPRING * SPRING * above
        pulled = SPRING * above
        a = fields[0] + extra - square * inv_a
        b = fields[1] - square * inv_b
        c = fields[2] + extra - square * inv_c
        right_one = fields[3] + pulled * one
        right_two = fields[4] + pulled * two
        scale = 1.0 / (a * c - b * b)
        inv_a, inv_b, inv_c = c * scale, -b * scale, a * scale
        one, two = inv_a * right_one + inv_b * right_two, inv_b * right_one + inv_c * right_two
        for k, member in enumerate((inv_a, inv_b, inv_c)):
            inverse[section, k] = member
        partial[section, 0], partial[section, 1] = one, two
        return inv_a, inv_b, inv_c, one, two

    def backward(number, carry):
        one, two, own_one, own_two = carry
        section = count - 1 - number
        inv_a, inv_b, inv_c = (inverse[section, k] for k in range(3))
        fresh_one = partial[section, 0] + SPRING * (inv_a * one + inv_b * two)
        fresh_two = partial[section, 1] + SPRING * (inv_b * one + inv_c * two)
        mine = section == place
        own_one = jnp.where(mine, fresh_one, own_one)
        own_two = jnp.where(mine, fresh_two, own_two)
        return fresh_one, fresh_two, own_one, own_two

    zero = jnp.zeros((size, 128), jnp.float32)
    unroll = count <= 16
    lax.fori_loop(0, count, forward, (zero,) * 5, unroll=unroll)
    _, _, one, two = lax.fori_loop(0, count, backward, (zero,) * 4, unroll=unroll)
    halves = size // bands
    for number, solved in enumerate((one, two)):
        for band in range(bands):
            for half in range(halves):
                row = half * bands + band
                start = (band * halves + half) * 128
                out[number, :, start : start + 128] = solved[row : row + 1]


def body(image, conv_one, conv_two, tissue):
    height, extent = image.shape[1:]
    width = extent // 4
    rows = height // 4
    channels = conv_two.shape[0]
    across, bands = width // WIDE, rows // TALL
    tiles = across * bands
    peers, total = lax.axis_size("gz"), lax.axis_size("gy")
    vmem = pl.BlockSpec(memory_space=pltpu.VMEM)

    main = lax.ppermute(image, "gz", [(z, z + 1) for z in range(peers - 1)])
    top, bottom = image[:, :HALO], image[:, height - HALO :]
    odd = lax.axis_index("gy") % 2 == 1
    pairs = [(y, y + 1) for y in range(0, total - 1, 2)]
    near = lax.ppermute(
        jnp.where(odd, top, bottom), "gy", pairs + [(b, a) for a, b in pairs]
    )
    pairs = [(y, y + 1) for y in range(1, total - 1, 2)]
    far = lax.ppermute(jnp.where(odd, bottom, top), "gy", pairs + [(b, a) for a, b in pairs])
    corner = lax.ppermute(
        bottom,
        ("gz", "gy"),
        [
            (z * total + y, (z + 1) * total + y + 1)
            for z in range(peers - 1)
            for y in range(total - 1)
        ],
    )

    key_rows = rows + 2 * REACH
    map_rows = -(-(2 * key_rows + 1) // CHUNK) * CHUNK
    maps = pltpu.VMEM((map_rows, 3, conv_one.shape[0], width), jnp.bfloat16)
    inner = conv_one.shape[0]
    shapes = (
        (key_rows // GROUP, width + 2 * EDGE, GROUP * channels),
        (3, extent, 2 * width),
        (CHUNK * inner, 3 * DEPTH),
        (2 * channels, 15 * inner),
    )
    keys, *matrices = pl.pallas_call(
        functools.partial(keys_kernel, total),
        out_shape=[jax.ShapeDtypeStruct(shape, jnp.bfloat16) for shape in shapes],
        in_specs=[vmem] * 5,
        out_specs=[vmem] * 4,
        scratch_shapes=[maps],
        compiler_params=pltpu.CompilerParams(vmem_limit_bytes=16 << 20),
        name="keys",
        cost_estimate=pl.CostEstimate(flops=10**9, bytes_accessed=2 * 10**6, transcendentals=0),
    )(image, near, far, conv_one, conv_two)

    size = tiles * TALL * WIDE // (width // NODES) ** 2 // 128
    out_lanes = TALL * NODES * NODES // width
    limit = pltpu.CompilerParams(vmem_limit_bytes=16 << 20)

    def scratch(tiles, maps):
        return [
            maps,
            pltpu.VMEM((tiles, channels, TALL * WIDE), jnp.bfloat16),
            pltpu.VMEM((6, tiles, TALL * WIDE), jnp.float32),
        ]

    pooled, kept = pl.pallas_call(
        rest_kernel,
        out_shape=[
            jax.ShapeDtypeStruct((5 * (bands - 1), out_lanes), jnp.float32),
            jax.ShapeDtypeStruct((TALL - 2, channels, width), jnp.float32),
        ],
        in_specs=[vmem] * 5,
        out_specs=[vmem] * 2,
        scratch_shapes=scratch(tiles - across, maps),
        compiler_params=limit,
        name="rest",
        cost_estimate=pl.CostEstimate(flops=10**9, bytes_accessed=2 * 10**6, transcendentals=0),
    )(main, *matrices, keys)
    blocks = pl.pallas_call(
        first_kernel,
        out_shape=jax.ShapeDtypeStruct((peers, 6 * size, 128), jnp.float32),
        in_specs=[vmem] * 9,
        out_specs=vmem,
        scratch_shapes=scratch(across, pltpu.VMEM((5, 3, inner, width), jnp.bfloat16)),
        compiler_params=limit,
        name="first",
        cost_estimate=pl.CostEstimate(flops=10**9, bytes_accessed=2 * 10**6, transcendentals=0),
    )(main, corner, *matrices, keys, kept, pooled, tissue)

    gathered = lax.all_to_all(blocks, "gz", split_axis=0, concat_axis=0, tiled=True)
    return pl.pallas_call(
        functools.partial(solve_kernel, bands),
        out_shape=jax.ShapeDtypeStruct((2, 1, tissue.shape[1]), jnp.float32),
        in_specs=[vmem],
        out_specs=vmem,
        scratch_shapes=[
            pltpu.VMEM((peers, 3, size, 128), jnp.float32),
            pltpu.VMEM((peers, 2, size, 128), jnp.float32),
        ],
        compiler_params=pltpu.CompilerParams(vmem_limit_bytes=16 << 20),
        name="solve",
    )(gathered)


def solution(mesh):
    placed = (P("gz", "gy", None), P(), P(), P("gz", "gy"))
    return jax.shard_map(
        body, mesh=mesh, in_specs=placed, out_specs=P(None, "gz", "gy"), check_vma=False
    )
```

```python
import functools

import jax
import jax.numpy as jnp
from jax import lax
from jax.experimental import pallas as pl
from jax.experimental.pallas import tpu as pltpu
from jax.sharding import PartitionSpec as P


NODES = 64
REACH = 6
SPRING = 8.0
ANCHOR = 0.02
PRIOR = 1.0

HALO = 32
CHUNK = 32
DEPTH = 80
TALL = 8
WIDE = 16
EDGE = 8
GROUP = 4
FAR = -1e30

FIRST_ROW = HALO - (4 * REACH + 3)


def iota(shape, dim):
    return lax.broadcasted_iota(jnp.int32, shape, dim)


def pick_columns(extent):
    quarter = extent // 4
    parts = []
    for b in range(3):
        source = iota((extent, 2 * quarter), 0)
        place = iota((extent, 2 * quarter), 1)
        wanted = 4 * (place % quarter) + 2 * (place // quarter) + b - 1
        parts.append(jnp.where(source == wanted, 1.0, 0.0).astype(jnp.bfloat16))
    return parts


def first_matrix(conv_one):
    channels = conv_one.shape[0]
    spread = []
    for a in range(3):
        tap = iota((9, 3 * DEPTH), 0)
        b = iota((9, 3 * DEPTH), 1) // DEPTH
        chosen = jnp.where(tap == 3 * a + b, 1.0, 0.0).astype(jnp.bfloat16)
        spread.append(jnp.dot(conv_one, chosen, preferred_element_type=jnp.float32))
    row = iota((channels, 3 * DEPTH), 1) % DEPTH - FIRST_ROW
    blocks = []
    for out in range(CHUNK):
        block = jnp.zeros_like(spread[0])
        for a in range(3):
            block = jnp.where(row == 2 * out + a, spread[a], block)
        blocks.append(block.astype(jnp.bfloat16))
    return jnp.concatenate(blocks, axis=0)


def second_matrix(conv_two):
    taps = conv_two.shape[1]
    inner = taps // 9
    rows = []
    for out in range(2):
        source = iota((taps, 15 * inner), 0)
        place = iota((taps, 15 * inner), 1)
        a = place // (3 * inner) - 2 * out
        b = (place // inner) % 3
        wanted = 9 * (place % inner) + 3 * a + b
        inside = (a >= 0) & (a < 3) & (source == wanted)
        chosen = jnp.where(inside, 1.0, 0.0).astype(jnp.bfloat16)
        rows.append(jnp.dot(conv_two, chosen, preferred_element_type=jnp.float32))
    return jnp.concatenate(rows, axis=0).astype(jnp.bfloat16)


def split_columns(pixels, picks):
    return [
        jnp.dot(pixels, part, preferred_element_type=jnp.float32).astype(jnp.bfloat16)
        for part in picks
    ]


def first_maps(columns, matrix, maps, start):
    channels, quarter = maps.shape[2:]
    taken = jnp.concatenate([part[start : start + DEPTH] for part in columns], axis=0)
    values = jnp.maximum(jnp.dot(matrix, taken, preferred_element_type=jnp.float32), 0.0)
    even, odd = values[:, :quarter], values[:, quarter:]
    before = jnp.where(iota(odd.shape, 1) == 0, 0.0, pltpu.roll(odd, 1, 1))
    for b, part in enumerate((before, even, odd)):
        maps[:, b] = part.astype(jnp.bfloat16).reshape(-1, channels, quarter)


def all_maps(pixels, picks, matrix, maps):
    columns = split_columns(pixels, picks)
    for chunk in range(maps.shape[0] // CHUNK):
        first_maps(
            columns, matrix, maps.at[chunk * CHUNK : (chunk + 1) * CHUNK], 2 * CHUNK * chunk
        )


def two_rows(maps, matrix, pair):
    rows = maps[4 * pair : 4 * pair + 5]
    rows = rows.reshape(-1, rows.shape[-1])
    return jnp.maximum(jnp.dot(matrix, rows, preferred_element_type=jnp.float32), 0.0)


def keys_kernel(
    total, image, near, far, conv_one, conv_two, keys, columns, matrix_one, matrix_two, maps
):
    place = lax.axis_index("gy")
    odd = place % 2 == 1
    a, b = near[0], far[0]
    above = jnp.where(place == 0, jnp.zeros_like(a), jnp.where(odd, a, b))
    below = jnp.where(odd, b, a)
    spare = jnp.zeros((DEPTH - 2 * CHUNK, above.shape[1]), jnp.bfloat16)
    pixels = jnp.concatenate([above, image[0], below, spare], axis=0)
    picks = pick_columns(image.shape[2])
    for b, part in enumerate(picks):
        columns[b] = part
    first = first_matrix(conv_one[...])
    matrix_one[...] = first
    all_maps(pixels, picks, first, maps)
    matrix = second_matrix(conv_two[...])
    matrix_two[...] = matrix
    channels = conv_two.shape[0]
    local = image.shape[1] // 4
    last = place == total - 1
    edge = jnp.zeros((EDGE, GROUP * channels), jnp.float32)
    for group in range(keys.shape[0]):
        both = [two_rows(maps, matrix, 2 * group + half) for half in range(2)]
        both = jnp.concatenate(both, axis=0)
        if GROUP * (group + 1) > local + REACH:
            row = GROUP * group + iota(both.shape, 0) // channels
            both = jnp.where(last & (row >= local + REACH), 0.0, both)
        turned = jnp.concatenate([edge, both.T, edge], axis=0)
        keys[group] = turned.astype(jnp.bfloat16)


def swap_blocks(rows, width):
    count = len(rows)
    lanes = rows[0].shape[1]
    step = 1
    while step < count:
        low = (iota(rows[0].shape, 1) // width) % (2 * step) < step
        fresh = list(rows)
        for index in range(count):
            if index & step == 0:
                one, two = rows[index], rows[index + step]
                shift = width * step
                fresh[index] = jnp.where(low, one, pltpu.roll(two, shift, 1))
                fresh[index + step] = jnp.where(low, pltpu.roll(one, lanes - shift, 1), two)
        rows = fresh
        step *= 2
    return rows


def match_tiles(queries, keys, sums, band):
    channels = queries.shape[1]
    lanes = TALL * WIDE
    tiles = queries.shape[0]
    across = (keys.shape[1] - 2 * EDGE) // WIDE
    depth, breadth = TALL + 2 * REACH, 2 * WIDE
    span = 2 * REACH + 1
    own_row = iota((WIDE, lanes), 1) // WIDE
    own_col = iota((WIDE, lanes), 1) % WIDE
    shift_col = iota((WIDE, lanes), 0) - EDGE - own_col
    left = shift_col >= -REACH
    shift_col = jnp.where(left, shift_col, shift_col + WIDE)
    outside = jnp.where(jnp.abs(shift_col) > REACH, FAR, 0.0)
    shift_col = shift_col.astype(jnp.float32)
    shift_row = []
    for row in range(span):
        shift = row - REACH - own_row[:8]
        shift_row.append(jnp.where(shift < -REACH, shift + span, shift).astype(jnp.float32))
    factor = channels**-0.5 * 1.4426950408889634

    for tile in range(tiles):
        tall, wide = band + tile // across, tile % across
        window = keys[
            TALL // GROUP * tall : TALL // GROUP * tall + depth // GROUP,
            WIDE * wide : WIDE * wide + breadth,
            :,
        ]
        own = queries[tile]
        empty = jnp.zeros_like(own)
        spread = jnp.concatenate(
            [
                jnp.concatenate([own if i == j else empty for j in range(GROUP)], axis=1)
                for i in range(GROUP)
            ],
            axis=0,
        )
        scores = jnp.dot(
            window.reshape(-1, GROUP * channels), spread, preferred_element_type=jnp.float32
        )
        parts = []
        for row in range(depth):
            i, j = row // GROUP, row % GROUP
            part = scores[i * breadth : (i + 1) * breadth, j * lanes : (j + 1) * lanes]
            parts.append(jnp.where(left, part[:WIDE], part[WIDE:]))
        for row in range(depth - span):
            parts[row] = jnp.where(own_row <= row, parts[row], parts[row + span])
        parts = [part + outside for part in parts[:span]]
        highest = functools.reduce(jnp.maximum, parts)
        highest = jnp.max(highest, axis=0, keepdims=True)
        mass = jnp.zeros((WIDE, lanes), jnp.float32)
        once = mass
        twice = jnp.zeros((8, lanes), jnp.float32)
        for row in range(span):
            prob = jnp.exp2((parts[row] - highest) * factor)
            mass = mass + prob
            weighted = (prob.reshape(-1, 8, lanes) * shift_row[row]).reshape(WIDE, lanes)
            once = once + weighted
            twice = twice + jnp.sum(weighted.reshape(-1, 8, lanes), axis=0) * shift_row[row]
        moments = (
            mass,
            once,
            twice,
            mass * shift_col,
            mass * shift_col * shift_col,
            once * shift_col,
        )
        for number, moment in enumerate(moments):
            sums[number, tile : tile + 1, :] = jnp.sum(moment, axis=0, keepdims=True)


def pooled_fields(sums, across):
    total = sums[0]
    mean_row = sums[1] / total
    row_square = sums[2] / total
    col_mean = sums[3] / total
    col_square = sums[4] / total
    product = sums[5] / total
    var_row = row_square - mean_row * mean_row + PRIOR
    var_col = col_square - col_mean * col_mean + PRIOR
    covar = product - mean_row * col_mean
    determ = var_row * var_col - covar * covar
    info_rr = var_col / determ
    info_rc = -covar / determ
    info_cc = var_row / determ
    pull_row = info_rr * mean_row + info_rc * col_mean
    pull_col = info_rc * mean_row + info_cc * col_mean
    fields = jnp.concatenate([info_rr, info_rc, info_cc, pull_row, pull_col], axis=0)

    lanes = TALL * WIDE
    patch = across * WIDE // NODES
    high, broad = TALL // patch, WIDE // patch
    out_lanes = high * NODES
    source = iota((lanes, out_lanes), 0)
    place = iota((lanes, out_lanes), 1)
    same = (source // WIDE // patch == place // NODES) & (
        source % WIDE // patch == place % NODES % broad
    )
    pool = jnp.where(same, 1.0 / (patch * patch), 0.0)
    pooled = jnp.dot(
        fields, pool, preferred_element_type=jnp.float32, precision=lax.Precision.HIGHEST
    )
    mine = iota(pooled.shape, 0) % across == iota(pooled.shape, 1) % NODES // broad
    pooled = jnp.where(mine, pooled, 0.0)
    return jnp.sum(pooled.reshape(-1, across, out_lanes), axis=1)


def rest_kernel(image, columns, matrix_one, matrix_two, keys, pooled, kept, maps, queries, sums):
    extent = image.shape[2]
    above = jnp.zeros((HALO, extent), jnp.bfloat16)
    below = jnp.zeros((HALO + DEPTH - 2 * CHUNK, extent), jnp.bfloat16)
    pixels = jnp.concatenate([above, image[0], below], axis=0)
    all_maps(pixels, [columns[b] for b in range(3)], matrix_one[...], maps)
    matrix = matrix_two[...]
    channels = queries.shape[1]
    across = (keys.shape[1] - 2 * EDGE) // WIDE
    for band in range(queries.shape[0] // across + 1):
        rows = []
        for pair in range(TALL // 2):
            if band + pair == 0:
                continue
            both = two_rows(maps, matrix, (REACH + TALL * band) // 2 + pair)
            rows += [both[:channels], both[channels:]]
        if band == 0:
            for number, row in enumerate(rows):
                kept[number] = row
            continue
        for wide, block in enumerate(swap_blocks(rows, WIDE)):
            queries[across * (band - 1) + wide] = block.astype(jnp.bfloat16)
    match_tiles(queries, keys, sums, 1)
    pooled[...] = pooled_fields(sums, across)


def first_kernel(
    image, corner, columns, matrix_one, matrix_two, keys, kept, pooled, tissue,
    blocks, maps, queries, sums,
):
    channels = queries.shape[1]
    across = queries.shape[0]
    above = jnp.where(lax.axis_index("gy") == 0, jnp.zeros_like(corner[0]), corner[0])
    pixels = jnp.concatenate([above, image[0, : DEPTH - HALO]], axis=0)
    begin = 2 * REACH * matrix_one.shape[0] // CHUNK
    matrix = matrix_one[begin : begin + maps.shape[0] * maps.shape[2]]
    first_maps(split_columns(pixels, [columns[b] for b in range(3)]), matrix, maps, 0)
    both = two_rows(maps, matrix_two[...], 0)
    rows = [both[:channels], both[channels:]] + [kept[n] for n in range(TALL - 2)]
    for wide, block in enumerate(swap_blocks(rows, WIDE)):
        queries[wide] = block.astype(jnp.bfloat16)
    match_tiles(queries, keys, sums, 0)
    first = pooled_fields(sums, across)

    halves = first.shape[1] // 128
    others = pooled.shape[0] // 5
    pieces = []
    for field in range(5):
        for half in range(halves):
            place = slice(half * 128, (half + 1) * 128)
            pieces.append(first[field : field + 1, place])
            pieces.append(pooled[field * others : (field + 1) * others, place])
    for half in range(halves):
        for band in range(others + 1):
            start = (band * halves + half) * 128
            pieces.append(tissue[:, start : start + 128].astype(jnp.float32))
    block = jnp.concatenate(pieces, axis=0)

    def put(peer, carry):
        blocks[peer] = block
        return carry

    lax.fori_loop(0, blocks.shape[0], put, 0)


def solve_kernel(bands, gathered, out, inverse, partial):
    count = gathered.shape[0]
    place = lax.axis_index("gz")
    size = gathered.shape[1] // 6

    def forward(section, carry):
        inv_a, inv_b, inv_c, one, two = carry
        inside = jnp.where(section < count - 1, 1.0, 0.0)
        above = jnp.where(section > 0, 1.0, 0.0)
        extra = SPRING * (inside + above) + ANCHOR
        data = gathered[jnp.minimum(section + 1, count - 1)]
        keep = gathered[section, 5 * size :] * inside
        fields = [data[k * size : (k + 1) * size] * keep for k in range(5)]
        square = SPRING * SPRING * above
        pulled = SPRING * above
        a = fields[0] + extra - square * inv_a
        b = fields[1] - square * inv_b
        c = fields[2] + extra - square * inv_c
        right_one = fields[3] + pulled * one
        right_two = fields[4] + pulled * two
        scale = 1.0 / (a * c - b * b)
        inv_a, inv_b, inv_c = c * scale, -b * scale, a * scale
        one, two = inv_a * right_one + inv_b * right_two, inv_b * right_one + inv_c * right_two
        for k, member in enumerate((inv_a, inv_b, inv_c)):
            inverse[section, k] = member
        partial[section, 0], partial[section, 1] = one, two
        return inv_a, inv_b, inv_c, one, two

    def backward(number, carry):
        one, two, own_one, own_two = carry
        section = count - 1 - number
        inv_a, inv_b, inv_c = (inverse[section, k] for k in range(3))
        fresh_one = partial[section, 0] + SPRING * (inv_a * one + inv_b * two)
        fresh_two = partial[section, 1] + SPRING * (inv_b * one + inv_c * two)
        mine = section == place
        own_one = jnp.where(mine, fresh_one, own_one)
        own_two = jnp.where(mine, fresh_two, own_two)
        return fresh_one, fresh_two, own_one, own_two

    zero = jnp.zeros((size, 128), jnp.float32)
    unroll = count <= 16
    lax.fori_loop(0, count, forward, (zero,) * 5, unroll=unroll)
    _, _, one, two = lax.fori_loop(0, count, backward, (zero,) * 4, unroll=unroll)
    halves = size // bands
    for number, solved in enumerate((one, two)):
        for band in range(bands):
            for half in range(halves):
                row = half * bands + band
                start = (band * halves + half) * 128
                out[number, :, start : start + 128] = solved[row : row + 1]


def body(image, conv_one, conv_two, tissue):
    height, extent = image.shape[1:]
    width = extent // 4
    rows = height // 4
    channels = conv_two.shape[0]
    across, bands = width // WIDE, rows // TALL
    tiles = across * bands
    peers, total = lax.axis_size("gz"), lax.axis_size("gy")
    vmem = pl.BlockSpec(memory_space=pltpu.VMEM)

    main = lax.ppermute(image, "gz", [(z, (z + 1) % peers) for z in range(peers)])
    top, bottom = image[:, :HALO], image[:, height - HALO :]
    odd = lax.axis_index("gy") % 2 == 1

    def swapped(block, first):
        pairs = [(y, (y + 1) % total) for y in range(first, total, 2)]
        return lax.ppermute(block, "gy", pairs + [(b, a) for a, b in pairs])

    near = swapped(jnp.where(odd, top, bottom), 0)
    far = swapped(jnp.where(odd, bottom, top), 1)
    corner = lax.ppermute(
        bottom,
        ("gz", "gy"),
        [
            (z * total + y, (z + 1) % peers * total + (y + 1) % total)
            for z in range(peers)
            for y in range(total)
        ],
    )

    key_rows = rows + 2 * REACH
    map_rows = -(-(2 * key_rows + 1) // CHUNK) * CHUNK
    maps = pltpu.VMEM((map_rows, 3, conv_one.shape[0], width), jnp.bfloat16)
    inner = conv_one.shape[0]
    shapes = (
        (key_rows // GROUP, width + 2 * EDGE, GROUP * channels),
        (3, extent, 2 * width),
        (CHUNK * inner, 3 * DEPTH),
        (2 * channels, 15 * inner),
    )
    keys, *matrices = pl.pallas_call(
        functools.partial(keys_kernel, total),
        out_shape=[jax.ShapeDtypeStruct(shape, jnp.bfloat16) for shape in shapes],
        in_specs=[vmem] * 5,
        out_specs=[vmem] * 4,
        scratch_shapes=[maps],
        compiler_params=pltpu.CompilerParams(vmem_limit_bytes=16 << 20),
        name="keys",
        cost_estimate=pl.CostEstimate(flops=10**9, bytes_accessed=2 * 10**6, transcendentals=0),
    )(image, near, far, conv_one, conv_two)

    size = tiles * TALL * WIDE // (width // NODES) ** 2 // 128
    out_lanes = TALL * NODES * NODES // width
    limit = pltpu.CompilerParams(vmem_limit_bytes=16 << 20)

    def scratch(tiles, maps):
        return [
            maps,
            pltpu.VMEM((tiles, channels, TALL * WIDE), jnp.bfloat16),
            pltpu.VMEM((6, tiles, TALL * WIDE), jnp.float32),
        ]

    pooled, kept = pl.pallas_call(
        rest_kernel,
        out_shape=[
            jax.ShapeDtypeStruct((5 * (bands - 1), out_lanes), jnp.float32),
            jax.ShapeDtypeStruct((TALL - 2, channels, width), jnp.float32),
        ],
        in_specs=[vmem] * 5,
        out_specs=[vmem] * 2,
        scratch_shapes=scratch(tiles - across, maps),
        compiler_params=limit,
        name="rest",
        cost_estimate=pl.CostEstimate(flops=10**9, bytes_accessed=2 * 10**6, transcendentals=0),
    )(main, *matrices, keys)
    blocks = pl.pallas_call(
        first_kernel,
        out_shape=jax.ShapeDtypeStruct((peers, 6 * size, 128), jnp.float32),
        in_specs=[vmem] * 9,
        out_specs=vmem,
        scratch_shapes=scratch(across, pltpu.VMEM((5, 3, inner, width), jnp.bfloat16)),
        compiler_params=limit,
        name="first",
        cost_estimate=pl.CostEstimate(flops=10**9, bytes_accessed=2 * 10**6, transcendentals=0),
    )(main, corner, *matrices, keys, kept, pooled, tissue)

    gathered = lax.all_to_all(blocks, "gz", split_axis=0, concat_axis=0, tiled=True)
    return pl.pallas_call(
        functools.partial(solve_kernel, bands),
        out_shape=jax.ShapeDtypeStruct((2, 1, tissue.shape[1]), jnp.float32),
        in_specs=[vmem],
        out_specs=vmem,
        scratch_shapes=[
            pltpu.VMEM((peers, 3, size, 128), jnp.float32),
            pltpu.VMEM((peers, 2, size, 128), jnp.float32),
        ],
        compiler_params=pltpu.CompilerParams(vmem_limit_bytes=16 << 20),
        name="solve",
    )(gathered)


def solution(mesh):
    placed = (P("gz", "gy", None), P(), P(), P("gz", "gy"))
    return jax.shard_map(
        body, mesh=mesh, in_specs=placed, out_specs=P(None, "gz", "gy"), check_vma=False
    )
```

```python
import functools

import jax
import jax.numpy as jnp
from jax import lax
from jax.experimental import pallas as pl
from jax.experimental.pallas import tpu as pltpu
from jax.sharding import PartitionSpec as P


NODES = 64
REACH = 6
SPRING = 8.0
ANCHOR = 0.02
PRIOR = 1.0

HALO = 32
CHUNK = 32
DEPTH = 80
TALL = 8
WIDE = 16
EDGE = 8
GROUP = 4
FAR = -1e30
LATE = 2

FIRST_ROW = HALO - (4 * REACH + 3)


def iota(shape, dim):
    return lax.broadcasted_iota(jnp.int32, shape, dim)


def pick_columns(extent):
    quarter = extent // 4
    source = iota((extent, extent), 0)
    place = iota((extent, extent), 1)
    wanted = 4 * (place % quarter) + place // quarter
    return jnp.where(source == wanted, 1.0, 0.0).astype(jnp.bfloat16)


def first_matrix(conv_one):
    channels = conv_one.shape[0]
    spread = []
    for a in range(3):
        tap = iota((9, 3 * DEPTH), 0)
        b = iota((9, 3 * DEPTH), 1) // DEPTH
        chosen = jnp.where(tap == 3 * a + b, 1.0, 0.0).astype(jnp.bfloat16)
        spread.append(jnp.dot(conv_one, chosen, preferred_element_type=jnp.float32))
    row = iota((channels, 3 * DEPTH), 1) % DEPTH - FIRST_ROW
    blocks = []
    for out in range(CHUNK):
        block = jnp.zeros_like(spread[0])
        for a in range(3):
            block = jnp.where(row == 2 * out + a, spread[a], block)
        blocks.append(block.astype(jnp.bfloat16))
    return jnp.concatenate(blocks, axis=0)


def second_matrix(conv_two):
    taps = conv_two.shape[1]
    inner = taps // 9
    rows = []
    for out in range(2):
        source = iota((taps, 15 * inner), 0)
        place = iota((taps, 15 * inner), 1)
        a = place // (3 * inner) - 2 * out
        b = (place // inner) % 3
        wanted = 9 * (place % inner) + 3 * a + b
        inside = (a >= 0) & (a < 3) & (source == wanted)
        chosen = jnp.where(inside, 1.0, 0.0).astype(jnp.bfloat16)
        rows.append(jnp.dot(conv_two, chosen, preferred_element_type=jnp.float32))
    return jnp.concatenate(rows, axis=0).astype(jnp.bfloat16)


def split_columns(pixels, picks):
    quarter = pixels.shape[1] // 4
    split = jnp.dot(pixels, picks, preferred_element_type=jnp.float32)
    parts = [split[:, q * quarter : (q + 1) * quarter] for q in range(4)]
    before = jnp.where(iota(parts[3].shape, 1) == 0, 0.0, pltpu.roll(parts[3], 1, 1))
    return [part.astype(jnp.bfloat16) for part in [before] + parts]


def first_maps(columns, matrix, maps, start):
    channels, quarter = maps.shape[2:]
    span = slice(start, start + DEPTH)
    taken = jnp.concatenate(
        [jnp.concatenate([columns[b][span], columns[b + 2][span]], axis=1) for b in range(3)],
        axis=0,
    )
    values = jnp.maximum(jnp.dot(matrix, taken, preferred_element_type=jnp.float32), 0.0)
    even, odd = values[:, :quarter], values[:, quarter:]
    before = jnp.where(iota(odd.shape, 1) == 0, 0.0, pltpu.roll(odd, 1, 1))
    for b, part in enumerate((before, even, odd)):
        maps[:, b] = part.astype(jnp.bfloat16).reshape(-1, channels, quarter)


def maps_between(columns, matrix, maps, low, high):
    channels = maps.shape[2]
    for chunk in range(low // CHUNK, -(-high // CHUNK)):
        one, two = max(low - chunk * CHUNK, 0), min(high - chunk * CHUNK, CHUNK)
        first_maps(
            columns,
            matrix[one * channels : two * channels],
            maps.at[chunk * CHUNK + one : chunk * CHUNK + two],
            2 * CHUNK * chunk,
        )


def feature_rows(maps, matrix, pair, count):
    parts = []
    for number in range(pair, pair + count):
        part = maps[4 * number : 4 * number + 5]
        parts.append(part.reshape(-1, part.shape[-1]))
    taken = jnp.concatenate(parts, axis=1) if count > 1 else parts[0]
    values = jnp.maximum(jnp.dot(matrix, taken, preferred_element_type=jnp.float32), 0.0)
    lanes = values.shape[1] // count
    return [values[:, n * lanes : (n + 1) * lanes] for n in range(count)]


def prepare_kernel(
    image, conv_one, conv_two, tissue, picks, matrix_one, matrix_two, split, middle, marks
):
    marks[...] = tissue[...].astype(jnp.float32)
    picks[...] = pick_columns(image.shape[2])
    matrix_one[...] = first_matrix(conv_one[...])
    matrix_two[...] = second_matrix(conv_two[...])
    columns = split_columns(image[0], picks[...])
    for number, part in enumerate(columns):
        split[number] = part
    first_maps(columns, matrix_one[...], middle, 2 * CHUNK - HALO)


def keys_kernel(total, near, far, picks, matrix_one, matrix_two, split, middle, keys, maps):
    place = lax.axis_index("gy")
    odd = place % 2 == 1
    a, b = near[0], far[0]
    above = jnp.where(place == 0, jnp.zeros_like(a), jnp.where(odd, a, b))
    below = jnp.where(odd, b, a)
    outer = split_columns(jnp.concatenate([above, below], axis=0), picks[...])
    local = split.shape[1] // 4
    spare = jnp.zeros((DEPTH - 2 * CHUNK, split.shape[2]), jnp.bfloat16)
    columns = [
        jnp.concatenate([part[:HALO], split[n], part[HALO:], spare], axis=0)
        for n, part in enumerate(outer)
    ]
    channels = matrix_two.shape[0] // 2
    matrix = matrix_one[...]
    maps_between(columns, matrix, maps, 0, CHUNK)
    maps[CHUNK : 2 * CHUNK] = middle[...]
    maps_between(columns, matrix, maps, 2 * CHUNK, 2 * GROUP * keys.shape[0] + 1)
    last = place == total - 1
    edge = jnp.zeros((EDGE, GROUP * channels), jnp.float32)
    matrix = matrix_two[...]
    for group in range(keys.shape[0]):
        both = jnp.concatenate(feature_rows(maps, matrix, 2 * group, 2), axis=0)
        if GROUP * (group + 1) > local + REACH:
            row = GROUP * group + iota(both.shape, 0) // channels
            both = jnp.where(last & (row >= local + REACH), 0.0, both)
        turned = jnp.concatenate([edge, both.T, edge], axis=0)
        keys[group] = turned.astype(jnp.bfloat16)


def swap_blocks(rows, width):
    count = len(rows)
    lanes = rows[0].shape[1]
    step = 1
    while step < count:
        low = (iota(rows[0].shape, 1) // width) % (2 * step) < step
        fresh = list(rows)
        for index in range(count):
            if index & step == 0:
                one, two = rows[index], rows[index + step]
                shift = width * step
                fresh[index] = jnp.where(low, one, pltpu.roll(two, shift, 1))
                fresh[index + step] = jnp.where(low, pltpu.roll(one, lanes - shift, 1), two)
        rows = fresh
        step *= 2
    return rows


def match_tiles(queries, keys, sums, band):
    channels = queries.shape[1]
    lanes = TALL * WIDE
    tiles = queries.shape[0]
    across = (keys.shape[1] - 2 * EDGE) // WIDE
    depth, breadth = TALL + 2 * REACH, 2 * WIDE
    span = 2 * REACH + 1
    own_row = iota((WIDE, lanes), 1) // WIDE
    own_col = iota((WIDE, lanes), 1) % WIDE
    shift_col = iota((WIDE, lanes), 0) - EDGE - own_col
    left = shift_col >= -REACH
    shift_col = jnp.where(left, shift_col, shift_col + WIDE)
    outside = jnp.where(jnp.abs(shift_col) > REACH, FAR, 0.0)
    shift_col = shift_col.astype(jnp.float32)
    shift_row = []
    for row in range(span):
        shift = row - REACH - own_row[:8]
        shift_row.append(jnp.where(shift < -REACH, shift + span, shift).astype(jnp.float32))
    factor = channels**-0.5 * 1.4426950408889634

    for tile in reversed(range(tiles)):
        tall, wide = band + tile // across, tile % across
        window = keys[
            TALL // GROUP * tall : TALL // GROUP * tall + depth // GROUP,
            WIDE * wide : WIDE * wide + breadth,
            :,
        ]
        own = queries[tile]
        empty = jnp.zeros_like(own)
        spread = jnp.concatenate(
            [
                jnp.concatenate([own if i == j else empty for j in range(GROUP)], axis=1)
                for i in range(GROUP)
            ],
            axis=0,
        )
        scores = jnp.dot(
            window.reshape(-1, GROUP * channels), spread, preferred_element_type=jnp.float32
        )
        parts = []
        for row in range(depth):
            i, j = row // GROUP, row % GROUP
            part = scores[i * breadth : (i + 1) * breadth, j * lanes : (j + 1) * lanes]
            parts.append(jnp.where(left, part[:WIDE], part[WIDE:]))
        for row in range(depth - span):
            parts[row] = jnp.where(own_row <= row, parts[row], parts[row + span])
        parts = [part + outside for part in parts[:span]]
        highest = functools.reduce(jnp.maximum, parts)
        highest = jnp.max(highest, axis=0, keepdims=True)
        mass = jnp.zeros((WIDE, lanes), jnp.float32)
        once = mass
        twice = jnp.zeros((8, lanes), jnp.float32)
        for row in range(span):
            prob = jnp.exp2((parts[row] - highest) * factor)
            mass = mass + prob
            weighted = (prob.reshape(-1, 8, lanes) * shift_row[row]).reshape(WIDE, lanes)
            once = once + weighted
            twice = twice + jnp.sum(weighted.reshape(-1, 8, lanes), axis=0) * shift_row[row]
        moments = (
            mass,
            once,
            twice,
            mass * shift_col,
            mass * shift_col * shift_col,
            once * shift_col,
        )
        for number, moment in enumerate(moments):
            sums[number, tile : tile + 1, :] = jnp.sum(moment, axis=0, keepdims=True)


def pooled_fields(sums, across):
    total = sums[0]
    mean_row = sums[1] / total
    row_square = sums[2] / total
    col_mean = sums[3] / total
    col_square = sums[4] / total
    product = sums[5] / total
    var_row = row_square - mean_row * mean_row + PRIOR
    var_col = col_square - col_mean * col_mean + PRIOR
    covar = product - mean_row * col_mean
    determ = var_row * var_col - covar * covar
    info_rr = var_col / determ
    info_rc = -covar / determ
    info_cc = var_row / determ
    pull_row = info_rr * mean_row + info_rc * col_mean
    pull_col = info_rc * mean_row + info_cc * col_mean
    fields = jnp.concatenate([info_rr, info_rc, info_cc, pull_row, pull_col], axis=0)

    lanes = TALL * WIDE
    patch = across * WIDE // NODES
    high, broad = TALL // patch, WIDE // patch
    out_lanes = high * NODES
    source = iota((lanes, out_lanes), 0)
    place = iota((lanes, out_lanes), 1)
    same = (source // WIDE // patch == place // NODES) & (
        source % WIDE // patch == place % NODES % broad
    )
    pool = jnp.where(same, 1.0 / (patch * patch), 0.0)
    pooled = jnp.dot(
        fields, pool, preferred_element_type=jnp.float32, precision=lax.Precision.HIGHEST
    )
    mine = iota(pooled.shape, 0) % across == iota(pooled.shape, 1) % NODES // broad
    pooled = jnp.where(mine, pooled, 0.0)
    return jnp.sum(pooled.reshape(-1, across, out_lanes), axis=1)


def rest_kernel(
    image, picks, matrix_one, matrix_two, keys, pooled, kept, ready, maps, queries, sums
):
    columns = []
    for part in split_columns(image[0], picks[...]):
        above = jnp.zeros((HALO, part.shape[1]), jnp.bfloat16)
        below = jnp.zeros((HALO + DEPTH - 2 * CHUNK, part.shape[1]), jnp.bfloat16)
        columns.append(jnp.concatenate([above, part, below], axis=0))
    channels = queries.shape[1]
    across = (keys.shape[1] - 2 * EDGE) // WIDE
    bands = queries.shape[0] // across + LATE
    first = 2 * REACH
    maps_between(columns, matrix_one, maps, first + 2, first + 2 * TALL * bands + 1)
    matrix = matrix_two[...]
    for band in range(bands):
        rows = []
        skip = 1 if band == 0 else 0
        pair = (REACH + TALL * band) // 2
        values = []
        for number in range(skip, TALL // 2, 2):
            values += feature_rows(maps, matrix, pair + number, min(2, TALL // 2 - number))
        for both in values:
            rows += [both[:channels], both[channels:]]
        if band == 0:
            for number, row in enumerate(rows):
                kept[number] = row
            continue
        place, start = (ready, 1) if band < LATE else (queries, LATE)
        for wide, block in enumerate(swap_blocks(rows, WIDE)):
            place[across * (band - start) + wide] = block.astype(jnp.bfloat16)
    match_tiles(queries, keys, sums, LATE)
    pooled[...] = pooled_fields(sums, across)


def first_kernel(
    image, corner, picks, matrix_one, matrix_two, keys, kept, ready, pooled, marks,
    blocks, maps, queries, sums,
):
    channels = queries.shape[1]
    across = queries.shape[0] // LATE
    above = jnp.where(lax.axis_index("gy") == 0, jnp.zeros_like(corner[0]), corner[0])
    pixels = jnp.concatenate([above, image[0, : DEPTH - HALO]], axis=0)
    begin = 2 * REACH * maps.shape[2]
    matrix = matrix_one[begin : begin + maps.shape[0] * maps.shape[2]]
    first_maps(split_columns(pixels, picks[...]), matrix, maps, 0)
    both = feature_rows(maps, matrix_two[...], 0, 1)[0]
    rows = [both[:channels], both[channels:]] + [kept[n] for n in range(TALL - 2)]
    for wide, block in enumerate(swap_blocks(rows, WIDE)):
        queries[wide] = block.astype(jnp.bfloat16)
    for tile in range(across, LATE * across):
        queries[tile] = ready[tile - across]
    match_tiles(queries, keys, sums, 0)
    first = pooled_fields(sums, across)

    halves = first.shape[1] // 128
    others = pooled.shape[0] // 5
    pieces, signs = [], []
    for field in range(5):
        for half in range(halves):
            place = slice(half * 128, (half + 1) * 128)
            pieces.append(first[field * LATE : (field + 1) * LATE, place])
            pieces.append(pooled[field * others : (field + 1) * others, place])
    for half in range(halves):
        for band in range(others + LATE):
            start = (band * halves + half) * 128
            signs.append(marks[:, start : start + 128])
    block = jnp.concatenate(pieces, axis=0)
    size = block.shape[0] // 5
    signed = block[:size] * (2.0 * jnp.concatenate(signs, axis=0) - 1.0)
    block = jnp.concatenate([signed, block[size:]], axis=0)

    def put(peer, carry):
        blocks[peer] = block
        return carry

    lax.fori_loop(0, blocks.shape[0], put, 0, unroll=blocks.shape[0] <= 16)


def solve_kernel(bands, gathered, out, inverse, partial):
    count = gathered.shape[0]
    place = lax.axis_index("gz")
    size = gathered.shape[1] // 5

    def forward(section, carry):
        inv_a, inv_b, inv_c, one, two = carry
        inside = jnp.where(section < count - 1, 1.0, 0.0)
        above = jnp.where(section > 0, 1.0, 0.0)
        extra = SPRING * (inside + above) + ANCHOR
        data = gathered[jnp.minimum(section + 1, count - 1)]
        keep = jnp.where(gathered[section, :size] > 0.0, inside, 0.0)
        fields = [data[k * size : (k + 1) * size] for k in range(5)]
        fields = [member * keep for member in [jnp.abs(fields[0])] + fields[1:]]
        square = SPRING * SPRING * above
        pulled = SPRING * above
        a = fields[0] + extra - square * inv_a
        b = fields[1] - square * inv_b
        c = fields[2] + extra - square * inv_c
        right_one = fields[3] + pulled * one
        right_two = fields[4] + pulled * two
        scale = 1.0 / (a * c - b * b)
        inv_a, inv_b, inv_c = c * scale, -b * scale, a * scale
        one, two = inv_a * right_one + inv_b * right_two, inv_b * right_one + inv_c * right_two
        for k, member in enumerate((inv_a, inv_b, inv_c)):
            inverse[section, k] = member
        partial[section, 0], partial[section, 1] = one, two
        return inv_a, inv_b, inv_c, one, two

    def backward(number, carry):
        one, two, own_one, own_two = carry
        section = count - 1 - number
        inv_a, inv_b, inv_c = (inverse[section, k] for k in range(3))
        fresh_one = partial[section, 0] + SPRING * (inv_a * one + inv_b * two)
        fresh_two = partial[section, 1] + SPRING * (inv_b * one + inv_c * two)
        mine = section == place
        own_one = jnp.where(mine, fresh_one, own_one)
        own_two = jnp.where(mine, fresh_two, own_two)
        return fresh_one, fresh_two, own_one, own_two

    zero = jnp.zeros((size, 128), jnp.float32)
    unroll = count <= 16
    lax.fori_loop(0, count, forward, (zero,) * 5, unroll=unroll)
    _, _, one, two = lax.fori_loop(0, count, backward, (zero,) * 4, unroll=unroll)
    halves = size // bands
    for number, solved in enumerate((one, two)):
        for band in range(bands):
            for half in range(halves):
                row = half * bands + band
                start = (band * halves + half) * 128
                out[number, :, start : start + 128] = solved[row : row + 1]


def body(image, conv_one, conv_two, tissue):
    height, extent = image.shape[1:]
    width = extent // 4
    rows = height // 4
    channels = conv_two.shape[0]
    across, bands = width // WIDE, rows // TALL
    tiles = across * bands
    peers, total = lax.axis_size("gz"), lax.axis_size("gy")
    vmem = pl.BlockSpec(memory_space=pltpu.VMEM)

    limit = pltpu.CompilerParams(vmem_limit_bytes=16 << 20)

    def call(kernel, name, ins, outs, scratch=()):
        return pl.pallas_call(
            kernel,
            out_shape=[jax.ShapeDtypeStruct(*out) for out in outs],
            in_specs=[vmem] * len(ins),
            out_specs=[vmem] * len(outs),
            scratch_shapes=list(scratch),
            compiler_params=limit,
            name=name,
            cost_estimate=pl.CostEstimate(
                flops=10**9, bytes_accessed=2 * 10**6, transcendentals=0
            ),
        )(*ins)

    main = lax.ppermute(image, "gz", [(z, (z + 1) % peers) for z in range(peers)])
    top, bottom = image[:, :HALO], image[:, height - HALO :]
    odd = lax.axis_index("gy") % 2 == 1
    near, far = jnp.where(odd, top, bottom), jnp.where(odd, bottom, top)

    def swapped(block, first):
        pairs = [(y, (y + 1) % total) for y in range(first, total, 2)]
        return lax.ppermute(block, "gy", pairs + [(b, a) for a, b in pairs])

    near, far = swapped(near, 0), swapped(far, 1)
    corner = lax.ppermute(
        bottom,
        ("gz", "gy"),
        [
            (z * total + y, (z + 1) % peers * total + (y + 1) % total)
            for z in range(peers)
            for y in range(total)
        ],
    )

    inner = conv_one.shape[0]
    key_rows = rows + 2 * REACH
    map_rows = -(-(2 * key_rows + 1) // CHUNK) * CHUNK
    maps = pltpu.VMEM((map_rows, 3, inner, width), jnp.bfloat16)
    shapes = (
        (extent, extent),
        (CHUNK * inner, 3 * DEPTH),
        (2 * channels, 15 * inner),
        (5, height, width),
        (CHUNK, 3, inner, width),
    )
    *matrices, split, middle, marks = call(
        prepare_kernel,
        "prepare",
        (image, conv_one, conv_two, tissue),
        [(shape, jnp.bfloat16) for shape in shapes] + [(tissue.shape, jnp.float32)],
    )
    (keys,) = call(
        functools.partial(keys_kernel, total),
        "keys",
        (near, far, *matrices, split, middle),
        [((key_rows // GROUP, width + 2 * EDGE, GROUP * channels), jnp.bfloat16)],
        [maps],
    )

    size = tiles * TALL * WIDE // (width // NODES) ** 2 // 128
    out_lanes = TALL * NODES * NODES // width

    def scratch(tiles, maps):
        return [
            maps,
            pltpu.VMEM((tiles, channels, TALL * WIDE), jnp.bfloat16),
            pltpu.VMEM((6, tiles, TALL * WIDE), jnp.float32),
        ]

    pooled, kept, ready = call(
        rest_kernel,
        "rest",
        (main, *matrices, keys),
        [
            ((5 * (bands - LATE), out_lanes), jnp.float32),
            ((TALL - 2, channels, width), jnp.float32),
            (((LATE - 1) * across, channels, TALL * WIDE), jnp.bfloat16),
        ],
        scratch(tiles - LATE * across, maps),
    )
    (blocks,) = call(
        first_kernel,
        "first",
        (main, corner, *matrices, keys, kept, ready, pooled, marks),
        [((peers, 5 * size, 128), jnp.float32)],
        scratch(LATE * across, pltpu.VMEM((5, 3, inner, width), jnp.bfloat16)),
    )
    gathered = lax.all_to_all(blocks, "gz", split_axis=0, concat_axis=0, tiled=True)
    (out,) = call(
        functools.partial(solve_kernel, bands),
        "solve",
        (gathered,),
        [((2, 1, tissue.shape[1]), jnp.float32)],
        [
            pltpu.VMEM((peers, 3, size, 128), jnp.float32),
            pltpu.VMEM((peers, 2, size, 128), jnp.float32),
        ],
    )
    return out


def solution(mesh):
    placed = (P("gz", "gy", None), P(), P(), P("gz", "gy"))
    return jax.shard_map(
        body, mesh=mesh, in_specs=placed, out_specs=P(None, "gz", "gy"), check_vma=False
    )
```

```python
import functools

import jax
import jax.numpy as jnp
from jax import lax
from jax.experimental import pallas as pl
from jax.experimental.pallas import tpu as pltpu
from jax.sharding import PartitionSpec as P


NODES = 64
REACH = 6
SPRING = 8.0
ANCHOR = 0.02
PRIOR = 1.0

HALO = 32
CHUNK = 32
DEPTH = 80
TALL = 8
WIDE = 16
EDGE = 8
GROUP = 2
FAR = -1e30
LATE = 2

FIRST_ROW = HALO - (4 * REACH + 3)


def iota(shape, dim):
    return lax.broadcasted_iota(jnp.int32, shape, dim)


def pick_columns(extent):
    quarter = extent // 4
    source = iota((extent, extent), 0)
    place = iota((extent, extent), 1)
    wanted = 4 * (place % quarter) + place // quarter
    return jnp.where(source == wanted, 1.0, 0.0).astype(jnp.bfloat16)


def first_matrix(conv_one):
    channels = conv_one.shape[0]
    spread = []
    for a in range(3):
        tap = iota((9, 3 * DEPTH), 0)
        b = iota((9, 3 * DEPTH), 1) // DEPTH
        chosen = jnp.where(tap == 3 * a + b, 1.0, 0.0).astype(jnp.bfloat16)
        spread.append(jnp.dot(conv_one, chosen, preferred_element_type=jnp.float32))
    row = iota((channels, 3 * DEPTH), 1) % DEPTH - FIRST_ROW
    blocks = []
    for out in range(CHUNK):
        block = jnp.zeros_like(spread[0])
        for a in range(3):
            block = jnp.where(row == 2 * out + a, spread[a], block)
        blocks.append(block.astype(jnp.bfloat16))
    return jnp.concatenate(blocks, axis=0)


def second_matrix(conv_two):
    taps = conv_two.shape[1]
    inner = taps // 9
    rows = []
    for out in range(2):
        source = iota((taps, 15 * inner), 0)
        place = iota((taps, 15 * inner), 1)
        a = place // (3 * inner) - 2 * out
        b = (place // inner) % 3
        wanted = 9 * (place % inner) + 3 * a + b
        inside = (a >= 0) & (a < 3) & (source == wanted)
        chosen = jnp.where(inside, 1.0, 0.0).astype(jnp.bfloat16)
        rows.append(jnp.dot(conv_two, chosen, preferred_element_type=jnp.float32))
    return jnp.concatenate(rows, axis=0).astype(jnp.bfloat16)


def split_columns(pixels, picks):
    quarter = pixels.shape[1] // 4
    split = jnp.dot(pixels, picks, preferred_element_type=jnp.float32)
    parts = [split[:, q * quarter : (q + 1) * quarter] for q in range(4)]
    before = jnp.where(iota(parts[3].shape, 1) == 0, 0.0, pltpu.roll(parts[3], 1, 1))
    return [part.astype(jnp.bfloat16) for part in [before] + parts]


def first_maps(columns, matrix, maps, start):
    channels, quarter = maps.shape[2:]
    span = slice(start, start + DEPTH)
    taken = jnp.concatenate(
        [jnp.concatenate([columns[b][span], columns[b + 2][span]], axis=1) for b in range(3)],
        axis=0,
    )
    values = jnp.maximum(jnp.dot(matrix, taken, preferred_element_type=jnp.float32), 0.0)
    even, odd = values[:, :quarter], values[:, quarter:]
    before = jnp.where(iota(odd.shape, 1) == 0, 0.0, pltpu.roll(odd, 1, 1))
    for b, part in enumerate((before, even, odd)):
        maps[:, b] = part.astype(jnp.bfloat16).reshape(-1, channels, quarter)


def maps_between(columns, matrix, maps, low, high):
    channels = maps.shape[2]
    for chunk in range(low // CHUNK, -(-high // CHUNK)):
        one, two = max(low - chunk * CHUNK, 0), min(high - chunk * CHUNK, CHUNK)
        first_maps(
            columns,
            matrix[one * channels : two * channels],
            maps.at[chunk * CHUNK + one : chunk * CHUNK + two],
            2 * CHUNK * chunk,
        )


def feature_rows(maps, matrix, pair, count):
    parts = []
    for number in range(pair, pair + count):
        part = maps[4 * number : 4 * number + 5]
        parts.append(part.reshape(-1, part.shape[-1]))
    taken = jnp.concatenate(parts, axis=1) if count > 1 else parts[0]
    values = jnp.maximum(jnp.dot(matrix, taken, preferred_element_type=jnp.float32), 0.0)
    lanes = values.shape[1] // count
    return [values[:, n * lanes : (n + 1) * lanes] for n in range(count)]


def prepare_kernel(
    image, conv_one, conv_two, tissue, picks, matrix_one, matrix_two, split, middle, marks
):
    marks[...] = tissue[...].astype(jnp.float32)
    picks[...] = pick_columns(image.shape[2])
    matrix_one[...] = first_matrix(conv_one[...])
    matrix_two[...] = second_matrix(conv_two[...])
    columns = split_columns(image[0], picks[...])
    for number, part in enumerate(columns):
        split[number] = part
    first_maps(columns, matrix_one[...], middle, 2 * CHUNK - HALO)


def keys_kernel(total, near, far, picks, matrix_one, matrix_two, split, middle, keys, maps):
    place = lax.axis_index("gy")
    odd = place % 2 == 1
    a, b = near[0], far[0]
    above = jnp.where(place == 0, jnp.zeros_like(a), jnp.where(odd, a, b))
    below = jnp.where(odd, b, a)
    outer = split_columns(jnp.concatenate([above, below], axis=0), picks[...])
    local = split.shape[1] // 4
    spare = jnp.zeros((DEPTH - 2 * CHUNK, split.shape[2]), jnp.bfloat16)
    columns = [
        jnp.concatenate([part[:HALO], split[n], part[HALO:], spare], axis=0)
        for n, part in enumerate(outer)
    ]
    channels = matrix_two.shape[0] // 2
    matrix = matrix_one[...]
    maps_between(columns, matrix, maps, 0, CHUNK)
    maps[CHUNK : 2 * CHUNK] = middle[...]
    maps_between(columns, matrix, maps, 2 * CHUNK, 2 * GROUP * keys.shape[0] + 1)
    last = place == total - 1
    edge = jnp.zeros((EDGE, GROUP * channels), jnp.float32)
    matrix = matrix_two[...]
    shape = (keys.shape[1], WIDE)
    column = jnp.where(iota(shape, 0) % WIDE == iota(shape, 1), 1.0, 0.0).astype(jnp.bfloat16)
    groups = keys.shape[0]
    for group in range(0, groups, 2):
        for both in feature_rows(maps, matrix, group, min(2, groups - group)):
            if GROUP * (group + 1) > local + REACH:
                row = GROUP * group + iota(both.shape, 0) // channels
                both = jnp.where(last & (row >= local + REACH), 0.0, both)
            turned = jnp.concatenate([edge, both.T, edge], axis=0)
            turned = jnp.concatenate([turned.astype(jnp.bfloat16), column], axis=1)
            keys[group] = turned
            group += 1


def swap_blocks(rows, width):
    count = len(rows)
    lanes = rows[0].shape[1]
    step = 1
    while step < count:
        low = (iota(rows[0].shape, 1) // width) % (2 * step) < step
        fresh = list(rows)
        for index in range(count):
            if index & step == 0:
                one, two = rows[index], rows[index + step]
                shift = width * step
                fresh[index] = jnp.where(low, one, pltpu.roll(two, shift, 1))
                fresh[index + step] = jnp.where(low, pltpu.roll(one, lanes - shift, 1), two)
        rows = fresh
        step *= 2
    return rows


def match_tiles(queries, keys, sums, band):
    channels = queries.shape[1]
    lanes = TALL * WIDE
    tiles = queries.shape[0]
    across = (keys.shape[1] - 2 * EDGE) // WIDE
    depth, breadth = TALL + 2 * REACH, 2 * WIDE
    span = 2 * REACH + 1
    own_row = iota((WIDE, lanes), 1) // WIDE
    own_col = iota((WIDE, lanes), 1) % WIDE
    shift_col = iota((WIDE, lanes), 0) - EDGE - own_col
    left = shift_col >= -REACH
    shift_col = jnp.where(left, shift_col, shift_col + WIDE)
    barred = jnp.where(jnp.abs(shift_col) > REACH, FAR, 0.0).astype(jnp.bfloat16)
    barred = jnp.concatenate([barred] * GROUP, axis=1)
    shift_col = shift_col.astype(jnp.float32)
    shift_row = []
    for row in range(span):
        shift = row - REACH - own_row[:8]
        shift_row.append(jnp.where(shift < -REACH, shift + span, shift).astype(jnp.float32))
    factor = channels**-0.5 * 1.4426950408889634

    for tile in reversed(range(tiles)):
        tall, wide = band + tile // across, tile % across
        window = keys[
            TALL // GROUP * tall : TALL // GROUP * tall + depth // GROUP,
            WIDE * wide : WIDE * wide + breadth,
            :,
        ]
        own = queries[tile]
        empty = jnp.zeros_like(own)
        spread = jnp.concatenate(
            [
                jnp.concatenate([own if i == j else empty for j in range(GROUP)], axis=1)
                for i in range(GROUP)
            ]
            + [barred],
            axis=0,
        )
        scores = jnp.dot(
            window.reshape(-1, window.shape[-1]), spread, preferred_element_type=jnp.float32
        )
        parts = []
        for row in range(depth):
            i, j = row // GROUP, row % GROUP
            part = scores[i * breadth : (i + 1) * breadth, j * lanes : (j + 1) * lanes]
            parts.append(jnp.where(left, part[:WIDE], part[WIDE:]))
        for row in range(depth - span):
            parts[row] = jnp.where(own_row <= row, parts[row], parts[row + span])
        parts = parts[:span]
        highest = functools.reduce(jnp.maximum, parts)
        highest = jnp.max(highest, axis=0, keepdims=True)
        mass = jnp.zeros((WIDE, lanes), jnp.float32)
        once = mass
        twice = jnp.zeros((8, lanes), jnp.float32)
        for row in range(span):
            prob = jnp.exp2((parts[row] - highest) * factor)
            mass = mass + prob
            weighted = (prob.reshape(-1, 8, lanes) * shift_row[row]).reshape(WIDE, lanes)
            once = once + weighted
            twice = twice + jnp.sum(weighted.reshape(-1, 8, lanes), axis=0) * shift_row[row]
        moments = (
            mass,
            once,
            twice,
            mass * shift_col,
            mass * shift_col * shift_col,
            once * shift_col,
        )
        for number, moment in enumerate(moments):
            sums[number, tile : tile + 1, :] = jnp.sum(moment, axis=0, keepdims=True)


def pooled_fields(sums, across):
    total = sums[0]
    mean_row = sums[1] / total
    row_square = sums[2] / total
    col_mean = sums[3] / total
    col_square = sums[4] / total
    product = sums[5] / total
    var_row = row_square - mean_row * mean_row + PRIOR
    var_col = col_square - col_mean * col_mean + PRIOR
    covar = product - mean_row * col_mean
    determ = var_row * var_col - covar * covar
    info_rr = var_col / determ
    info_rc = -covar / determ
    info_cc = var_row / determ
    pull_row = info_rr * mean_row + info_rc * col_mean
    pull_col = info_rc * mean_row + info_cc * col_mean
    fields = jnp.concatenate([info_rr, info_rc, info_cc, pull_row, pull_col], axis=0)

    lanes = TALL * WIDE
    patch = across * WIDE // NODES
    high, broad = TALL // patch, WIDE // patch
    out_lanes = high * NODES
    source = iota((lanes, out_lanes), 0)
    place = iota((lanes, out_lanes), 1)
    same = (source // WIDE // patch == place // NODES) & (
        source % WIDE // patch == place % NODES % broad
    )
    pool = jnp.where(same, 1.0 / (patch * patch), 0.0)
    pooled = jnp.dot(
        fields, pool, preferred_element_type=jnp.float32, precision=lax.Precision.HIGHEST
    )
    mine = iota(pooled.shape, 0) % across == iota(pooled.shape, 1) % NODES // broad
    pooled = jnp.where(mine, pooled, 0.0)
    return jnp.sum(pooled.reshape(-1, across, out_lanes), axis=1)


def rest_kernel(
    image, picks, matrix_one, matrix_two, keys, sums, kept, ready, maps, queries
):
    columns = []
    for part in split_columns(image[0], picks[...]):
        above = jnp.zeros((HALO, part.shape[1]), jnp.bfloat16)
        below = jnp.zeros((HALO + DEPTH - 2 * CHUNK, part.shape[1]), jnp.bfloat16)
        columns.append(jnp.concatenate([above, part, below], axis=0))
    channels = queries.shape[1]
    across = (keys.shape[1] - 2 * EDGE) // WIDE
    bands = queries.shape[0] // across + LATE
    first = 2 * REACH
    maps_between(columns, matrix_one, maps, first + 2, first + 2 * TALL * bands + 1)
    matrix = matrix_two[...]
    for band in range(bands):
        rows = []
        skip = 1 if band == 0 else 0
        pair = (REACH + TALL * band) // 2
        values = []
        for number in range(skip, TALL // 2, 2):
            values += feature_rows(maps, matrix, pair + number, min(2, TALL // 2 - number))
        for both in values:
            rows += [both[:channels], both[channels:]]
        if band == 0:
            for number, row in enumerate(rows):
                kept[number] = row
            continue
        place, start = (ready, 1) if band < LATE else (queries, LATE)
        for wide, block in enumerate(swap_blocks(rows, WIDE)):
            place[across * (band - start) + wide] = block.astype(jnp.bfloat16)
    match_tiles(queries, keys, sums, LATE)


def first_kernel(
    image, corner, picks, matrix_one, matrix_two, keys, kept, ready, others, marks,
    blocks, maps, queries, sums,
):
    channels = queries.shape[1]
    across = queries.shape[0] // LATE
    above = jnp.where(lax.axis_index("gy") == 0, jnp.zeros_like(corner[0]), corner[0])
    pixels = jnp.concatenate([above, image[0, : DEPTH - HALO]], axis=0)
    begin = 2 * REACH * maps.shape[2]
    matrix = matrix_one[begin : begin + maps.shape[0] * maps.shape[2]]
    first_maps(split_columns(pixels, picks[...]), matrix, maps, 0)
    both = feature_rows(maps, matrix_two[...], 0, 1)[0]
    rows = [both[:channels], both[channels:]] + [kept[n] for n in range(TALL - 2)]
    for wide, block in enumerate(swap_blocks(rows, WIDE)):
        queries[wide] = block.astype(jnp.bfloat16)
    for tile in range(across, LATE * across):
        queries[tile] = ready[tile - across]
    match_tiles(queries, keys, sums, 0)
    pooled = pooled_fields(
        [jnp.concatenate([sums[n], others[n]], axis=0) for n in range(6)], across
    )

    halves = pooled.shape[1] // 128
    bands = pooled.shape[0] // 5
    pieces, signs = [], []
    for field in range(5):
        for half in range(halves):
            place = slice(half * 128, (half + 1) * 128)
            pieces.append(pooled[field * bands : (field + 1) * bands, place])
    for half in range(halves):
        for band in range(bands):
            start = (band * halves + half) * 128
            signs.append(marks[:, start : start + 128])
    block = jnp.concatenate(pieces, axis=0)
    size = block.shape[0] // 5
    signed = block[:size] * (2.0 * jnp.concatenate(signs, axis=0) - 1.0)
    block = jnp.concatenate([signed, block[size:]], axis=0)

    def put(peer, carry):
        blocks[peer] = block
        return carry

    lax.fori_loop(0, blocks.shape[0], put, 0, unroll=blocks.shape[0] <= 16)


def solve_kernel(bands, gathered, out, inverse, partial):
    count = gathered.shape[0]
    place = lax.axis_index("gz")
    size = gathered.shape[1] // 5

    def forward(section, carry):
        inv_a, inv_b, inv_c, one, two = carry
        inside = jnp.where(section < count - 1, 1.0, 0.0)
        above = jnp.where(section > 0, 1.0, 0.0)
        extra = SPRING * (inside + above) + ANCHOR
        data = gathered[jnp.minimum(section + 1, count - 1)]
        keep = jnp.where(gathered[section, :size] > 0.0, inside, 0.0)
        fields = [data[k * size : (k + 1) * size] for k in range(5)]
        fields = [member * keep for member in [jnp.abs(fields[0])] + fields[1:]]
        square = SPRING * SPRING * above
        pulled = SPRING * above
        a = fields[0] + extra - square * inv_a
        b = fields[1] - square * inv_b
        c = fields[2] + extra - square * inv_c
        right_one = fields[3] + pulled * one
        right_two = fields[4] + pulled * two
        scale = 1.0 / (a * c - b * b)
        inv_a, inv_b, inv_c = c * scale, -b * scale, a * scale
        one, two = inv_a * right_one + inv_b * right_two, inv_b * right_one + inv_c * right_two
        for k, member in enumerate((inv_a, inv_b, inv_c)):
            inverse[section, k] = member
        partial[section, 0], partial[section, 1] = one, two
        return inv_a, inv_b, inv_c, one, two

    def backward(number, carry):
        one, two, own_one, own_two = carry
        section = count - 1 - number
        inv_a, inv_b, inv_c = (inverse[section, k] for k in range(3))
        fresh_one = partial[section, 0] + SPRING * (inv_a * one + inv_b * two)
        fresh_two = partial[section, 1] + SPRING * (inv_b * one + inv_c * two)
        mine = section == place
        own_one = jnp.where(mine, fresh_one, own_one)
        own_two = jnp.where(mine, fresh_two, own_two)
        return fresh_one, fresh_two, own_one, own_two

    zero = jnp.zeros((size, 128), jnp.float32)
    unroll = count <= 16
    lax.fori_loop(0, count, forward, (zero,) * 5, unroll=unroll)
    _, _, one, two = lax.fori_loop(0, count, backward, (zero,) * 4, unroll=unroll)
    halves = size // bands
    for number, solved in enumerate((one, two)):
        for band in range(bands):
            for half in range(halves):
                row = half * bands + band
                start = (band * halves + half) * 128
                out[number, :, start : start + 128] = solved[row : row + 1]


def body(image, conv_one, conv_two, tissue):
    height, extent = image.shape[1:]
    width = extent // 4
    rows = height // 4
    channels = conv_two.shape[0]
    across, bands = width // WIDE, rows // TALL
    tiles = across * bands
    peers, total = lax.axis_size("gz"), lax.axis_size("gy")
    vmem = pl.BlockSpec(memory_space=pltpu.VMEM)

    limit = pltpu.CompilerParams(vmem_limit_bytes=16 << 20)

    def call(kernel, name, ins, outs, scratch=()):
        return pl.pallas_call(
            kernel,
            out_shape=[jax.ShapeDtypeStruct(*out) for out in outs],
            in_specs=[vmem] * len(ins),
            out_specs=[vmem] * len(outs),
            scratch_shapes=list(scratch),
            compiler_params=limit,
            name=name,
            cost_estimate=pl.CostEstimate(
                flops=10**9, bytes_accessed=2 * 10**6, transcendentals=0
            ),
        )(*ins)

    main = lax.ppermute(image, "gz", [(z, (z + 1) % peers) for z in range(peers)])
    top, bottom = image[:, :HALO], image[:, height - HALO :]
    odd = lax.axis_index("gy") % 2 == 1
    near, far = jnp.where(odd, top, bottom), jnp.where(odd, bottom, top)

    def swapped(block, first):
        pairs = [(y, (y + 1) % total) for y in range(first, total, 2)]
        return lax.ppermute(block, "gy", pairs + [(b, a) for a, b in pairs])

    near, far = swapped(near, 0), swapped(far, 1)
    corner = lax.ppermute(
        bottom,
        ("gz", "gy"),
        [
            (z * total + y, (z + 1) % peers * total + (y + 1) % total)
            for z in range(peers)
            for y in range(total)
        ],
    )

    inner = conv_one.shape[0]
    key_rows = rows + 2 * REACH
    map_rows = -(-(2 * key_rows + 1) // CHUNK) * CHUNK
    maps = pltpu.VMEM((map_rows, 3, inner, width), jnp.bfloat16)
    shapes = (
        (extent, extent),
        (CHUNK * inner, 3 * DEPTH),
        (2 * channels, 15 * inner),
        (5, height, width),
        (CHUNK, 3, inner, width),
    )
    *matrices, split, middle, marks = call(
        prepare_kernel,
        "prepare",
        (image, conv_one, conv_two, tissue),
        [(shape, jnp.bfloat16) for shape in shapes] + [(tissue.shape, jnp.float32)],
    )
    (keys,) = call(
        functools.partial(keys_kernel, total),
        "keys",
        (near, far, *matrices, split, middle),
        [((key_rows // GROUP, width + 2 * EDGE, GROUP * channels + WIDE), jnp.bfloat16)],
        [maps],
    )

    size = tiles * TALL * WIDE // (width // NODES) ** 2 // 128

    def scratch(tiles, maps):
        return [
            maps,
            pltpu.VMEM((tiles, channels, TALL * WIDE), jnp.bfloat16),
            pltpu.VMEM((6, tiles, TALL * WIDE), jnp.float32),
        ]

    others, kept, ready = call(
        rest_kernel,
        "rest",
        (main, *matrices, keys),
        [
            ((6, tiles - LATE * across, TALL * WIDE), jnp.float32),
            ((TALL - 2, channels, width), jnp.float32),
            (((LATE - 1) * across, channels, TALL * WIDE), jnp.bfloat16),
        ],
        scratch(tiles - LATE * across, maps)[:2],
    )
    (blocks,) = call(
        first_kernel,
        "first",
        (main, corner, *matrices, keys, kept, ready, others, marks),
        [((peers, 5 * size, 128), jnp.float32)],
        scratch(LATE * across, pltpu.VMEM((5, 3, inner, width), jnp.bfloat16)),
    )
    gathered = lax.all_to_all(blocks, "gz", split_axis=0, concat_axis=0, tiled=True)
    (out,) = call(
        functools.partial(solve_kernel, bands),
        "solve",
        (gathered,),
        [((2, 1, tissue.shape[1]), jnp.float32)],
        [
            pltpu.VMEM((peers, 3, size, 128), jnp.float32),
            pltpu.VMEM((peers, 2, size, 128), jnp.float32),
        ],
    )
    return out


def solution(mesh):
    placed = (P("gz", "gy", None), P(), P(), P("gz", "gy"))
    return jax.shard_map(
        body, mesh=mesh, in_specs=placed, out_specs=P(None, "gz", "gy"), check_vma=False
    )
```

```python
import functools

import jax
import jax.numpy as jnp
from jax import lax
from jax.experimental import pallas as pl
from jax.experimental.pallas import tpu as pltpu
from jax.sharding import PartitionSpec as P


NODES = 64
REACH = 6
SPRING = 8.0
ANCHOR = 0.02
PRIOR = 1.0

HALO = 32
CHUNK = 32
DEPTH = 80
TALL = 8
WIDE = 16
EDGE = 8
GROUP = 2
FAR = -1e30
PACE = 2
LATE = 2

FIRST_ROW = HALO - (4 * REACH + 3)


def iota(shape, dim):
    return lax.broadcasted_iota(jnp.int32, shape, dim)


def pick_columns(extent):
    quarter = extent // 4
    source = iota((extent, extent), 0)
    place = iota((extent, extent), 1)
    wanted = 4 * (place % quarter) + place // quarter
    return jnp.where(source == wanted, 1.0, 0.0).astype(jnp.bfloat16)


def first_matrix(conv_one):
    channels = conv_one.shape[0]
    spread = []
    for a in range(3):
        tap = iota((9, 3 * DEPTH), 0)
        b = iota((9, 3 * DEPTH), 1) // DEPTH
        chosen = jnp.where(tap == 3 * a + b, 1.0, 0.0).astype(jnp.bfloat16)
        spread.append(jnp.dot(conv_one, chosen, preferred_element_type=jnp.float32))
    row = iota((channels, 3 * DEPTH), 1) % DEPTH - FIRST_ROW
    blocks = []
    for out in range(CHUNK):
        block = jnp.zeros_like(spread[0])
        for a in range(3):
            block = jnp.where(row == 2 * out + a, spread[a], block)
        blocks.append(block.astype(jnp.bfloat16))
    return jnp.concatenate(blocks, axis=0)


def second_matrix(conv_two):
    taps = conv_two.shape[1]
    inner = taps // 9
    rows = []
    for out in range(2):
        source = iota((taps, 15 * inner), 0)
        place = iota((taps, 15 * inner), 1)
        a = place // (3 * inner) - 2 * out
        b = (place // inner) % 3
        wanted = 9 * (place % inner) + 3 * a + b
        inside = (a >= 0) & (a < 3) & (source == wanted)
        chosen = jnp.where(inside, 1.0, 0.0).astype(jnp.bfloat16)
        rows.append(jnp.dot(conv_two, chosen, preferred_element_type=jnp.float32))
    return jnp.concatenate(rows, axis=0).astype(jnp.bfloat16)


def split_columns(pixels, picks):
    quarter = pixels.shape[1] // 4
    split = jnp.dot(pixels, picks, preferred_element_type=jnp.float32)
    parts = [split[:, q * quarter : (q + 1) * quarter] for q in range(4)]
    before = jnp.where(iota(parts[3].shape, 1) == 0, 0.0, pltpu.roll(parts[3], 1, 1))
    return [part.astype(jnp.bfloat16) for part in [before] + parts]


def first_maps(columns, matrix, maps, start):
    channels, quarter = maps.shape[2:]
    span = slice(start, start + DEPTH)
    taken = jnp.concatenate(
        [jnp.concatenate([columns[b][span], columns[b + 2][span]], axis=1) for b in range(3)],
        axis=0,
    )
    values = jnp.maximum(jnp.dot(matrix, taken, preferred_element_type=jnp.float32), 0.0)
    even, odd = values[:, :quarter], values[:, quarter:]
    before = jnp.where(iota(odd.shape, 1) == 0, 0.0, pltpu.roll(odd, 1, 1))
    for b, part in enumerate((before, even, odd)):
        maps[:, b] = part.astype(jnp.bfloat16).reshape(-1, channels, quarter)


def maps_between(columns, matrix, maps, low, high):
    channels = maps.shape[2]
    for chunk in range(low // CHUNK, -(-high // CHUNK)):
        one, two = max(low - chunk * CHUNK, 0), min(high - chunk * CHUNK, CHUNK)
        first_maps(
            columns,
            matrix[one * channels : two * channels],
            maps.at[chunk * CHUNK + one : chunk * CHUNK + two],
            2 * CHUNK * chunk,
        )


def feature_rows(maps, matrix, pair, count):
    parts = []
    for number in range(pair, pair + count):
        part = maps[4 * number : 4 * number + 5]
        parts.append(part.reshape(-1, part.shape[-1]))
    taken = jnp.concatenate(parts, axis=1) if count > 1 else parts[0]
    values = jnp.maximum(jnp.dot(matrix, taken, preferred_element_type=jnp.float32), 0.0)
    lanes = values.shape[1] // count
    return [values[:, n * lanes : (n + 1) * lanes] for n in range(count)]


def prepare_kernel(
    image, conv_one, conv_two, tissue, picks, matrix_one, matrix_two, split, middle, marks
):
    marks[...] = tissue[...].astype(jnp.float32)
    picks[...] = pick_columns(image.shape[2])
    matrix_one[...] = first_matrix(conv_one[...])
    matrix_two[...] = second_matrix(conv_two[...])
    columns = split_columns(image[0], picks[...])
    for number, part in enumerate(columns):
        split[number] = part
    first_maps(columns, matrix_one[...], middle, 2 * CHUNK - HALO)


def keys_kernel(total, near, far, picks, matrix_one, matrix_two, split, middle, keys, maps):
    place = lax.axis_index("gy")
    odd = place % 2 == 1
    a, b = near[0], far[0]
    above = jnp.where(place == 0, jnp.zeros_like(a), jnp.where(odd, a, b))
    below = jnp.where(odd, b, a)
    outer = split_columns(jnp.concatenate([above, below], axis=0), picks[...])
    local = split.shape[1] // 4
    spare = jnp.zeros((DEPTH - 2 * CHUNK, split.shape[2]), jnp.bfloat16)
    columns = [
        jnp.concatenate([part[:HALO], split[n], part[HALO:], spare], axis=0)
        for n, part in enumerate(outer)
    ]
    channels = matrix_two.shape[0] // 2
    matrix = matrix_one[...]
    maps_between(columns, matrix, maps, 0, CHUNK)
    maps[CHUNK : 2 * CHUNK] = middle[...]
    maps_between(columns, matrix, maps, 2 * CHUNK, 2 * GROUP * keys.shape[0] + 1)
    last = place == total - 1
    edge = jnp.zeros((EDGE, GROUP * channels), jnp.float32)
    matrix = matrix_two[...]
    shape = (keys.shape[1], WIDE)
    column = jnp.where(iota(shape, 0) % WIDE == iota(shape, 1), 1.0, 0.0).astype(jnp.bfloat16)
    groups = keys.shape[0]
    for group in range(0, groups, 2):
        for both in feature_rows(maps, matrix, group, min(2, groups - group)):
            if GROUP * (group + 1) > local + REACH:
                row = GROUP * group + iota(both.shape, 0) // channels
                both = jnp.where(last & (row >= local + REACH), 0.0, both)
            turned = jnp.concatenate([edge, both.T, edge], axis=0)
            turned = jnp.concatenate([turned.astype(jnp.bfloat16), column], axis=1)
            keys[group] = turned
            group += 1


def swap_blocks(rows, width):
    count = len(rows)
    lanes = rows[0].shape[1]
    step = 1
    while step < count:
        low = (iota(rows[0].shape, 1) // width) % (2 * step) < step
        fresh = list(rows)
        for index in range(count):
            if index & step == 0:
                one, two = rows[index], rows[index + step]
                shift = width * step
                fresh[index] = jnp.where(low, one, pltpu.roll(two, shift, 1))
                fresh[index + step] = jnp.where(low, pltpu.roll(one, lanes - shift, 1), two)
        rows = fresh
        step *= 2
    return rows


def matcher(queries, keys, sums, band):
    channels = queries.shape[1]
    lanes = TALL * WIDE
    across = (keys.shape[1] - 2 * EDGE) // WIDE
    depth, breadth = TALL + 2 * REACH, 2 * WIDE
    span = 2 * REACH + 1
    own_row = iota((WIDE, lanes), 1) // WIDE
    own_col = iota((WIDE, lanes), 1) % WIDE
    shift_col = iota((WIDE, lanes), 0) - EDGE - own_col
    left = shift_col >= -REACH
    shift_col = jnp.where(left, shift_col, shift_col + WIDE)
    barred = jnp.where(jnp.abs(shift_col) > REACH, FAR, 0.0).astype(jnp.bfloat16)
    barred = jnp.concatenate([barred] * GROUP, axis=1)
    shift_col = shift_col.astype(jnp.float32)
    shift_row = []
    for row in range(span):
        shift = row - REACH - own_row[:8]
        shift_row.append(jnp.where(shift < -REACH, shift + span, shift).astype(jnp.float32))
    factor = channels**-0.5 * 1.4426950408889634

    def match(tile):
        tall, wide = band + tile // across, tile % across
        window = keys[
            TALL // GROUP * tall : TALL // GROUP * tall + depth // GROUP,
            WIDE * wide : WIDE * wide + breadth,
            :,
        ]
        own = queries[tile]
        empty = jnp.zeros_like(own)
        spread = jnp.concatenate(
            [
                jnp.concatenate([own if i == j else empty for j in range(GROUP)], axis=1)
                for i in range(GROUP)
            ]
            + [barred],
            axis=0,
        )
        scores = jnp.dot(
            window.reshape(-1, window.shape[-1]), spread, preferred_element_type=jnp.float32
        )
        parts = []
        for row in range(depth):
            i, j = row // GROUP, row % GROUP
            part = scores[i * breadth : (i + 1) * breadth, j * lanes : (j + 1) * lanes]
            parts.append(jnp.where(left, part[:WIDE], part[WIDE:]))
        for row in range(depth - span):
            parts[row] = jnp.where(own_row <= row, parts[row], parts[row + span])
        parts = parts[:span]
        highest = functools.reduce(jnp.maximum, parts)
        highest = jnp.max(highest, axis=0, keepdims=True)
        mass = jnp.zeros((WIDE, lanes), jnp.float32)
        once = mass
        twice = jnp.zeros((8, lanes), jnp.float32)
        for row in range(span):
            prob = jnp.exp2((parts[row] - highest) * factor)
            mass = mass + prob
            weighted = (prob.reshape(-1, 8, lanes) * shift_row[row]).reshape(WIDE, lanes)
            once = once + weighted
            twice = twice + jnp.sum(weighted.reshape(-1, 8, lanes), axis=0) * shift_row[row]
        moments = (
            mass,
            once,
            twice,
            mass * shift_col,
            mass * shift_col * shift_col,
            once * shift_col,
        )
        for number, moment in enumerate(moments):
            sums[number, tile : tile + 1, :] = jnp.sum(moment, axis=0, keepdims=True)

    return match


def pooled_fields(sums, across):
    total = sums[0]
    mean_row = sums[1] / total
    row_square = sums[2] / total
    col_mean = sums[3] / total
    col_square = sums[4] / total
    product = sums[5] / total
    var_row = row_square - mean_row * mean_row + PRIOR
    var_col = col_square - col_mean * col_mean + PRIOR
    covar = product - mean_row * col_mean
    determ = var_row * var_col - covar * covar
    info_rr = var_col / determ
    info_rc = -covar / determ
    info_cc = var_row / determ
    pull_row = info_rr * mean_row + info_rc * col_mean
    pull_col = info_rc * mean_row + info_cc * col_mean
    fields = jnp.concatenate([info_rr, info_rc, info_cc, pull_row, pull_col], axis=0)

    lanes = TALL * WIDE
    patch = across * WIDE // NODES
    high, broad = TALL // patch, WIDE // patch
    out_lanes = high * NODES
    source = iota((lanes, out_lanes), 0)
    place = iota((lanes, out_lanes), 1)
    same = (source // WIDE // patch == place // NODES) & (
        source % WIDE // patch == place % NODES % broad
    )
    pool = jnp.where(same, 1.0 / (patch * patch), 0.0)
    pooled = jnp.dot(
        fields, pool, preferred_element_type=jnp.float32, precision=lax.Precision.HIGHEST
    )
    mine = iota(pooled.shape, 0) % across == iota(pooled.shape, 1) % NODES // broad
    pooled = jnp.where(mine, pooled, 0.0)
    return jnp.sum(pooled.reshape(-1, across, out_lanes), axis=1)


def rest_kernel(
    image, picks, matrix_one, matrix_two, keys, sums, kept, ready, maps, queries
):
    columns = []
    for part in split_columns(image[0], picks[...]):
        above = jnp.zeros((HALO, part.shape[1]), jnp.bfloat16)
        below = jnp.zeros((HALO + DEPTH - 2 * CHUNK, part.shape[1]), jnp.bfloat16)
        columns.append(jnp.concatenate([above, part, below], axis=0))
    channels = queries.shape[1]
    across = (keys.shape[1] - 2 * EDGE) // WIDE
    bands = queries.shape[0] // across + LATE
    first = 2 * REACH
    maps_between(columns, matrix_one, maps, first + 2, first + 2 * TALL * bands + 1)
    matrix = matrix_two[...]
    for band in range(bands):
        rows = []
        skip = 1 if band == 0 else 0
        pair = (REACH + TALL * band) // 2
        values = []
        for number in range(skip, TALL // 2, 2):
            values += feature_rows(maps, matrix, pair + number, min(2, TALL // 2 - number))
        for both in values:
            rows += [both[:channels], both[channels:]]
        if band == 0:
            for number, row in enumerate(rows):
                kept[number] = row
            continue
        place, start = (ready, 1) if band < LATE else (queries, LATE)
        for wide, block in enumerate(swap_blocks(rows, WIDE)):
            place[across * (band - start) + wide] = block.astype(jnp.bfloat16)
    match = matcher(queries, keys, sums, LATE)
    for tile in reversed(range(queries.shape[0])):
        match(tile)


def first_kernel(
    image, corner, picks, matrix_one, matrix_two, keys, kept, ready, others, marks,
    blocks, maps, queries, sums,
):
    channels = queries.shape[1]
    across = queries.shape[0] // LATE
    above = jnp.where(lax.axis_index("gy") == 0, jnp.zeros_like(corner[0]), corner[0])
    pixels = jnp.concatenate([above, image[0, : DEPTH - HALO]], axis=0)
    begin = 2 * REACH * maps.shape[2]
    matrix = matrix_one[begin : begin + maps.shape[0] * maps.shape[2]]
    for tile in range(across, LATE * across):
        queries[tile] = ready[tile - across]
    match = matcher(queries, keys, sums, 0)
    waiting = [*range(across, LATE * across)]

    def pause():
        for _ in range(min(PACE, len(waiting))):
            match(waiting.pop(0))

    columns = split_columns(pixels, picks[...])
    pause()
    first_maps(columns, matrix, maps, 0)
    pause()
    both = feature_rows(maps, matrix_two[...], 0, 1)[0]
    pause()
    rows = [both[:channels], both[channels:]] + [kept[n] for n in range(TALL - 2)]
    for wide, block in enumerate(swap_blocks(rows, WIDE)):
        queries[wide] = block.astype(jnp.bfloat16)
    waiting += range(across)
    while waiting:
        pause()
    pooled = pooled_fields(
        [jnp.concatenate([sums[n], others[n]], axis=0) for n in range(6)], across
    )

    halves = pooled.shape[1] // 128
    bands = pooled.shape[0] // 5
    pieces, signs = [], []
    for field in range(5):
        for half in range(halves):
            place = slice(half * 128, (half + 1) * 128)
            pieces.append(pooled[field * bands : (field + 1) * bands, place])
    for half in range(halves):
        for band in range(bands):
            start = (band * halves + half) * 128
            signs.append(marks[:, start : start + 128])
    block = jnp.concatenate(pieces, axis=0)
    size = block.shape[0] // 5
    signed = block[:size] * (2.0 * jnp.concatenate(signs, axis=0) - 1.0)
    pull = block[3 * size :]
    part = pull.astype(jnp.bfloat16).astype(jnp.float32)
    block = jnp.concatenate([signed, block[size : 3 * size], part, pull - part], axis=0)
    block = block.astype(jnp.bfloat16)

    def put(peer, carry):
        blocks[peer] = block
        return carry

    lax.fori_loop(0, blocks.shape[0], put, 0, unroll=blocks.shape[0] <= 16)


def solve_kernel(bands, gathered, out, inverse, partial):
    count = gathered.shape[0]
    place = lax.axis_index("gz")
    size = gathered.shape[1] // 7

    def forward(section, carry):
        inv_a, inv_b, inv_c, one, two = carry
        inside = jnp.where(section < count - 1, 1.0, 0.0)
        above = jnp.where(section > 0, 1.0, 0.0)
        extra = SPRING * (inside + above) + ANCHOR
        data = gathered[jnp.minimum(section + 1, count - 1)].astype(jnp.float32)
        own = gathered[section].astype(jnp.float32)
        keep = jnp.where(own[:size] > 0.0, inside, 0.0)
        data = jnp.concatenate(
            [data[: 3 * size], data[3 * size : 5 * size] + data[5 * size :]], axis=0
        )
        fields = [data[k * size : (k + 1) * size] for k in range(5)]
        fields = [member * keep for member in [jnp.abs(fields[0])] + fields[1:]]
        square = SPRING * SPRING * above
        pulled = SPRING * above
        a = fields[0] + extra - square * inv_a
        b = fields[1] - square * inv_b
        c = fields[2] + extra - square * inv_c
        right_one = fields[3] + pulled * one
        right_two = fields[4] + pulled * two
        scale = 1.0 / (a * c - b * b)
        inv_a, inv_b, inv_c = c * scale, -b * scale, a * scale
        one, two = inv_a * right_one + inv_b * right_two, inv_b * right_one + inv_c * right_two
        for k, member in enumerate((inv_a, inv_b, inv_c)):
            inverse[section, k] = member
        partial[section, 0], partial[section, 1] = one, two
        return inv_a, inv_b, inv_c, one, two

    def backward(number, carry):
        one, two, own_one, own_two = carry
        section = count - 1 - number
        inv_a, inv_b, inv_c = (inverse[section, k] for k in range(3))
        fresh_one = partial[section, 0] + SPRING * (inv_a * one + inv_b * two)
        fresh_two = partial[section, 1] + SPRING * (inv_b * one + inv_c * two)
        mine = section == place
        own_one = jnp.where(mine, fresh_one, own_one)
        own_two = jnp.where(mine, fresh_two, own_two)
        return fresh_one, fresh_two, own_one, own_two

    zero = jnp.zeros((size, 128), jnp.float32)
    unroll = count <= 16
    lax.fori_loop(0, count, forward, (zero,) * 5, unroll=unroll)
    _, _, one, two = lax.fori_loop(0, count, backward, (zero,) * 4, unroll=unroll)
    halves = size // bands
    for number, solved in enumerate((one, two)):
        for band in range(bands):
            for half in range(halves):
                row = half * bands + band
                start = (band * halves + half) * 128
                out[number, :, start : start + 128] = solved[row : row + 1]


def body(image, conv_one, conv_two, tissue):
    height, extent = image.shape[1:]
    width = extent // 4
    rows = height // 4
    channels = conv_two.shape[0]
    across, bands = width // WIDE, rows // TALL
    tiles = across * bands
    peers, total = lax.axis_size("gz"), lax.axis_size("gy")
    vmem = pl.BlockSpec(memory_space=pltpu.VMEM)

    limit = pltpu.CompilerParams(vmem_limit_bytes=16 << 20)

    def call(kernel, name, ins, outs, scratch=()):
        return pl.pallas_call(
            kernel,
            out_shape=[jax.ShapeDtypeStruct(*out) for out in outs],
            in_specs=[vmem] * len(ins),
            out_specs=[vmem] * len(outs),
            scratch_shapes=list(scratch),
            compiler_params=limit,
            name=name,
            cost_estimate=pl.CostEstimate(
                flops=10**9, bytes_accessed=2 * 10**6, transcendentals=0
            ),
        )(*ins)

    main = lax.ppermute(image, "gz", [(z, (z + 1) % peers) for z in range(peers)])
    top, bottom = image[:, :HALO], image[:, height - HALO :]
    odd = lax.axis_index("gy") % 2 == 1
    near, far = jnp.where(odd, top, bottom), jnp.where(odd, bottom, top)

    def swapped(block, first):
        pairs = [(y, (y + 1) % total) for y in range(first, total, 2)]
        return lax.ppermute(block, "gy", pairs + [(b, a) for a, b in pairs])

    near, far = swapped(near, 0), swapped(far, 1)
    corner = lax.ppermute(
        bottom,
        ("gz", "gy"),
        [
            (z * total + y, (z + 1) % peers * total + (y + 1) % total)
            for z in range(peers)
            for y in range(total)
        ],
    )

    inner = conv_one.shape[0]
    key_rows = rows + 2 * REACH
    map_rows = -(-(2 * key_rows + 1) // CHUNK) * CHUNK
    maps = pltpu.VMEM((map_rows, 3, inner, width), jnp.bfloat16)
    shapes = (
        (extent, extent),
        (CHUNK * inner, 3 * DEPTH),
        (2 * channels, 15 * inner),
        (5, height, width),
        (CHUNK, 3, inner, width),
    )
    *matrices, split, middle, marks = call(
        prepare_kernel,
        "prepare",
        (image, conv_one, conv_two, tissue),
        [(shape, jnp.bfloat16) for shape in shapes] + [(tissue.shape, jnp.float32)],
    )
    (keys,) = call(
        functools.partial(keys_kernel, total),
        "keys",
        (near, far, *matrices, split, middle),
        [((key_rows // GROUP, width + 2 * EDGE, GROUP * channels + WIDE), jnp.bfloat16)],
        [maps],
    )

    size = tiles * TALL * WIDE // (width // NODES) ** 2 // 128

    def scratch(tiles, maps):
        return [
            maps,
            pltpu.VMEM((tiles, channels, TALL * WIDE), jnp.bfloat16),
            pltpu.VMEM((6, tiles, TALL * WIDE), jnp.float32),
        ]

    others, kept, ready = call(
        rest_kernel,
        "rest",
        (main, *matrices, keys),
        [
            ((6, tiles - LATE * across, TALL * WIDE), jnp.float32),
            ((TALL - 2, channels, width), jnp.float32),
            (((LATE - 1) * across, channels, TALL * WIDE), jnp.bfloat16),
        ],
        scratch(tiles - LATE * across, maps)[:2],
    )
    (blocks,) = call(
        first_kernel,
        "first",
        (main, corner, *matrices, keys, kept, ready, others, marks),
        [((peers, 7 * size, 128), jnp.bfloat16)],
        scratch(LATE * across, pltpu.VMEM((5, 3, inner, width), jnp.bfloat16)),
    )
    gathered = lax.all_to_all(blocks, "gz", split_axis=0, concat_axis=0, tiled=True)
    (out,) = call(
        functools.partial(solve_kernel, bands),
        "solve",
        (gathered,),
        [((2, 1, tissue.shape[1]), jnp.float32)],
        [
            pltpu.VMEM((peers, 3, size, 128), jnp.float32),
            pltpu.VMEM((peers, 2, size, 128), jnp.float32),
        ],
    )
    return out


def solution(mesh):
    placed = (P("gz", "gy", None), P(), P(), P("gz", "gy"))
    return jax.shard_map(
        body, mesh=mesh, in_specs=placed, out_specs=P(None, "gz", "gy"), check_vma=False
    )
```

```python
import functools

import jax
import jax.numpy as jnp
from jax import lax
from jax.experimental import pallas as pl
from jax.experimental.pallas import tpu as pltpu
from jax.sharding import PartitionSpec as P


NODES = 64
REACH = 6
SPRING = 8.0
ANCHOR = 0.02
PRIOR = 1.0

HALO = 32
CHUNK = 32
DEPTH = 80
TALL = 8
WIDE = 16
EDGE = 8
GROUP = 2
FAR = -1e30
PACE = 2
LATE = 2

FIRST_ROW = HALO - (4 * REACH + 3)


def iota(shape, dim):
    return lax.broadcasted_iota(jnp.int32, shape, dim)


def pick_columns(extent):
    quarter = extent // 4
    shift = iota((extent, quarter), 0) - 4 * iota((extent, quarter), 1)
    return [jnp.where(shift == q, 1.0, 0.0).astype(jnp.bfloat16) for q in range(4)]


def first_matrix(conv_one):
    channels = conv_one.shape[0]
    spread = []
    for a in range(3):
        tap = iota((9, 3 * DEPTH), 0)
        b = iota((9, 3 * DEPTH), 1) // DEPTH
        chosen = jnp.where(tap == 3 * a + b, 1.0, 0.0).astype(jnp.bfloat16)
        spread.append(jnp.dot(conv_one, chosen, preferred_element_type=jnp.float32))
    row = iota((channels, 3 * DEPTH), 1) % DEPTH - FIRST_ROW
    blocks = []
    for out in range(CHUNK):
        block = jnp.zeros_like(spread[0])
        for a in range(3):
            block = jnp.where(row == 2 * out + a, spread[a], block)
        blocks.append(block.astype(jnp.bfloat16))
    return jnp.concatenate(blocks, axis=0)


def second_matrix(conv_two):
    taps = conv_two.shape[1]
    inner = taps // 9
    rows = []
    for out in range(2):
        source = iota((taps, 15 * inner), 0)
        place = iota((taps, 15 * inner), 1)
        a = place // (3 * inner) - 2 * out
        b = (place // inner) % 3
        wanted = 9 * (place % inner) + 3 * a + b
        inside = (a >= 0) & (a < 3) & (source == wanted)
        chosen = jnp.where(inside, 1.0, 0.0).astype(jnp.bfloat16)
        rows.append(jnp.dot(conv_two, chosen, preferred_element_type=jnp.float32))
    return jnp.concatenate(rows, axis=0).astype(jnp.bfloat16)


def split_columns(pixels, picks):
    quarter = pixels.shape[1] // 4
    split = jnp.dot(pixels, picks, preferred_element_type=jnp.float32)
    parts = [split[:, q * quarter : (q + 1) * quarter] for q in range(4)]
    before = jnp.where(iota(parts[3].shape, 1) == 0, 0.0, pltpu.roll(parts[3], 1, 1))
    return [part.astype(jnp.bfloat16) for part in [before] + parts]


def first_maps(columns, matrix, maps, start):
    channels, quarter = maps.shape[2:]
    span = slice(start, start + DEPTH)
    taken = jnp.concatenate(
        [jnp.concatenate([columns[b][span], columns[b + 2][span]], axis=1) for b in range(3)],
        axis=0,
    )
    values = jnp.maximum(jnp.dot(matrix, taken, preferred_element_type=jnp.float32), 0.0)
    even, odd = values[:, :quarter], values[:, quarter:]
    before = jnp.where(iota(odd.shape, 1) == 0, 0.0, pltpu.roll(odd, 1, 1))
    for b, part in enumerate((before, even, odd)):
        maps[:, b] = part.astype(jnp.bfloat16).reshape(-1, channels, quarter)


def maps_between(columns, matrix, maps, low, high):
    channels = maps.shape[2]
    for chunk in range(low // CHUNK, -(-high // CHUNK)):
        one, two = max(low - chunk * CHUNK, 0), min(high - chunk * CHUNK, CHUNK)
        first_maps(
            columns,
            matrix[one * channels : two * channels],
            maps.at[chunk * CHUNK + one : chunk * CHUNK + two],
            2 * CHUNK * chunk,
        )


def feature_rows(maps, matrix, pair, count):
    parts = []
    for number in range(pair, pair + count):
        part = maps[4 * number : 4 * number + 5]
        parts.append(part.reshape(-1, part.shape[-1]))
    taken = jnp.concatenate(parts, axis=1) if count > 1 else parts[0]
    values = jnp.maximum(jnp.dot(matrix, taken, preferred_element_type=jnp.float32), 0.0)
    lanes = values.shape[1] // count
    return [values[:, n * lanes : (n + 1) * lanes] for n in range(count)]


def prepare_kernel(
    image, conv_one, conv_two, tissue, picks, matrix_one, matrix_two, split, middle, marks
):
    marks[...] = tissue[...].astype(jnp.float32)
    picks[...] = jnp.concatenate(pick_columns(image.shape[2]), axis=1)
    matrix_one[...] = first_matrix(conv_one[...])
    matrix_two[...] = second_matrix(conv_two[...])
    columns = split_columns(image[0], picks[...])
    for number, part in enumerate(columns):
        split[number] = part
    first_maps(columns, matrix_one[...], middle, 2 * CHUNK - HALO)


def keys_kernel(total, near, far, picks, matrix_one, matrix_two, split, middle, keys, maps):
    place = lax.axis_index("gy")
    odd = place % 2 == 1
    a, b = near[0], far[0]
    above = jnp.where(place == 0, jnp.zeros_like(a), jnp.where(odd, a, b))
    below = jnp.where(odd, b, a)
    outer = split_columns(jnp.concatenate([above, below], axis=0), picks[...])
    local = split.shape[1] // 4
    spare = jnp.zeros((DEPTH - 2 * CHUNK, split.shape[2]), jnp.bfloat16)
    columns = [
        jnp.concatenate([part[:HALO], split[n], part[HALO:], spare], axis=0)
        for n, part in enumerate(outer)
    ]
    channels = matrix_two.shape[0] // 2
    matrix = matrix_one[...]
    maps_between(columns, matrix, maps, 0, CHUNK)
    maps[CHUNK : 2 * CHUNK] = middle[...]
    maps_between(columns, matrix, maps, 2 * CHUNK, 2 * GROUP * keys.shape[0] + 1)
    last = place == total - 1
    edge = jnp.zeros((EDGE, GROUP * channels), jnp.float32)
    matrix = matrix_two[...]
    shape = (keys.shape[1], WIDE)
    column = jnp.where(iota(shape, 0) % WIDE == iota(shape, 1), 1.0, 0.0).astype(jnp.bfloat16)
    groups = keys.shape[0]
    for group in range(0, groups, 2):
        for both in feature_rows(maps, matrix, group, min(2, groups - group)):
            if GROUP * (group + 1) > local + REACH:
                row = GROUP * group + iota(both.shape, 0) // channels
                both = jnp.where(last & (row >= local + REACH), 0.0, both)
            turned = jnp.concatenate([edge, both.T, edge], axis=0)
            turned = jnp.concatenate([turned.astype(jnp.bfloat16), column], axis=1)
            keys[group] = turned
            group += 1


def swap_blocks(rows, width):
    count = len(rows)
    lanes = rows[0].shape[1]
    step = 1
    while step < count:
        low = (iota(rows[0].shape, 1) // width) % (2 * step) < step
        fresh = list(rows)
        for index in range(count):
            if index & step == 0:
                one, two = rows[index], rows[index + step]
                shift = width * step
                fresh[index] = jnp.where(low, one, pltpu.roll(two, shift, 1))
                fresh[index + step] = jnp.where(low, pltpu.roll(one, lanes - shift, 1), two)
        rows = fresh
        step *= 2
    return rows


def matcher(queries, keys, sums, band):
    channels = queries.shape[1]
    lanes = TALL * WIDE
    across = (keys.shape[1] - 2 * EDGE) // WIDE
    depth, breadth = TALL + 2 * REACH, 2 * WIDE
    span = 2 * REACH + 1
    own_row = iota((WIDE, lanes), 1) // WIDE
    own_col = iota((WIDE, lanes), 1) % WIDE
    shift_col = iota((WIDE, lanes), 0) - EDGE - own_col
    left = shift_col >= -REACH
    shift_col = jnp.where(left, shift_col, shift_col + WIDE)
    barred = jnp.where(jnp.abs(shift_col) > REACH, FAR, 0.0).astype(jnp.bfloat16)
    barred = jnp.concatenate([barred] * GROUP, axis=1)
    shift_col = shift_col.astype(jnp.float32)
    shift_row = []
    for row in range(span):
        shift = row - REACH - own_row[:8]
        shift_row.append(jnp.where(shift < -REACH, shift + span, shift).astype(jnp.float32))
    factor = channels**-0.5 * 1.4426950408889634

    def match(tile):
        tall, wide = band + tile // across, tile % across
        window = keys[
            TALL // GROUP * tall : TALL // GROUP * tall + depth // GROUP,
            WIDE * wide : WIDE * wide + breadth,
            :,
        ]
        own = queries[tile]
        empty = jnp.zeros_like(own)
        spread = jnp.concatenate(
            [
                jnp.concatenate([own if i == j else empty for j in range(GROUP)], axis=1)
                for i in range(GROUP)
            ]
            + [barred],
            axis=0,
        )
        scores = jnp.dot(
            window.reshape(-1, window.shape[-1]), spread, preferred_element_type=jnp.float32
        )
        parts = []
        for row in range(depth):
            i, j = row // GROUP, row % GROUP
            part = scores[i * breadth : (i + 1) * breadth, j * lanes : (j + 1) * lanes]
            parts.append(jnp.where(left, part[:WIDE], part[WIDE:]))
        for row in range(depth - span):
            parts[row] = jnp.where(own_row <= row, parts[row], parts[row + span])
        parts = parts[:span]
        highest = functools.reduce(jnp.maximum, parts)
        highest = jnp.max(highest, axis=0, keepdims=True)
        mass = jnp.zeros((WIDE, lanes), jnp.float32)
        once = mass
        twice = jnp.zeros((8, lanes), jnp.float32)
        for row in range(span):
            prob = jnp.exp2((parts[row] - highest) * factor)
            mass = mass + prob
            weighted = (prob.reshape(-1, 8, lanes) * shift_row[row]).reshape(WIDE, lanes)
            once = once + weighted
            twice = twice + jnp.sum(weighted.reshape(-1, 8, lanes), axis=0) * shift_row[row]
        moments = (
            mass,
            once,
            twice,
            mass * shift_col,
            mass * shift_col * shift_col,
            once * shift_col,
        )
        for number, moment in enumerate(moments):
            sums[number, tile : tile + 1, :] = jnp.sum(moment, axis=0, keepdims=True)

    return match


def pooled_fields(sums, across):
    total = sums[0]
    mean_row = sums[1] / total
    row_square = sums[2] / total
    col_mean = sums[3] / total
    col_square = sums[4] / total
    product = sums[5] / total
    var_row = row_square - mean_row * mean_row + PRIOR
    var_col = col_square - col_mean * col_mean + PRIOR
    covar = product - mean_row * col_mean
    determ = var_row * var_col - covar * covar
    info_rr = var_col / determ
    info_rc = -covar / determ
    info_cc = var_row / determ
    pull_row = info_rr * mean_row + info_rc * col_mean
    pull_col = info_rc * mean_row + info_cc * col_mean
    fields = jnp.concatenate([info_rr, info_rc, info_cc, pull_row, pull_col], axis=0)

    lanes = TALL * WIDE
    patch = across * WIDE // NODES
    high, broad = TALL // patch, WIDE // patch
    out_lanes = high * NODES
    source = iota((lanes, out_lanes), 0)
    place = iota((lanes, out_lanes), 1)
    same = (source // WIDE // patch == place // NODES) & (
        source % WIDE // patch == place % NODES % broad
    )
    pool = jnp.where(same, 1.0 / (patch * patch), 0.0).astype(jnp.bfloat16)
    parts = []
    for _ in range(3):
        parts.append(fields.astype(jnp.bfloat16))
        fields = fields - parts[-1].astype(jnp.float32)
    pooled = jnp.dot(
        jnp.concatenate(parts, axis=1),
        jnp.concatenate([pool] * 3, axis=0),
        preferred_element_type=jnp.float32,
    )
    mine = iota(pooled.shape, 0) % across == iota(pooled.shape, 1) % NODES // broad
    pooled = jnp.where(mine, pooled, 0.0)
    return jnp.sum(pooled.reshape(-1, across, out_lanes), axis=1)


def rest_kernel(
    image, picks, matrix_one, matrix_two, keys, sums, kept, ready, maps, queries
):
    columns = []
    for part in split_columns(image[0], picks[...]):
        above = jnp.zeros((HALO, part.shape[1]), jnp.bfloat16)
        below = jnp.zeros((HALO + DEPTH - 2 * CHUNK, part.shape[1]), jnp.bfloat16)
        columns.append(jnp.concatenate([above, part, below], axis=0))
    channels = queries.shape[1]
    across = (keys.shape[1] - 2 * EDGE) // WIDE
    bands = queries.shape[0] // across + LATE
    first = 2 * REACH
    maps_between(columns, matrix_one, maps, first + 2, first + 2 * TALL * bands + 1)
    matrix = matrix_two[...]
    for band in range(bands):
        rows = []
        skip = 1 if band == 0 else 0
        pair = (REACH + TALL * band) // 2
        values = []
        for number in range(skip, TALL // 2, 2):
            values += feature_rows(maps, matrix, pair + number, min(2, TALL // 2 - number))
        for both in values:
            rows += [both[:channels], both[channels:]]
        if band == 0:
            for number, row in enumerate(rows):
                kept[number] = row
            continue
        place, start = (ready, 1) if band < LATE else (queries, LATE)
        for wide, block in enumerate(swap_blocks(rows, WIDE)):
            place[across * (band - start) + wide] = block.astype(jnp.bfloat16)
    match = matcher(queries, keys, sums, LATE)
    for tile in reversed(range(queries.shape[0])):
        match(tile)


def first_kernel(
    image, corner, picks, matrix_one, matrix_two, keys, kept, ready, others, marks,
    blocks, maps, queries, sums,
):
    channels = queries.shape[1]
    across = queries.shape[0] // LATE
    above = jnp.where(lax.axis_index("gy") == 0, jnp.zeros_like(corner[0]), corner[0])
    pixels = jnp.concatenate([above, image[0, : DEPTH - HALO]], axis=0)
    begin = 2 * REACH * maps.shape[2]
    matrix = matrix_one[begin : begin + maps.shape[0] * maps.shape[2]]
    for tile in range(across, LATE * across):
        queries[tile] = ready[tile - across]
    match = matcher(queries, keys, sums, 0)
    waiting = [*range(across, LATE * across)]

    def pause():
        for _ in range(min(PACE, len(waiting))):
            match(waiting.pop(0))

    columns = split_columns(pixels, picks[...])
    pause()
    first_maps(columns, matrix, maps, 0)
    pause()
    both = feature_rows(maps, matrix_two[...], 0, 1)[0]
    pause()
    rows = [both[:channels], both[channels:]] + [kept[n] for n in range(TALL - 2)]
    for wide, block in enumerate(swap_blocks(rows, WIDE)):
        queries[wide] = block.astype(jnp.bfloat16)
    waiting += range(across)
    while waiting:
        pause()
    pooled = pooled_fields(
        [jnp.concatenate([sums[n], others[n]], axis=0) for n in range(6)], across
    )

    halves = pooled.shape[1] // 128
    bands = pooled.shape[0] // 5
    pieces, signs = [], []
    for field in range(5):
        for half in range(halves):
            place = slice(half * 128, (half + 1) * 128)
            pieces.append(pooled[field * bands : (field + 1) * bands, place])
    for half in range(halves):
        for band in range(bands):
            start = (band * halves + half) * 128
            signs.append(marks[:, start : start + 128])
    block = jnp.concatenate(pieces, axis=0)
    size = block.shape[0] // 5
    signed = block[:size] * (2.0 * jnp.concatenate(signs, axis=0) - 1.0)
    block = jnp.concatenate([signed, block[size:]], axis=0)

    def put(peer, carry):
        blocks[peer] = block
        return carry

    lax.fori_loop(0, blocks.shape[0], put, 0, unroll=blocks.shape[0] <= 16)


def solve_kernel(bands, gathered, out, inverse, partial):
    count = gathered.shape[0]
    place = lax.axis_index("gz")
    size = gathered.shape[1] // 5

    def forward(section, carry):
        inv_a, inv_b, inv_c, one, two = carry
        inside = jnp.where(section < count - 1, 1.0, 0.0)
        above = jnp.where(section > 0, 1.0, 0.0)
        extra = SPRING * (inside + above) + ANCHOR
        data = gathered[jnp.minimum(section + 1, count - 1)]
        keep = jnp.where(gathered[section, :size] > 0.0, inside, 0.0)
        fields = [data[k * size : (k + 1) * size] for k in range(5)]
        fields = [member * keep for member in [jnp.abs(fields[0])] + fields[1:]]
        square = SPRING * SPRING * above
        pulled = SPRING * above
        a = fields[0] + extra - square * inv_a
        b = fields[1] - square * inv_b
        c = fields[2] + extra - square * inv_c
        right_one = fields[3] + pulled * one
        right_two = fields[4] + pulled * two
        scale = 1.0 / (a * c - b * b)
        inv_a, inv_b, inv_c = c * scale, -b * scale, a * scale
        one, two = inv_a * right_one + inv_b * right_two, inv_b * right_one + inv_c * right_two
        for k, member in enumerate((inv_a, inv_b, inv_c)):
            inverse[section, k] = member
        partial[section, 0], partial[section, 1] = one, two
        return inv_a, inv_b, inv_c, one, two

    def backward(number, carry):
        one, two, own_one, own_two = carry
        section = count - 1 - number
        inv_a, inv_b, inv_c = (inverse[section, k] for k in range(3))
        fresh_one = partial[section, 0] + SPRING * (inv_a * one + inv_b * two)
        fresh_two = partial[section, 1] + SPRING * (inv_b * one + inv_c * two)
        mine = section == place
        own_one = jnp.where(mine, fresh_one, own_one)
        own_two = jnp.where(mine, fresh_two, own_two)
        return fresh_one, fresh_two, own_one, own_two

    zero = jnp.zeros((size, 128), jnp.float32)
    unroll = count <= 16
    lax.fori_loop(0, count, forward, (zero,) * 5, unroll=unroll)
    _, _, one, two = lax.fori_loop(0, count, backward, (zero,) * 4, unroll=unroll)
    halves = size // bands
    for number, solved in enumerate((one, two)):
        for band in range(bands):
            for half in range(halves):
                row = half * bands + band
                start = (band * halves + half) * 128
                out[number, :, start : start + 128] = solved[row : row + 1]


def body(image, conv_one, conv_two, tissue):
    height, extent = image.shape[1:]
    width = extent // 4
    rows = height // 4
    channels = conv_two.shape[0]
    across, bands = width // WIDE, rows // TALL
    tiles = across * bands
    peers, total = lax.axis_size("gz"), lax.axis_size("gy")
    vmem = pl.BlockSpec(memory_space=pltpu.VMEM)

    limit = pltpu.CompilerParams(vmem_limit_bytes=16 << 20)

    def call(kernel, name, ins, outs, scratch=()):
        return pl.pallas_call(
            kernel,
            out_shape=[jax.ShapeDtypeStruct(*out) for out in outs],
            in_specs=[vmem] * len(ins),
            out_specs=[vmem] * len(outs),
            scratch_shapes=list(scratch),
            compiler_params=limit,
            name=name,
            cost_estimate=pl.CostEstimate(
                flops=10**9, bytes_accessed=2 * 10**6, transcendentals=0
            ),
        )(*ins)

    main = lax.ppermute(image, "gz", [(z, (z + 1) % peers) for z in range(peers)])
    top, bottom = image[:, :HALO], image[:, height - HALO :]
    odd = lax.axis_index("gy") % 2 == 1
    near, far = jnp.where(odd, top, bottom), jnp.where(odd, bottom, top)

    def swapped(block, first):
        pairs = [(y, (y + 1) % total) for y in range(first, total, 2)]
        return lax.ppermute(block, "gy", pairs + [(b, a) for a, b in pairs])

    near, far = swapped(near, 0), swapped(far, 1)
    corner = lax.ppermute(
        bottom,
        ("gz", "gy"),
        [
            (z * total + y, (z + 1) % peers * total + (y + 1) % total)
            for z in range(peers)
            for y in range(total)
        ],
    )

    inner = conv_one.shape[0]
    key_rows = rows + 2 * REACH
    map_rows = -(-(2 * key_rows + 1) // CHUNK) * CHUNK
    maps = pltpu.VMEM((map_rows, 3, inner, width), jnp.bfloat16)
    shapes = (
        (extent, extent),
        (CHUNK * inner, 3 * DEPTH),
        (2 * channels, 15 * inner),
        (5, height, width),
        (CHUNK, 3, inner, width),
    )
    *matrices, split, middle, marks = call(
        prepare_kernel,
        "prepare",
        (image, conv_one, conv_two, tissue),
        [(shape, jnp.bfloat16) for shape in shapes] + [(tissue.shape, jnp.float32)],
    )
    (keys,) = call(
        functools.partial(keys_kernel, total),
        "keys",
        (near, far, *matrices, split, middle),
        [((key_rows // GROUP, width + 2 * EDGE, GROUP * channels + WIDE), jnp.bfloat16)],
        [maps],
    )

    size = tiles * TALL * WIDE // (width // NODES) ** 2 // 128

    def scratch(tiles, maps):
        return [
            maps,
            pltpu.VMEM((tiles, channels, TALL * WIDE), jnp.bfloat16),
            pltpu.VMEM((6, tiles, TALL * WIDE), jnp.float32),
        ]

    others, kept, ready = call(
        rest_kernel,
        "rest",
        (main, *matrices, keys),
        [
            ((6, tiles - LATE * across, TALL * WIDE), jnp.float32),
            ((TALL - 2, channels, width), jnp.float32),
            (((LATE - 1) * across, channels, TALL * WIDE), jnp.bfloat16),
        ],
        scratch(tiles - LATE * across, maps)[:2],
    )
    (blocks,) = call(
        first_kernel,
        "first",
        (main, corner, *matrices, keys, kept, ready, others, marks),
        [((peers, 5 * size, 128), jnp.float32)],
        scratch(LATE * across, pltpu.VMEM((5, 3, inner, width), jnp.bfloat16)),
    )
    gathered = lax.all_to_all(blocks, "gz", split_axis=0, concat_axis=0, tiled=True)
    (out,) = call(
        functools.partial(solve_kernel, bands),
        "solve",
        (gathered,),
        [((2, 1, tissue.shape[1]), jnp.float32)],
        [
            pltpu.VMEM((peers, 3, size, 128), jnp.float32),
            pltpu.VMEM((peers, 2, size, 128), jnp.float32),
        ],
    )
    return out


def solution(mesh):
    placed = (P("gz", "gy", None), P(), P(), P("gz", "gy"))
    return jax.shard_map(
        body, mesh=mesh, in_specs=placed, out_specs=P(None, "gz", "gy"), check_vma=False
    )
```

```python
import functools

import jax
import jax.numpy as jnp
from jax import lax
from jax.experimental import pallas as pl
from jax.experimental.pallas import tpu as pltpu
from jax.sharding import PartitionSpec as P


NODES = 64
REACH = 6
SPRING = 8.0
ANCHOR = 0.02
PRIOR = 1.0

HALO = 32
CHUNK = 32
DEPTH = 80
TALL = 8
WIDE = 16
EDGE = 8
GROUP = 2
FAR = -1e30
PACE = 4
LATE = 3

FIRST_ROW = HALO - (4 * REACH + 3)


def iota(shape, dim):
    return lax.broadcasted_iota(jnp.int32, shape, dim)


def pick_columns(extent):
    quarter = extent // 4
    shift = iota((extent, quarter), 0) - 4 * iota((extent, quarter), 1)
    return [jnp.where(shift == q, 1.0, 0.0).astype(jnp.bfloat16) for q in range(4)]


def first_matrix(conv_one):
    channels = conv_one.shape[0]
    spread = []
    for a in range(3):
        tap = iota((9, 3 * DEPTH), 0)
        b = iota((9, 3 * DEPTH), 1) // DEPTH
        chosen = jnp.where(tap == 3 * a + b, 1.0, 0.0).astype(jnp.bfloat16)
        spread.append(jnp.dot(conv_one, chosen, preferred_element_type=jnp.float32))
    row = iota((channels, 3 * DEPTH), 1) % DEPTH - FIRST_ROW
    blocks = []
    for out in range(CHUNK):
        block = jnp.zeros_like(spread[0])
        for a in range(3):
            block = jnp.where(row == 2 * out + a, spread[a], block)
        blocks.append(block.astype(jnp.bfloat16))
    return jnp.concatenate(blocks, axis=0)


def second_matrix(conv_two):
    taps = conv_two.shape[1]
    inner = taps // 9
    rows = []
    for out in range(2):
        source = iota((taps, 15 * inner), 0)
        place = iota((taps, 15 * inner), 1)
        a = place // (3 * inner) - 2 * out
        b = (place // inner) % 3
        wanted = 9 * (place % inner) + 3 * a + b
        inside = (a >= 0) & (a < 3) & (source == wanted)
        chosen = jnp.where(inside, 1.0, 0.0).astype(jnp.bfloat16)
        rows.append(jnp.dot(conv_two, chosen, preferred_element_type=jnp.float32))
    return jnp.concatenate(rows, axis=0).astype(jnp.bfloat16)


def split_columns(pixels, picks):
    quarter = pixels.shape[1] // 4
    split = jnp.dot(pixels, picks, preferred_element_type=jnp.float32)
    parts = [split[:, q * quarter : (q + 1) * quarter] for q in range(4)]
    before = jnp.where(iota(parts[3].shape, 1) == 0, 0.0, pltpu.roll(parts[3], 1, 1))
    return [part.astype(jnp.bfloat16) for part in [before] + parts]


def first_maps(columns, matrix, maps, start):
    channels, quarter = maps.shape[2:]
    span = slice(start, start + DEPTH)
    taken = jnp.concatenate(
        [jnp.concatenate([columns[b][span], columns[b + 2][span]], axis=1) for b in range(3)],
        axis=0,
    )
    values = jnp.maximum(jnp.dot(matrix, taken, preferred_element_type=jnp.float32), 0.0)
    even, odd = values[:, :quarter], values[:, quarter:]
    before = jnp.where(iota(odd.shape, 1) == 0, 0.0, pltpu.roll(odd, 1, 1))
    for b, part in enumerate((before, even, odd)):
        maps[:, b] = part.astype(jnp.bfloat16).reshape(-1, channels, quarter)


def maps_between(columns, matrix, maps, low, high):
    channels = maps.shape[2]
    for chunk in range(low // CHUNK, -(-high // CHUNK)):
        one, two = max(low - chunk * CHUNK, 0), min(high - chunk * CHUNK, CHUNK)
        first_maps(
            columns,
            matrix[one * channels : two * channels],
            maps.at[chunk * CHUNK + one : chunk * CHUNK + two],
            2 * CHUNK * chunk,
        )


def feature_rows(maps, matrix, pair, count):
    parts = []
    for number in range(pair, pair + count):
        part = maps[4 * number : 4 * number + 5]
        parts.append(part.reshape(-1, part.shape[-1]))
    taken = jnp.concatenate(parts, axis=1) if count > 1 else parts[0]
    values = jnp.maximum(jnp.dot(matrix, taken, preferred_element_type=jnp.float32), 0.0)
    lanes = values.shape[1] // count
    return [values[:, n * lanes : (n + 1) * lanes] for n in range(count)]


def prepare_kernel(
    image, conv_one, conv_two, tissue, picks, matrix_one, matrix_two, split, middle, marks
):
    marks[...] = tissue[...].astype(jnp.float32)
    picks[...] = jnp.concatenate(pick_columns(image.shape[2]), axis=1)
    matrix_one[...] = first_matrix(conv_one[...])
    matrix_two[...] = second_matrix(conv_two[...])
    columns = split_columns(image[0], picks[...])
    for number, part in enumerate(columns):
        split[number] = part
    first_maps(columns, matrix_one[...], middle, 2 * CHUNK - HALO)


def keys_kernel(total, near, far, picks, matrix_one, matrix_two, split, middle, keys, maps):
    place = lax.axis_index("gy")
    odd = place % 2 == 1
    a, b = near[0], far[0]
    above = jnp.where(place == 0, jnp.zeros_like(a), jnp.where(odd, a, b))
    below = jnp.where(odd, b, a)
    outer = split_columns(jnp.concatenate([above, below], axis=0), picks[...])
    local = split.shape[1] // 4
    spare = jnp.zeros((DEPTH - 2 * CHUNK, split.shape[2]), jnp.bfloat16)
    columns = [
        jnp.concatenate([part[:HALO], split[n], part[HALO:], spare], axis=0)
        for n, part in enumerate(outer)
    ]
    channels = matrix_two.shape[0] // 2
    matrix = matrix_one[...]
    maps_between(columns, matrix, maps, 0, CHUNK)
    maps[CHUNK : 2 * CHUNK] = middle[...]
    maps_between(columns, matrix, maps, 2 * CHUNK, 2 * GROUP * keys.shape[0] + 1)
    last = place == total - 1
    edge = jnp.zeros((EDGE, GROUP * channels), jnp.float32)
    matrix = matrix_two[...]
    shape = (keys.shape[1], WIDE)
    column = jnp.where(iota(shape, 0) % WIDE == iota(shape, 1), 1.0, 0.0).astype(jnp.bfloat16)
    groups = keys.shape[0]
    for group in range(0, groups, 2):
        for both in feature_rows(maps, matrix, group, min(2, groups - group)):
            if GROUP * (group + 1) > local + REACH:
                row = GROUP * group + iota(both.shape, 0) // channels
                both = jnp.where(last & (row >= local + REACH), 0.0, both)
            turned = jnp.concatenate([edge, both.T, edge], axis=0)
            keys[group, :, : GROUP * channels] = turned.astype(jnp.bfloat16)
            keys[group, :, GROUP * channels :] = column
            group += 1


def swap_blocks(rows, width):
    count = len(rows)
    lanes = rows[0].shape[1]
    step = 1
    while step < count:
        low = (iota(rows[0].shape, 1) // width) % (2 * step) < step
        fresh = list(rows)
        for index in range(count):
            if index & step == 0:
                one, two = rows[index], rows[index + step]
                shift = width * step
                fresh[index] = jnp.where(low, one, pltpu.roll(two, shift, 1))
                fresh[index + step] = jnp.where(low, pltpu.roll(one, lanes - shift, 1), two)
        rows = fresh
        step *= 2
    return rows


def matcher(queries, keys, sums, band):
    channels = queries.shape[1]
    lanes = TALL * WIDE
    across = (keys.shape[1] - 2 * EDGE) // WIDE
    depth, breadth = TALL + 2 * REACH, 2 * WIDE
    span = 2 * REACH + 1
    own_row = iota((WIDE, lanes), 1) // WIDE
    own_col = iota((WIDE, lanes), 1) % WIDE
    shift_col = iota((WIDE, lanes), 0) - EDGE - own_col
    left = shift_col >= -REACH
    shift_col = jnp.where(left, shift_col, shift_col + WIDE)
    barred = jnp.where(jnp.abs(shift_col) > REACH, FAR, 0.0).astype(jnp.bfloat16)
    barred = jnp.concatenate([barred] * GROUP, axis=1)
    shift_col = shift_col.astype(jnp.float32)
    shift_row = []
    for row in range(span):
        shift = row - REACH - own_row[:8]
        shift_row.append(jnp.where(shift < -REACH, shift + span, shift).astype(jnp.float32))
    factor = channels**-0.5 * 1.4426950408889634

    def match(tile):
        tall, wide = band + tile // across, tile % across
        window = keys[
            TALL // GROUP * tall : TALL // GROUP * tall + depth // GROUP,
            WIDE * wide : WIDE * wide + breadth,
            :,
        ]
        own = queries[tile]
        empty = jnp.zeros_like(own)
        spread = jnp.concatenate(
            [
                jnp.concatenate([own if i == j else empty for j in range(GROUP)], axis=1)
                for i in range(GROUP)
            ]
            + [barred],
            axis=0,
        )
        scores = jnp.dot(
            window.reshape(-1, window.shape[-1]), spread, preferred_element_type=jnp.float32
        )
        parts = []
        for row in range(depth):
            i, j = row // GROUP, row % GROUP
            part = scores[i * breadth : (i + 1) * breadth, j * lanes : (j + 1) * lanes]
            parts.append(jnp.where(left, part[:WIDE], part[WIDE:]))
        for row in range(depth - span):
            parts[row] = jnp.where(own_row <= row, parts[row], parts[row + span])
        parts = parts[:span]
        highest = functools.reduce(jnp.maximum, parts)
        highest = jnp.max(highest, axis=0, keepdims=True)
        mass = jnp.zeros((WIDE, lanes), jnp.float32)
        once = mass
        twice = jnp.zeros((8, lanes), jnp.float32)
        for row in range(span):
            prob = jnp.exp2((parts[row] - highest) * factor)
            mass = mass + prob
            weighted = (prob.reshape(-1, 8, lanes) * shift_row[row]).reshape(WIDE, lanes)
            once = once + weighted
            twice = twice + jnp.sum(weighted.reshape(-1, 8, lanes), axis=0) * shift_row[row]
        moments = (
            mass,
            once,
            twice,
            mass * shift_col,
            mass * shift_col * shift_col,
            once * shift_col,
        )
        for number, moment in enumerate(moments):
            sums[number, tile : tile + 1, :] = jnp.sum(moment, axis=0, keepdims=True)

    return match


def pooled_fields(sums, across):
    total = sums[0]
    mean_row = sums[1] / total
    row_square = sums[2] / total
    col_mean = sums[3] / total
    col_square = sums[4] / total
    product = sums[5] / total
    var_row = row_square - mean_row * mean_row + PRIOR
    var_col = col_square - col_mean * col_mean + PRIOR
    covar = product - mean_row * col_mean
    determ = var_row * var_col - covar * covar
    info_rr = var_col / determ
    info_rc = -covar / determ
    info_cc = var_row / determ
    pull_row = info_rr * mean_row + info_rc * col_mean
    pull_col = info_rc * mean_row + info_cc * col_mean
    fields = jnp.concatenate([info_rr, info_rc, info_cc, pull_row, pull_col], axis=0)

    lanes = TALL * WIDE
    patch = across * WIDE // NODES
    high, broad = TALL // patch, WIDE // patch
    out_lanes = high * NODES
    source = iota((lanes, out_lanes), 0)
    place = iota((lanes, out_lanes), 1)
    same = (source // WIDE // patch == place // NODES) & (
        source % WIDE // patch == place % NODES % broad
    )
    pool = jnp.where(same, 1.0 / (patch * patch), 0.0).astype(jnp.bfloat16)
    parts = []
    for _ in range(3):
        parts.append(fields.astype(jnp.bfloat16))
        fields = fields - parts[-1].astype(jnp.float32)
    pooled = jnp.dot(
        jnp.concatenate(parts, axis=1),
        jnp.concatenate([pool] * 3, axis=0),
        preferred_element_type=jnp.float32,
    )
    mine = iota(pooled.shape, 0) % across == iota(pooled.shape, 1) % NODES // broad
    pooled = jnp.where(mine, pooled, 0.0)
    return jnp.sum(pooled.reshape(-1, across, out_lanes), axis=1)


def rest_kernel(
    image, picks, matrix_one, matrix_two, keys, sums, kept, ready, maps, queries
):
    columns = []
    for part in split_columns(image[0], picks[...]):
        above = jnp.zeros((HALO, part.shape[1]), jnp.bfloat16)
        below = jnp.zeros((HALO + DEPTH - 2 * CHUNK, part.shape[1]), jnp.bfloat16)
        columns.append(jnp.concatenate([above, part, below], axis=0))
    channels = queries.shape[1]
    across = (keys.shape[1] - 2 * EDGE) // WIDE
    bands = queries.shape[0] // across + LATE
    first = 2 * REACH
    maps_between(columns, matrix_one, maps, first + 2, first + 2 * TALL * bands + 1)
    matrix = matrix_two[...]
    for band in range(bands):
        rows = []
        skip = 1 if band == 0 else 0
        pair = (REACH + TALL * band) // 2
        values = []
        for number in range(skip, TALL // 2, 2):
            values += feature_rows(maps, matrix, pair + number, min(2, TALL // 2 - number))
        for both in values:
            rows += [both[:channels], both[channels:]]
        if band == 0:
            for number, row in enumerate(rows):
                kept[number] = row
            continue
        place, start = (ready, 1) if band < LATE else (queries, LATE)
        for wide, block in enumerate(swap_blocks(rows, WIDE)):
            place[across * (band - start) + wide] = block.astype(jnp.bfloat16)
    match = matcher(queries, keys, sums, LATE)
    for tile in reversed(range(queries.shape[0])):
        match(tile)


def first_kernel(
    image, corner, picks, matrix_one, matrix_two, keys, kept, ready, others, marks,
    blocks, maps, queries, sums,
):
    channels = queries.shape[1]
    across = queries.shape[0] // LATE
    above = jnp.where(lax.axis_index("gy") == 0, jnp.zeros_like(corner[0]), corner[0])
    pixels = jnp.concatenate([above, image[0, : DEPTH - HALO]], axis=0)
    begin = 2 * REACH * maps.shape[2]
    matrix = matrix_one[begin : begin + maps.shape[0] * maps.shape[2]]
    for tile in range(across, LATE * across):
        queries[tile] = ready[tile - across]
    match = matcher(queries, keys, sums, 0)
    waiting = [*range(across, LATE * across)]

    def pause():
        for _ in range(min(PACE, len(waiting))):
            match(waiting.pop(0))

    columns = split_columns(pixels, picks[...])
    pause()
    first_maps(columns, matrix, maps, 0)
    pause()
    both = feature_rows(maps, matrix_two[...], 0, 1)[0]
    pause()
    rows = [both[:channels], both[channels:]] + [kept[n] for n in range(TALL - 2)]
    for wide, block in enumerate(swap_blocks(rows, WIDE)):
        queries[wide] = block.astype(jnp.bfloat16)
    waiting += range(across)
    while waiting:
        pause()
    pooled = pooled_fields(
        [jnp.concatenate([sums[n], others[n]], axis=0) for n in range(6)], across
    )

    halves = pooled.shape[1] // 128
    bands = pooled.shape[0] // 5
    pieces, signs = [], []
    for field in range(5):
        for half in range(halves):
            place = slice(half * 128, (half + 1) * 128)
            pieces.append(pooled[field * bands : (field + 1) * bands, place])
    for half in range(halves):
        for band in range(bands):
            start = (band * halves + half) * 128
            signs.append(marks[:, start : start + 128])
    block = jnp.concatenate(pieces, axis=0)
    size = block.shape[0] // 5
    signed = block[:size] * (2.0 * jnp.concatenate(signs, axis=0) - 1.0)
    block = jnp.concatenate([signed, block[size:]], axis=0)

    def put(peer, carry):
        blocks[peer] = block
        return carry

    lax.fori_loop(0, blocks.shape[0], put, 0, unroll=blocks.shape[0] <= 16)


def solve_kernel(bands, gathered, out, inverse, partial):
    count = gathered.shape[0]
    place = lax.axis_index("gz")
    size = gathered.shape[1] // 5

    def forward(section, carry):
        inv_a, inv_b, inv_c, one, two = carry
        inside = jnp.where(section < count - 1, 1.0, 0.0)
        above = jnp.where(section > 0, 1.0, 0.0)
        extra = SPRING * (inside + above) + ANCHOR
        data = gathered[jnp.minimum(section + 1, count - 1)]
        keep = jnp.where(gathered[section, :size] > 0.0, inside, 0.0)
        fields = [data[k * size : (k + 1) * size] for k in range(5)]
        fields = [member * keep for member in [jnp.abs(fields[0])] + fields[1:]]
        square = SPRING * SPRING * above
        pulled = SPRING * above
        a = fields[0] + extra - square * inv_a
        b = fields[1] - square * inv_b
        c = fields[2] + extra - square * inv_c
        right_one = fields[3] + pulled * one
        right_two = fields[4] + pulled * two
        scale = 1.0 / (a * c - b * b)
        inv_a, inv_b, inv_c = c * scale, -b * scale, a * scale
        one, two = inv_a * right_one + inv_b * right_two, inv_b * right_one + inv_c * right_two
        for k, member in enumerate((inv_a, inv_b, inv_c)):
            inverse[section, k] = member
        partial[section, 0], partial[section, 1] = one, two
        return inv_a, inv_b, inv_c, one, two

    def backward(number, carry):
        one, two, own_one, own_two = carry
        section = count - 1 - number
        inv_a, inv_b, inv_c = (inverse[section, k] for k in range(3))
        fresh_one = partial[section, 0] + SPRING * (inv_a * one + inv_b * two)
        fresh_two = partial[section, 1] + SPRING * (inv_b * one + inv_c * two)
        mine = section == place
        own_one = jnp.where(mine, fresh_one, own_one)
        own_two = jnp.where(mine, fresh_two, own_two)
        return fresh_one, fresh_two, own_one, own_two

    zero = jnp.zeros((size, 128), jnp.float32)
    unroll = count <= 16
    lax.fori_loop(0, count, forward, (zero,) * 5, unroll=unroll)
    _, _, one, two = lax.fori_loop(0, count, backward, (zero,) * 4, unroll=unroll)
    halves = size // bands
    for number, solved in enumerate((one, two)):
        for band in range(bands):
            for half in range(halves):
                row = half * bands + band
                start = (band * halves + half) * 128
                out[number, :, start : start + 128] = solved[row : row + 1]


def body(image, conv_one, conv_two, tissue):
    height, extent = image.shape[1:]
    width = extent // 4
    rows = height // 4
    channels = conv_two.shape[0]
    across, bands = width // WIDE, rows // TALL
    tiles = across * bands
    peers, total = lax.axis_size("gz"), lax.axis_size("gy")
    vmem = pl.BlockSpec(memory_space=pltpu.VMEM)

    limit = pltpu.CompilerParams(vmem_limit_bytes=16 << 20)

    def call(kernel, ins, outs, scratch=()):
        return pl.pallas_call(
            kernel,
            out_shape=[jax.ShapeDtypeStruct(*out) for out in outs],
            in_specs=[vmem] * len(ins),
            out_specs=[vmem] * len(outs),
            scratch_shapes=list(scratch),
            compiler_params=limit,
            cost_estimate=pl.CostEstimate(
                flops=10**9, bytes_accessed=2 * 10**6, transcendentals=0
            ),
        )(*ins)

    main = lax.ppermute(image, "gz", [(z, (z + 1) % peers) for z in range(peers)])
    top, bottom = image[:, :HALO], image[:, height - HALO :]
    odd = lax.axis_index("gy") % 2 == 1
    near, far = jnp.where(odd, top, bottom), jnp.where(odd, bottom, top)

    def swapped(block, first):
        pairs = [(y, (y + 1) % total) for y in range(first, total, 2)]
        return lax.ppermute(block, "gy", pairs + [(b, a) for a, b in pairs])

    diagonal = [
        (z * total + y, (z + 1) % peers * total + (y + 1) % total)
        for z in range(peers)
        for y in range(total)
    ]
    near = swapped(near, 0)
    far = swapped(far, 1)
    corner = lax.ppermute(bottom, ("gz", "gy"), diagonal)

    inner = conv_one.shape[0]
    key_rows = rows + 2 * REACH
    map_rows = -(-(2 * key_rows + 1) // CHUNK) * CHUNK
    maps = pltpu.VMEM((map_rows, 3, inner, width), jnp.bfloat16)
    shapes = (
        (extent, extent),
        (CHUNK * inner, 3 * DEPTH),
        (2 * channels, 15 * inner),
        (5, height, width),
        (CHUNK, 3, inner, width),
    )
    *matrices, split, middle, marks = call(
        prepare_kernel,
        (image, conv_one, conv_two, tissue),
        [(shape, jnp.bfloat16) for shape in shapes] + [(tissue.shape, jnp.float32)],
    )
    (keys,) = call(
        functools.partial(keys_kernel, total),
        (near, far, *matrices, split, middle),
        [((key_rows // GROUP, width + 2 * EDGE, GROUP * channels + WIDE), jnp.bfloat16)],
        [maps],
    )

    size = tiles * TALL * WIDE // (width // NODES) ** 2 // 128

    def scratch(tiles, maps):
        return [
            maps,
            pltpu.VMEM((tiles, channels, TALL * WIDE), jnp.bfloat16),
            pltpu.VMEM((6, tiles, TALL * WIDE), jnp.float32),
        ]

    others, kept, ready = call(
        rest_kernel,
        (main, *matrices, keys),
        [
            ((6, tiles - LATE * across, TALL * WIDE), jnp.float32),
            ((TALL - 2, channels, width), jnp.float32),
            (((LATE - 1) * across, channels, TALL * WIDE), jnp.bfloat16),
        ],
        scratch(tiles - LATE * across, maps)[:2],
    )
    (blocks,) = call(
        first_kernel,
        (main, corner, *matrices, keys, kept, ready, others, marks),
        [((peers, 5 * size, 128), jnp.float32)],
        scratch(LATE * across, pltpu.VMEM((5, 3, inner, width), jnp.bfloat16)),
    )
    gathered = lax.all_to_all(blocks, "gz", split_axis=0, concat_axis=0, tiled=True)
    (out,) = call(
        functools.partial(solve_kernel, bands),
        (gathered,),
        [((2, 1, tissue.shape[1]), jnp.float32)],
        [
            pltpu.VMEM((peers, 3, size, 128), jnp.float32),
            pltpu.VMEM((peers, 2, size, 128), jnp.float32),
        ],
    )
    return out


def solution(mesh):
    placed = (P("gz", "gy", None), P(), P(), P("gz", "gy"))
    return jax.shard_map(
        body, mesh=mesh, in_specs=placed, out_specs=P(None, "gz", "gy"), check_vma=False
    )
```
